128 devices in a mesh: tok: 16 (over z, y), mdl: 8 (over x, core).
Axes of the slice: x: 4, y: 4, z: 4, core: 2. Of those that a mesh axis runs over, the one named last changes fastest.
Arguments:
- tokens: bfloat16 [4096, 5120], P('tok'), may hold values from -32 to 32
- norm_gain: bfloat16 [5120], replicated, may hold values from 0.099609375 to 1.8984375
- w_query: bfloat16 [5120, 4096], P(None, 'mdl'), may hold values from -0.078125 to 0.078125
- w_key: bfloat16 [5120, 1024], P(None, 'mdl'), may hold values from -0.3125 to 0.3125
- w_value: bfloat16 [5120, 1024], P(None, 'mdl'), may hold values from -0.078125 to 0.078125
- w_out: bfloat16 [4096, 5120], P('mdl'), may hold values from -0.09375 to 0.09375
- prompt_keys: bfloat16 [6, 4096, 8, 128], P(None, 'tok', 'mdl'), may hold values from -6 to 6
- prompt_values: bfloat16 [6, 4096, 8, 128], P(None, 'tok', 'mdl'), may hold values from -24 to 24
- cache_keys: bfloat16 [128, 2048, 8, 128], P('tok', None, 'mdl'), may hold values from -6 to 6
- cache_values: bfloat16 [128, 2048, 8, 128], P('tok', None, 'mdl'), may hold values from -24 to 24
- cache_length: int32 [128], P('tok'), may hold values from 1 to 2048, as said below
- request_group: int32 [128], replicated, may hold values from 0 to 5
- ancestors: int32 [128, 32, 32], P('tok'), may hold values from 0 to 1, as said below
- accepted: int32 [128, 8], P('tok'), may hold values from -1 to 31, as said below
Outputs:
- attention_out: bfloat16 [4096, 5120], P('tok', 'mdl')
- compact_rows: bfloat16 [128, 8, 5120], P('tok', None, 'mdl')
The draws below stay inside these ranges and needn't reach their ends.
Inputs may be any that keep to these rules, and one draw needn't show every extreme that they name: `cache_length`: some request has exactly 2048 live slots. ancestors[r, a, b] is 1 where tree slot b is slot a itself or an ancestor of it in request r's draft tree, else 0; each tree has one root, and slots are in no particular order. Entry k of request r is the tree slot of the accepted path's node at depth k, from the root on, for k below the path's length, and -1 after it; a path holds 1 to 8 nodes, and some request's path holds 8.
All inputs are finite; a program needn't handle non-finite values.
Results may differ from the reference program's by a relative error of at most 0.017.
Values may be sent and summed in bfloat16 or wider, within the bound.
No kernel may reach another device: no remote copies, remote signals or barrier semaphores. Data moves between devices by JAX's collectives and lax.ppermute only.
A program may use at most 128 MiB of HBM per device.

```python
import jax
import jax.numpy as jnp
from jax import lax

D = 5120
HQ = 32
KVH = 8
HD = 128
CACHE = 2048
TREE = 32
ACC = 8
PROMPT = 4096
GROUPS = 6
REQ = 128
TOKENS = 4096
N_TOK = 16


def draw_tokens(key, part):
    base = jax.random.fold_in(key, 1)
    key_rows, key_columns, key_main = jax.random.split(base, 3)
    column_scale = jnp.exp(jax.random.uniform(key_columns, (D,), jnp.float32, jnp.log(0.3), jnp.log(3.0)))
    row_scale = jnp.exp(jax.random.uniform(key_rows, (TOKENS, 1), jnp.float32, jnp.log(0.5), jnp.log(2.0)))
    values = jnp.clip(jax.random.normal(key_main, (TOKENS, D), jnp.float32), -5.0, 5.0)
    return (values * column_scale[None, :] * row_scale).astype(jnp.bfloat16)


def draw_cache_length(key, part):
    base = jax.random.fold_in(key, 3)
    key_length, key_shift, key_chosen = jax.random.split(base, 3)
    length = jax.random.randint(key_length, (REQ,), 1, CACHE + 1)
    shifts = jax.random.randint(key_shift, (REQ,), 0, 3)
    divisor = jnp.where(shifts == 0, 1, jnp.where(shifts == 1, 2, 4))
    length = jnp.maximum(length // divisor, 1)
    chosen = jax.random.randint(key_chosen, (), 0, REQ)
    return jnp.where(jnp.arange(REQ, dtype=jnp.int32) == chosen, CACHE, length).astype(jnp.int32)


def tree_tables(key):
    base = jax.random.fold_in(key, 7)
    key_order, key_parent, key_length, key_chosen = jax.random.split(base, 4)
    nodes = jnp.arange(TREE, dtype=jnp.int32)
    scores = jax.random.randint(key_order, (REQ, TREE), 0, 1 << 20) * TREE + nodes[None, :]
    slot_of = jnp.argsort(scores, axis=1).astype(jnp.int32)
    draws = jax.random.randint(key_parent, (REQ, TREE), 0, 1 << 20)
    parent = jnp.where(nodes[None, :] < ACC, nodes[None, :] - 1, draws % jnp.maximum(nodes[None, :], 1))
    ancestry = jnp.zeros((REQ, TREE, TREE), jnp.int32)
    for member in range(TREE):
        itself = jnp.broadcast_to((nodes == member).astype(jnp.int32)[None, :], (REQ, TREE))
        if member == 0:
            lineage = itself
        else:
            above = jnp.take_along_axis(ancestry, jnp.maximum(parent[:, member], 0)[:, None, None], axis=1)[:, 0, :]
            lineage = above + itself
        ancestry = ancestry.at[:, member, :].set(lineage)
    raw_of = jnp.argsort(slot_of, axis=1).astype(jnp.int32)
    first = jnp.take_along_axis(ancestry, raw_of[:, :, None], axis=1)
    table = jnp.take_along_axis(first, raw_of[:, None, :], axis=2)
    length = jax.random.randint(key_length, (REQ,), 1, ACC + 1)
    chosen = jax.random.randint(key_chosen, (), 0, REQ)
    length = jnp.where(jnp.arange(REQ, dtype=jnp.int32) == chosen, ACC, length)
    spine = slot_of[:, :ACC]
    paths = jnp.where(jnp.arange(ACC, dtype=jnp.int32)[None, :] < length[:, None], spine, -1)
    return (table.astype(jnp.int32), paths.astype(jnp.int32))


def draw_ancestors(key, part):
    return tree_tables(key)[0]


def draw_accepted(key, part):
    return tree_tables(key)[1]


def touch_ends(result, stream_key, smallest, high):
    index_at = [jax.random.randint(jax.random.fold_in(stream_key, axis), (), 0, length) for axis, length in enumerate(result.shape)]
    longest = result.shape.index(max(result.shape))
    beside = index_at[:longest] + [(index_at[longest] + 1) % result.shape[longest]] + index_at[longest + 1:]
    return result.at[tuple(index_at)].set(smallest).at[tuple(beside)].set(high)


def steps_of(own_key, extent, cuts, least, high):
    def one(dim, blocks):
        heights = jax.random.uniform(jax.random.fold_in(jax.random.fold_in(own_key, 6), dim), (blocks,), jnp.float32, least / len(cuts), high / len(cuts))
        return jnp.repeat(jnp.exp(heights), extent[dim] // blocks).reshape((-1,) + (1,) * (len(extent) - dim - 1))

    level = one(*cuts[0])
    for cut in cuts[1:]:
        level = level * one(*cut)
    return level


def normal_values(key, extent, deviation, limit, pieces=(), kind=jnp.bfloat16):
    result = deviation * jax.random.normal(key, extent, jnp.float32)
    if pieces:
        result = result * steps_of(key, extent, pieces, -0.22, 0.18)
    return jnp.clip(result, -limit, limit).astype(kind)


def setup_inputs(seed: int = 0) -> dict:
    key_list = jax.random.split(jax.random.key(seed), 15)
    tokens = draw_tokens(jax.random.fold_in(key_list[14], 71), 0)
    norm_gain = jnp.clip(1.0 + 0.18 * jax.random.normal(key_list[1], (D,), jnp.float32), 0.099609375, 1.8984375).astype(jnp.bfloat16)
    w_query = normal_values(key_list[2], (D, HQ * HD), D ** -0.5, 0.078125, ((1, 8),))
    w_key = normal_values(key_list[3], (D, KVH * HD), (D // 16) ** -0.5, 0.3125, ((1, 8),))
    w_value = normal_values(key_list[4], (D, KVH * HD), D ** -0.5, 0.078125, ((1, 8),))
    w_out = normal_values(key_list[5], (HQ * HD, D), (HQ * HD) ** -0.5, 0.09375, ((0, 8),))
    prompt_keys = normal_values(key_list[6], (GROUPS, PROMPT, KVH, HD), 1.0, 6.0, ((1, 16), (2, 8)))
    prompt_values = normal_values(key_list[7], (GROUPS, PROMPT, KVH, HD), 4.0, 24.0, ((1, 16), (2, 8)))
    cache_keys = normal_values(key_list[8], (REQ, CACHE, KVH, HD), 1.0, 6.0, ((0, 16), (2, 8)))
    cache_values = normal_values(key_list[9], (REQ, CACHE, KVH, HD), 4.0, 24.0, ((0, 16), (2, 8)))
    cache_length = draw_cache_length(jax.random.fold_in(key_list[14], 71), 0)
    request_group = touch_ends(jax.random.randint(key_list[11], (REQ,), 0, GROUPS), jax.random.fold_in(key_list[11], 1), 0, GROUPS - 1).astype(jnp.int32)
    ancestors = draw_ancestors(jax.random.fold_in(key_list[14], 71), 0)
    accepted = draw_accepted(jax.random.fold_in(key_list[14], 71), 0)
    return {"tokens": tokens, "norm_gain": norm_gain, "w_query": w_query, "w_key": w_key, "w_value": w_value, "w_out": w_out, "prompt_keys": prompt_keys, "prompt_values": prompt_values, "cache_keys": cache_keys, "cache_values": cache_values, "cache_length": cache_length, "request_group": request_group, "ancestors": ancestors, "accepted": accepted}


THETA = 100000000.0
EPS = 1e-05

def rotate_pairs(vectors, positions):
    middle = vectors.shape[-1] // 2
    exponent = jnp.arange(middle, dtype=jnp.float32) * (2.0 / vectors.shape[-1])
    inverse = jnp.power(jnp.float32(THETA), -exponent)
    angles = positions.astype(jnp.float32)[:, None] * inverse[None, :]
    cosine = jnp.cos(angles)[:, None, :]
    sine_part = jnp.sin(angles)[:, None, :]
    leading = vectors[..., :middle]
    trailing = vectors[..., middle:]
    return jnp.concatenate([leading * cosine - trailing * sine_part, trailing * cosine + leading * sine_part], axis=-1)

def round_bfloat(values):
    return lax.optimization_barrier(values.astype(jnp.bfloat16)).astype(jnp.float32)

def reference(tokens, norm_gain, w_query, w_key, w_value, w_out, prompt_keys, prompt_values, cache_keys, cache_values, cache_length, request_group, ancestors, accepted):
    wide = tokens.astype(jnp.float32)
    normed = (wide * lax.rsqrt(lax.optimization_barrier(jnp.mean(wide * wide, axis=1, keepdims=True)) + EPS) * norm_gain.astype(jnp.float32)).astype(jnp.bfloat16)
    queries = jnp.dot(normed, w_query, preferred_element_type=jnp.float32).reshape(TOKENS, HQ, HD)
    new_keys = jnp.dot(normed, w_key, preferred_element_type=jnp.float32).reshape(TOKENS, KVH, HD)
    new_values = jnp.dot(normed, w_value, preferred_element_type=jnp.float32).astype(jnp.bfloat16).reshape(REQ, TREE, KVH, HD)
    depth = lax.optimization_barrier(jnp.sum(ancestors, axis=2)) - 1
    positions = (PROMPT + cache_length[:, None] + depth).reshape(TOKENS)
    queries = rotate_pairs(queries, positions).astype(jnp.bfloat16).reshape(REQ, TREE, KVH, HQ // KVH, HD)
    new_keys = rotate_pairs(new_keys, positions).astype(jnp.bfloat16).reshape(REQ, TREE, KVH, HD)
    factor = HD ** (-0.5)
    slice_rows = PROMPT // N_TOK

    def one_request(operands):
        grouped, tree_keys, tree_values, group_index, own_keys, own_values, length, lineage = operands
        grouped = grouped.astype(jnp.float32)
        shared_keys = lax.dynamic_index_in_dim(prompt_keys, group_index, 0, keepdims=False).astype(jnp.float32).reshape(N_TOK, slice_rows, KVH, HD)
        shared_values = lax.dynamic_index_in_dim(prompt_values, group_index, 0, keepdims=False).astype(jnp.float32).reshape(N_TOK, slice_rows, KVH, HD)
        scores = jnp.einsum('tkgd,sckd->tkgsc', grouped, shared_keys) * factor
        weights = jnp.exp(scores)
        totals = lax.optimization_barrier(jnp.sum(weights, axis=4))
        numerator = jnp.einsum('tkgsc,sckd->tkgsd', round_bfloat(weights), shared_values)
        outputs = round_bfloat(numerator / totals[..., None])
        prompt_part = lax.optimization_barrier(jnp.sum(totals[..., None] * outputs, axis=3))
        prompt_total = lax.optimization_barrier(jnp.sum(totals, axis=3))
        cache_scores = jnp.einsum('tkgd,ckd->tkgc', grouped, own_keys.astype(jnp.float32)) * factor
        live = jnp.arange(CACHE, dtype=jnp.int32) < length
        cache_weights = jnp.where(live, jnp.exp(cache_scores), 0.0)
        cache_part = jnp.einsum('tkgc,ckd->tkgd', round_bfloat(cache_weights), own_values.astype(jnp.float32))
        tree_scores = jnp.einsum('tkgd,mkd->tkgm', grouped, tree_keys.astype(jnp.float32)) * factor
        tree_weights = jnp.where(lineage[:, None, None, :] > 0, jnp.exp(tree_scores), 0.0)
        tree_part = jnp.einsum('tkgm,mkd->tkgd', round_bfloat(tree_weights), tree_values.astype(jnp.float32))
        totals_all = prompt_total + lax.optimization_barrier(jnp.sum(cache_weights, axis=3)) + lax.optimization_barrier(jnp.sum(tree_weights, axis=3))
        merged = (prompt_part + cache_part + tree_part) / totals_all[..., None]
        return merged.astype(jnp.bfloat16).reshape(TREE, HQ * HD)
    attended = lax.map(one_request, (queries, new_keys, new_values, request_group, cache_keys, cache_values, cache_length, ancestors)).reshape(TOKENS, HQ * HD)
    attention_out = jnp.dot(attended, w_out, preferred_element_type=jnp.float32).astype(jnp.bfloat16)
    residual = wide + attention_out.astype(jnp.float32)
    rows_index = (jnp.arange(REQ, dtype=jnp.int32)[:, None] * TREE + jnp.maximum(accepted, 0)).reshape(REQ * ACC)
    picked = jnp.take(residual, rows_index, axis=0).reshape(REQ, ACC, D)
    compact_rows = jnp.where(accepted[:, :, None] >= 0, picked, 0.0).astype(jnp.bfloat16)
    return (attention_out, compact_rows)
```

```python
import math

import jax
import jax.numpy as jnp
import numpy as np
from jax import lax
from jax.experimental import pallas as pl
from jax.experimental.pallas import tpu as pltpu
from jax.sharding import PartitionSpec as P

PROMPT = 4096
THETA = 100000000.0
EPS = 1e-05

F32 = jnp.float32
BF16 = jnp.bfloat16

ANY = pl.BlockSpec(memory_space=pl.ANY)
SMEM = pl.BlockSpec(memory_space=pltpu.SMEM)
VM = pl.BlockSpec(memory_space=pltpu.VMEM)
LIMIT = 56 * 1024 * 1024
PARAMS = pltpu.CompilerParams(vmem_limit_bytes=LIMIT)
CHUNKS = 5
KB = 256
NT = (((1,), (1,)), ((), ()))


def dot(a, b):
    return jnp.dot(a, b, preferred_element_type=F32)


def dot_nt(a, b):
    return lax.dot_general(a, b, NT, preferred_element_type=F32)


def rotate(x, cosine, sine):
    return x * cosine + pltpu.roll(x, x.shape[1] // 2, 1) * sine


def query_kernel(len_ref, tok_hbm, gain_ref, wq_hbm, anc_ref, inv_ref, q_ref, normed_ref, cos_ref, sin_ref, tok, wq, sems):
    rows, width = tok.shape
    requests = len_ref.shape[0]
    tree = rows // requests
    get_tok = pltpu.make_async_copy(tok_hbm, tok, sems.at[0])
    get_tok.start()
    part = width // CHUNKS
    copies = []
    for i in range(CHUNKS):
        c = pltpu.make_async_copy(
            wq_hbm.at[pl.ds(i * part, part)], wq.at[pl.ds(i * part, part)], sems.at[1 + i]
        )
        c.start()
        copies.append(c)
    depth = jnp.sum(anc_ref[...], axis=1, keepdims=True).astype(F32) - 1.0
    places = jnp.concatenate(
        [
            depth[r * tree : (r + 1) * tree] + (PROMPT + len_ref[r]).astype(F32)
            for r in range(requests)
        ],
        axis=0,
    )
    angles = places * inv_ref[...]
    lane = lax.broadcasted_iota(jnp.int32, angles.shape, 1)
    cosine = jnp.cos(angles)
    sine = jnp.sin(angles)
    sine = jnp.where(lane < angles.shape[1] // 2, -sine, sine)
    cos_ref[...] = cosine
    sin_ref[...] = sine
    get_tok.wait()

    def norm(i, _):
        at = pl.ds(pl.multiple_of(i * 32, 32), 32)
        wide = tok[at, :].astype(F32)
        scale = lax.rsqrt(jnp.mean(wide * wide, axis=1, keepdims=True) + EPS)
        normed_ref[at, :] = (wide * scale * gain_ref[...].astype(F32)).astype(BF16)
        return 0

    lax.fori_loop(0, rows // 32, norm, 0)
    acc = None
    for i in range(CHUNKS):
        copies[i].wait()
        d = dot(normed_ref[:, i * part : (i + 1) * part], wq[i * part : (i + 1) * part, :])
        acc = d if acc is None else acc + d
    hd = inv_ref.shape[1]
    heads = acc.shape[1] // hd
    fold = hd**-0.5 * math.log2(math.e)
    for g in range(heads):
        turned = (rotate(acc[:, g * hd : (g + 1) * hd], cosine, sine) * fold).astype(BF16)
        for r in range(requests):
            q_ref[pl.ds((r * heads + g) * tree, tree), :] = turned[r * tree : (r + 1) * tree]


def query_call(lengths, tokens, gain, w_query, ancestors, inverse):
    rows, width = tokens.shape
    hd = inverse.shape[1]
    heads = w_query.shape[1] // hd
    return pl.pallas_call(
        query_kernel,
        in_specs=[SMEM, ANY, VM, ANY, VM, VM],
        out_specs=[VM, VM, VM, VM],
        out_shape=[
            jax.ShapeDtypeStruct((rows * heads, hd), BF16),
            jax.ShapeDtypeStruct((rows, width), BF16),
            jax.ShapeDtypeStruct((rows, hd), F32),
            jax.ShapeDtypeStruct((rows, hd), F32),
        ],
        scratch_shapes=[
            pltpu.VMEM((rows, width), BF16),
            pltpu.VMEM(w_query.shape, BF16),
            pltpu.SemaphoreType.DMA((1 + CHUNKS,)),
        ],
        compiler_params=PARAMS,
        name="query_proj",
    )(lengths, tokens, gain, w_query, ancestors, inverse)


def own_kernel(
    len_ref, normed_ref, wk_hbm, wv_hbm, cos_ref, sin_ref, q_ref, anc_ref, ck_hbm, cv_hbm, out_ref,
    w, keys, values, wsems, csems,
):
    requests, slots, hd = keys.shape
    rows, width = normed_ref.shape
    tree = rows // requests
    blocks = slots // KB
    group = q_ref.shape[0] // requests // tree
    qrows = group * tree
    get_k = pltpu.make_async_copy(wk_hbm, w.at[:, pl.ds(0, hd)], wsems.at[0])
    get_v = pltpu.make_async_copy(wv_hbm, w.at[:, pl.ds(hd, hd)], wsems.at[1])
    get_k.start()
    get_v.start()

    def cache_copies(r, b):
        at = pl.ds(pl.multiple_of(b * KB, KB), KB)
        return (
            pltpu.make_async_copy(ck_hbm.at[r, at], keys.at[r, at], csems.at[0, r, b]),
            pltpu.make_async_copy(cv_hbm.at[r, at], values.at[r, at], csems.at[1, r, b]),
        )

    for r in range(requests):

        def begin(b, _, r=r):
            for c in cache_copies(r, b):
                c.start()
            return 0

        lax.fori_loop(0, (len_ref[r] + KB - 1) // KB, begin, 0)
    get_k.wait()
    get_v.wait()
    both = dot(normed_ref[...], w[...])
    new_keys = rotate(both[:, :hd], cos_ref[...], sin_ref[...]).astype(BF16)
    new_values = both[:, hd:].astype(BF16)
    ones = jnp.ones((KB, hd), BF16)
    column = lax.broadcasted_iota(jnp.int32, (qrows, KB), 1)
    for r in range(requests):
        q = q_ref[pl.ds(r * qrows, qrows), :]
        at = slice(r * tree, (r + 1) * tree)
        scores = dot_nt(q, new_keys[at])
        seen = jnp.concatenate([anc_ref[at, :]] * group, axis=0)
        weights = jnp.where(seen > 0, jnp.exp2(scores), 0.0).astype(BF16)
        out_ref[pl.ds(r * qrows, qrows), :] = dot(
            weights, jnp.concatenate([new_values[at], ones[:tree]], axis=1)
        )

        def block(b, _, r=r, q=q):
            for c in cache_copies(r, b):
                c.wait()
            rows_at = pl.ds(pl.multiple_of(b * KB, KB), KB)
            s = dot_nt(q, keys[r, rows_at, :])
            p = jnp.where(column < len_ref[r] - b * KB, jnp.exp2(s), 0.0).astype(BF16)
            out_ref[pl.ds(r * qrows, qrows), :] += dot(
                p, jnp.concatenate([values[r, rows_at, :], ones], axis=1)
            )
            return 0

        lax.fori_loop(0, (len_ref[r] + KB - 1) // KB, block, 0)


def own_call(lengths, normed, w_key, w_value, cosine, sine, q, ancestors, cache_keys, cache_values):
    requests, slots, hd = cache_keys.shape
    return pl.pallas_call(
        own_kernel,
        in_specs=[SMEM, VM, ANY, ANY, VM, VM, VM, VM, ANY, ANY],
        out_specs=VM,
        out_shape=jax.ShapeDtypeStruct((q.shape[0], 2 * hd), F32),
        scratch_shapes=[
            pltpu.VMEM((normed.shape[1], 2 * hd), BF16),
            pltpu.VMEM(cache_keys.shape, BF16),
            pltpu.VMEM(cache_values.shape, BF16),
            pltpu.SemaphoreType.DMA((2,)),
            pltpu.SemaphoreType.DMA((2, requests, slots // KB)),
        ],
        compiler_params=PARAMS,
        name="own_attention",
    )(lengths, normed, w_key, w_value, cosine, sine, q, ancestors, cache_keys, cache_values)


def prompt_sum(q, g, pieces, ones):
    acc = None
    for kref, koff, vref, voff in pieces:
        p = jnp.exp2(dot_nt(q, kref[koff + g])).astype(BF16)
        d = dot(p, jnp.concatenate([vref[voff + g], ones], axis=1))
        acc = d if acc is None else acc + d
    return acc


def pieces_of(kv, kv_r, kv_l, k_o, v_o):
    n = k_o.shape[0]
    return [(kv, 0, kv, n), (kv_r, 0, kv_r, n), (kv_l, 0, kv_l, n), (k_o, 0, v_o, 0)]


def remote_kernel(group_ref, base_ref, q_ref, kv, kv_r, kv_l, k_o, v_o, out_ref, *, requests):
    hd = q_ref.shape[1]
    qrows = q_ref.shape[0] // requests
    pieces = pieces_of(kv, kv_r, kv_l, k_o, v_o)
    ones = jnp.ones((k_o.shape[1], hd), BF16)
    diagonal = lax.broadcasted_iota(jnp.int32, (qrows, hd), 0) == lax.broadcasted_iota(
        jnp.int32, (qrows, hd), 1
    )

    totals = []
    for r in range(requests):
        at = pl.ds(r * qrows, qrows)
        acc = prompt_sum(q_ref[at, :], group_ref[base_ref[0] + r], pieces, ones)
        out_ref[at, :] = acc[:, :hd].astype(BF16)
        totals.append(jnp.sum(jnp.where(diagonal, acc[:, hd:], 0.0), axis=0, keepdims=True))
    total = jnp.concatenate(totals, axis=0)
    high = total.astype(BF16)
    low = (total - high.astype(F32)).astype(BF16)
    out_ref[pl.ds(requests * qrows, 2 * requests), :] = jnp.concatenate([high, low], axis=0)


def remote_call(groups, base, q, prompts, requests):
    rows, hd = q.shape
    return pl.pallas_call(
        lambda *refs: remote_kernel(*refs, requests=requests),
        in_specs=[SMEM, SMEM] + [VM] * 6,
        out_specs=VM,
        out_shape=jax.ShapeDtypeStruct((rows + 2 * requests, hd), BF16),
        compiler_params=PARAMS,
        name="prompt_remote",
    )(groups, base, q, *prompts)


def home_kernel(group_ref, base_ref, q_ref, kv, kv_r, kv_l, k_o, v_o, own_ref, out_ref, *, requests):
    hd = q_ref.shape[1]
    qrows = q_ref.shape[0] // requests
    pieces = pieces_of(kv, kv_r, kv_l, k_o, v_o)
    ones = jnp.ones((k_o.shape[1], hd), BF16)
    for r in range(requests):
        at = pl.ds(r * qrows, qrows)
        out_ref[at, :] = own_ref[at, :] + prompt_sum(
            q_ref[at, :], group_ref[base_ref[0] + r], pieces, ones
        )


def home_call(groups, base, q, prompts, own, requests):
    return pl.pallas_call(
        lambda *refs: home_kernel(*refs, requests=requests),
        in_specs=[SMEM, SMEM] + [VM] * 7,
        out_specs=VM,
        out_shape=jax.ShapeDtypeStruct(own.shape, F32),
        compiler_params=PARAMS,
        name="prompt_home",
    )(groups, base, q, *prompts, own)


def merge_kernel(home_ref, a_ref, b_ref, c_ref, out_ref, *, requests):
    hd = a_ref.shape[1]
    qrows = home_ref.shape[0] // requests
    tree = out_ref.shape[0] // requests
    total = None
    for ref in (a_ref, b_ref, c_ref):
        both = ref[pl.ds(requests * qrows, 2 * requests), :].astype(F32)
        t = both[:requests] + both[requests:]
        total = t if total is None else total + t
    diagonal = lax.broadcasted_iota(jnp.int32, (qrows, hd), 0) == lax.broadcasted_iota(
        jnp.int32, (qrows, hd), 1
    )
    for r in range(requests):
        at = pl.ds(r * qrows, qrows)
        num = home_ref[at, pl.ds(0, hd)]
        for ref in (a_ref, b_ref, c_ref):
            num = num + ref[at, :].astype(F32)
        den = home_ref[at, pl.ds(hd, hd)] + jnp.sum(
            jnp.where(diagonal, jnp.broadcast_to(total[r : r + 1], (qrows, hd)), 0.0),
            axis=1,
            keepdims=True,
        )
        out = (num / den).astype(BF16)
        for g in range(qrows // tree):
            out_ref[pl.ds(r * tree, tree), pl.ds(g * hd, hd)] = out[g * tree : (g + 1) * tree]


def merge_call(home, a, b, c, requests, rows):
    hd = a.shape[1]
    return pl.pallas_call(
        lambda *refs: merge_kernel(*refs, requests=requests),
        in_specs=[VM] * 4,
        out_specs=VM,
        out_shape=jax.ShapeDtypeStruct((rows, home.shape[0] // rows * hd), BF16),
        compiler_params=PARAMS,
        name="merge",
    )(home, a, b, c)


def columns_kernel(at_ref, w_hbm, out_hbm, sems):
    count, _, cols = out_hbm.shape
    copies = []
    for i in range(count):
        start = pl.multiple_of(2 * cols * i + at_ref[0] * cols, 128)
        c = pltpu.make_async_copy(w_hbm.at[:, pl.ds(start, cols)], out_hbm.at[i], sems.at[i])
        c.start()
        copies.append(c)
    for c in copies:
        c.wait()


def columns_call(side, w_out, count):
    cols = w_out.shape[1] // (2 * count)
    return pl.pallas_call(
        columns_kernel,
        in_specs=[SMEM, ANY],
        out_specs=ANY,
        out_shape=jax.ShapeDtypeStruct((count, w_out.shape[0], cols), BF16),
        scratch_shapes=[pltpu.SemaphoreType.DMA((count,))],
        name="out_columns",
    )(side, w_out)


def out_kernel(where_ref, mine_ref, other_ref, w_hbm, wo_hbm, *refs):
    outs = refs[:-3]
    wa, wb, sems = refs[-3:]
    cols = wa.shape[2]
    copies = []
    for i in range(len(outs)):
        start = pl.multiple_of((2 * where_ref[i] + where_ref[3]) * cols, 128)
        ca = pltpu.make_async_copy(w_hbm.at[:, pl.ds(start, cols)], wa.at[i], sems.at[0, i])
        cb = pltpu.make_async_copy(wo_hbm.at[where_ref[i]], wb.at[i], sems.at[1, i])
        ca.start()
        cb.start()
        copies.append((ca, cb))
    for i, out in enumerate(outs):
        copies[i][0].wait()
        d = dot(mine_ref[...], wa[i])
        copies[i][1].wait()
        out[...] = (d + dot(other_ref[...], wb[i])).astype(out.dtype)


def out_call(where, mine, other, w_out, w_other, n, dtype):
    rows = mine.shape[0]
    cols = w_other.shape[2]
    inner = mine.shape[1]
    return pl.pallas_call(
        out_kernel,
        in_specs=[SMEM, VM, VM, ANY, ANY],
        out_specs=[VM] * n,
        out_shape=[jax.ShapeDtypeStruct((rows, cols), dtype)] * n,
        scratch_shapes=[
            pltpu.VMEM((n, inner, cols), BF16),
            pltpu.VMEM((n, inner, cols), BF16),
            pltpu.SemaphoreType.DMA((2, n)),
        ],
        compiler_params=PARAMS,
        name="out_proj",
    )(where, mine, other, w_out, w_other)


def last_kernel(acc_ref, at_ref, own_ref, a_ref, b_ref, c_ref, tok_hbm, out_ref, rows_ref, tok, sums, sem):
    cols = own_ref.shape[1]
    requests, most = acc_ref.shape
    tree = own_ref.shape[0] // requests
    get = pltpu.make_async_copy(
        tok_hbm.at[:, pl.ds(pl.multiple_of(at_ref[0] * cols, 128), cols)], tok, sem
    )
    get.start()
    total = own_ref[...] + a_ref[...].astype(F32) + b_ref[...].astype(F32) + c_ref[...].astype(F32)
    rounded = total.astype(BF16)
    out_ref[...] = rounded
    get.wait()
    sums[...] = tok[...].astype(F32) + rounded.astype(F32)
    for r in range(requests):
        for k in range(most):
            slot = acc_ref[r, k]
            row = sums[pl.ds(r * tree + jnp.maximum(slot, 0), 1), :]
            rows_ref[r, pl.ds(k, 1), :] = jnp.where(slot >= 0, row, 0.0)


def last_call(accepted, column, own, a, b, c, tokens):
    rows, cols = own.shape
    requests, most = accepted.shape
    return pl.pallas_call(
        last_kernel,
        in_specs=[SMEM, SMEM, VM, VM, VM, VM, ANY],
        out_specs=[VM, VM],
        out_shape=[
            jax.ShapeDtypeStruct((rows, cols), BF16),
            jax.ShapeDtypeStruct((requests, most, cols), F32),
        ],
        scratch_shapes=[
            pltpu.VMEM((rows, cols), BF16),
            pltpu.VMEM((rows, cols), F32),
            pltpu.SemaphoreType.DMA,
        ],
        compiler_params=PARAMS,
        name="last_sums",
    )(accepted, column, own, a, b, c, tokens)


def shards(
    tokens, norm_gain, w_query, w_key, w_value, w_out, prompt_keys, prompt_values, cache_keys,
    cache_values, cache_length, request_group, ancestors, accepted,
):
    requests, tree = ancestors.shape[:2]
    rows = tokens.shape[0]
    hd = prompt_keys.shape[3]
    n_tok = lax.axis_size("tok")
    n_mdl = lax.axis_size("mdl")
    n_y = 4
    n_z = n_tok // n_y
    n_x = n_mdl // 2
    tok = lax.axis_index("tok")
    mdl = lax.axis_index("mdl")

    def along_y(v, n):
        perm = [(t, t // n_y * n_y + (t + n) % n_y) for t in range(n_tok)]
        return lax.ppermute(v, "tok", perm)

    def along_z(v, n):
        return lax.ppermute(v, "tok", [(t, (t + n * n_y) % n_tok) for t in range(n_tok)])

    def along_x(v, n):
        return lax.ppermute(v, "mdl", [(m, (m + 2 * n) % n_mdl) for m in range(n_mdl)])

    def other_core(v):
        return lax.ppermute(v, "mdl", [(m, m ^ 1) for m in range(n_mdl)])

    squeeze = lambda v: v.reshape(v.shape[0], v.shape[1], v.shape[3])
    groups_n = prompt_keys.shape[0]
    kv = jnp.concatenate([squeeze(prompt_keys), squeeze(prompt_values)], axis=0)
    kv_r = along_y(kv, 1)
    kv_l = along_y(kv, -1)
    k_o = along_y(kv_r[:groups_n], 1)
    v_o = along_y(kv_l[groups_n:], -1)
    prompts = (kv, kv_r, kv_l, k_o, v_o)

    exponent = np.arange(hd // 2, dtype=np.float64) * (2.0 / hd)
    inverse = jnp.asarray(np.tile(THETA**-exponent, 2)[None, :], dtype=F32)
    table = ancestors.reshape(rows, tree)
    q, normed, cosine, sine = query_call(
        cache_length, tokens, norm_gain[None, :], w_query, table, inverse
    )
    shifts = (2, 1, -1)
    q_far = [along_z(q, n) for n in shifts]

    side = jnp.reshape(1 - mdl % 2, (1,)).astype(jnp.int32)
    w_other = other_core(columns_call(side, w_out, n_x))

    own = own_call(
        cache_length, normed, w_key, w_value, cosine, sine, q, table, squeeze(cache_keys),
        squeeze(cache_values),
    )
    back = []
    for n, qf in zip(shifts, q_far):
        source = (tok + n_tok - n * n_y) % n_tok
        base = jnp.reshape(source * requests, (1,)).astype(jnp.int32)
        part = remote_call(request_group, base, qf, prompts, requests)
        back.append(along_z(part, -n))
    base = jnp.reshape(tok * requests, (1,)).astype(jnp.int32)
    home = home_call(request_group, base, q, prompts, own, requests)
    attended = merge_call(home, *back, requests, rows)

    attended_other = other_core(attended)
    x = mdl // 2
    sent = []
    for group in ((2,), (1, -1), (0,)):
        where = jnp.stack(
            [(x + group[min(i, len(group) - 1)] + n_x) % n_x for i in range(3)] + [mdl % 2]
        ).astype(jnp.int32)
        outs = out_call(
            where, attended, attended_other, w_out, w_other, len(group), F32 if group == (0,) else BF16
        )
        sent += [along_x(o, n) if n else o for o, n in zip(outs, group)]
    far, up, down, own_sum = sent
    column = jnp.reshape(mdl, (1,)).astype(jnp.int32)
    attention_out, picked = last_call(accepted, column, own_sum, far, up, down, tokens)
    return attention_out, picked.astype(BF16)


def solution(mesh):
    placed = (
        P("tok", None),
        P(),
        P(None, "mdl"),
        P(None, "mdl"),
        P(None, "mdl"),
        P("mdl", None),
        P(None, "tok", "mdl", None),
        P(None, "tok", "mdl", None),
        P("tok", None, "mdl", None),
        P("tok", None, "mdl", None),
        P("tok"),
        P(),
        P("tok", None, None),
        P("tok", None),
    )
    return jax.shard_map(
        shards,
        mesh=mesh,
        in_specs=placed,
        out_specs=(P("tok", "mdl"), P("tok", None, "mdl")),
        check_vma=False,
    )
```

```python
import math

import jax
import jax.numpy as jnp
import numpy as np
from jax import lax
from jax.experimental import pallas as pl
from jax.experimental.pallas import tpu as pltpu
from jax.sharding import PartitionSpec as P


PROMPT = 4096
THETA = 100000000.0
EPS = 1e-05

F32 = jnp.float32
BF16 = jnp.bfloat16

ANY = pl.BlockSpec(memory_space=pl.ANY)
SMEM = pl.BlockSpec(memory_space=pltpu.SMEM)
VM = pl.BlockSpec(memory_space=pltpu.VMEM)
CHUNKS = 5
KB = 512
NT = (((1,), (1,)), ((), ()))


def params(mib):
    return pltpu.CompilerParams(vmem_limit_bytes=mib * 1024 * 1024)


def dot(a, b):
    return jnp.dot(a, b, preferred_element_type=F32)


def dot_nt(a, b):
    return lax.dot_general(a, b, NT, preferred_element_type=F32)


def rotate(x, cosine, sine):
    return x * cosine + pltpu.roll(x, x.shape[1] // 2, 1) * sine


def query_kernel(len_ref, tok_hbm, gain_ref, wq_hbm, anc_ref, inv_ref, q_ref, normed_ref, cos_ref, sin_ref, tok, wq, sems):
    rows, width = tok.shape
    requests = len_ref.shape[0]
    tree = rows // requests
    get_tok = pltpu.make_async_copy(tok_hbm, tok, sems.at[0])
    get_tok.start()
    part = width // CHUNKS
    copies = []
    for i in range(CHUNKS):
        c = pltpu.make_async_copy(
            wq_hbm.at[pl.ds(i * part, part)], wq.at[pl.ds(i * part, part)], sems.at[1 + i]
        )
        c.start()
        copies.append(c)
    depth = jnp.sum(anc_ref[...], axis=1, keepdims=True).astype(F32) - 1.0
    places = jnp.concatenate(
        [
            depth[r * tree : (r + 1) * tree] + (PROMPT + len_ref[r]).astype(F32)
            for r in range(requests)
        ],
        axis=0,
    )
    angles = places * inv_ref[...]
    lane = lax.broadcasted_iota(jnp.int32, angles.shape, 1)
    cosine = jnp.cos(angles)
    sine = jnp.sin(angles)
    sine = jnp.where(lane < angles.shape[1] // 2, -sine, sine)
    cos_ref[...] = cosine
    sin_ref[...] = sine
    get_tok.wait()

    def norm(i, _):
        at = pl.ds(pl.multiple_of(i * 32, 32), 32)
        wide = tok[at, :].astype(F32)
        scale = lax.rsqrt(jnp.mean(wide * wide, axis=1, keepdims=True) + EPS)
        normed_ref[at, :] = (wide * scale * gain_ref[...].astype(F32)).astype(BF16)
        return 0

    lax.fori_loop(0, rows // 32, norm, 0)
    acc = None
    for i in range(CHUNKS):
        copies[i].wait()
        d = dot(normed_ref[:, i * part : (i + 1) * part], wq[i * part : (i + 1) * part, :])
        acc = d if acc is None else acc + d
    hd = inv_ref.shape[1]
    heads = acc.shape[1] // hd
    fold = hd**-0.5 * math.log2(math.e)
    for g in range(heads):
        turned = (rotate(acc[:, g * hd : (g + 1) * hd], cosine, sine) * fold).astype(BF16)
        for r in range(requests):
            q_ref[pl.ds((r * heads + g) * tree, tree), :] = turned[r * tree : (r + 1) * tree]


def query_call(lengths, tokens, gain, w_query, ancestors, inverse):
    rows, width = tokens.shape
    hd = inverse.shape[1]
    heads = w_query.shape[1] // hd
    return pl.pallas_call(
        query_kernel,
        in_specs=[SMEM, ANY, VM, ANY, VM, VM],
        out_specs=[VM, VM, VM, VM],
        out_shape=[
            jax.ShapeDtypeStruct((rows * heads, hd), BF16),
            jax.ShapeDtypeStruct((rows, width), BF16),
            jax.ShapeDtypeStruct((rows, hd), F32),
            jax.ShapeDtypeStruct((rows, hd), F32),
        ],
        scratch_shapes=[
            pltpu.VMEM((rows, width), BF16),
            pltpu.VMEM(w_query.shape, BF16),
            pltpu.SemaphoreType.DMA((1 + CHUNKS,)),
        ],
        compiler_params=params(24),
        name="query_proj",
    )(lengths, tokens, gain, w_query, ancestors, inverse)


def tree_kernel(normed_ref, wk_hbm, wv_hbm, cos_ref, sin_ref, q_ref, anc_ref, out_ref, w, sems):
    rows, tree = anc_ref.shape
    hd = q_ref.shape[1]
    group = q_ref.shape[0] // rows
    qrows = group * tree
    part = w.shape[0] // CHUNKS
    copies = []
    for i in range(CHUNKS):
        at = pl.ds(i * part, part)
        ck = pltpu.make_async_copy(wk_hbm.at[at], w.at[at, pl.ds(0, hd)], sems.at[0, i])
        cv = pltpu.make_async_copy(wv_hbm.at[at], w.at[at, pl.ds(hd, hd)], sems.at[1, i])
        ck.start()
        cv.start()
        copies.append((ck, cv))
    both = None
    for i in range(CHUNKS):
        copies[i][0].wait()
        copies[i][1].wait()
        d = dot(normed_ref[:, i * part : (i + 1) * part], w[i * part : (i + 1) * part, :])
        both = d if both is None else both + d
    new_keys = rotate(both[:, :hd], cos_ref[...], sin_ref[...]).astype(BF16)
    new_values = both[:, hd:].astype(BF16)
    ones = jnp.ones((tree, hd), BF16)
    for r in range(rows // tree):
        at = slice(r * tree, (r + 1) * tree)
        here = pl.ds(r * qrows, qrows)
        scores = dot_nt(q_ref[here, :], new_keys[at])
        seen = jnp.concatenate([anc_ref[at, :]] * group, axis=0)
        weights = jnp.where(seen > 0, jnp.exp2(scores), 0.0).astype(BF16)
        out_ref[here, :] = dot(weights, jnp.concatenate([new_values[at], ones], axis=1))


def tree_call(normed, w_key, w_value, cosine, sine, q, ancestors):
    hd = q.shape[1]
    return pl.pallas_call(
        tree_kernel,
        in_specs=[VM, ANY, ANY, VM, VM, VM, VM],
        out_specs=VM,
        out_shape=jax.ShapeDtypeStruct((q.shape[0], 2 * hd), F32),
        scratch_shapes=[
            pltpu.VMEM((normed.shape[1], 2 * hd), BF16),
            pltpu.SemaphoreType.DMA((2, CHUNKS)),
        ],
        compiler_params=params(16),
        name="tree_attention",
    )(normed, w_key, w_value, cosine, sine, q, ancestors)


def prompt_sum(q, g, pieces, ones):
    weights, values = [], []
    for kref, koff, vref, voff in pieces:
        weights.append(jnp.exp2(dot_nt(q, kref[koff + g])).astype(BF16))
        values.append(jnp.concatenate([vref[voff + g], ones], axis=1))
    return dot(jnp.concatenate(weights, axis=1), jnp.concatenate(values, axis=0))


def pieces_of(kv, kv_r, kv_l, k_o, v_o):
    n = k_o.shape[0]
    return [(kv, 0, kv, n), (kv_r, 0, kv_r, n), (kv_l, 0, kv_l, n), (k_o, 0, v_o, 0)]


def remote_kernel(group_ref, at_ref, q_ref, kv, kv_r, kv_l, k_o, v_o, out_ref, *, requests, shift, n_tok):
    hd = q_ref.shape[1]
    qrows = q_ref.shape[0] // requests
    pieces = pieces_of(kv, kv_r, kv_l, k_o, v_o)
    ones = jnp.ones((k_o.shape[1], hd), BF16)
    diagonal = lax.broadcasted_iota(jnp.int32, (qrows, hd), 0) == lax.broadcasted_iota(
        jnp.int32, (qrows, hd), 1
    )

    base = lax.rem(at_ref[0] + n_tok - shift, n_tok) * requests
    totals = []
    for r in range(requests):
        at = pl.ds(r * qrows, qrows)
        acc = prompt_sum(q_ref[at, :], group_ref[base + r], pieces, ones)
        out_ref[at, :] = acc[:, :hd].astype(BF16)
        totals.append(jnp.sum(jnp.where(diagonal, acc[:, hd:], 0.0), axis=0, keepdims=True))
    total = jnp.concatenate(totals, axis=0)
    high = total.astype(BF16)
    low = (total - high.astype(F32)).astype(BF16)
    out_ref[pl.ds(requests * qrows, 2 * requests), :] = jnp.concatenate([high, low], axis=0)


def remote_call(groups, at, q, prompts, requests, shift, n_tok):
    rows, hd = q.shape
    return pl.pallas_call(
        lambda *refs: remote_kernel(*refs, requests=requests, shift=shift, n_tok=n_tok),
        in_specs=[SMEM, SMEM] + [VM] * 6,
        out_specs=VM,
        out_shape=jax.ShapeDtypeStruct((rows + 2 * requests, hd), BF16),
        compiler_params=params(12),
        name="prompt_remote",
    )(groups, at, q, *prompts)


def home_kernel(
    group_ref, at_ref, len_ref, q_ref, kv, kv_r, kv_l, k_o, v_o, own_ref, ck_hbm, cv_hbm, out_ref,
    keys, values, sems,
):
    requests, _, hd = keys.shape
    qrows = q_ref.shape[0] // requests

    def cache_copies(r, b):
        at = pl.ds(pl.multiple_of(b * KB, KB), KB)
        return (
            pltpu.make_async_copy(ck_hbm.at[r, at], keys.at[r, at], sems.at[0, r, b]),
            pltpu.make_async_copy(cv_hbm.at[r, at], values.at[r, at], sems.at[1, r, b]),
        )

    def live(r):
        return (len_ref[r] + KB - 1) // KB

    for r in range(requests):

        def begin(b, _, r=r):
            for c in cache_copies(r, b):
                c.start()
            return 0

        lax.fori_loop(0, live(r), begin, 0)
    pieces = pieces_of(kv, kv_r, kv_l, k_o, v_o)
    ones = jnp.ones((k_o.shape[1], hd), BF16)
    for r in range(requests):
        at = pl.ds(r * qrows, qrows)
        out_ref[at, :] = own_ref[at, :] + prompt_sum(
            q_ref[at, :], group_ref[at_ref[0] * requests + r], pieces, ones
        )
    column = lax.broadcasted_iota(jnp.int32, (qrows, KB), 1)
    ones = jnp.ones((KB, hd), BF16)
    for r in range(requests):
        at = pl.ds(r * qrows, qrows)

        def block(b, _, r=r, at=at):
            for c in cache_copies(r, b):
                c.wait()
            rows_at = pl.ds(pl.multiple_of(b * KB, KB), KB)
            s = dot_nt(q_ref[at, :], keys[r, rows_at, :])
            p = jnp.where(column < len_ref[r] - b * KB, jnp.exp2(s), 0.0).astype(BF16)
            out_ref[at, :] += dot(p, jnp.concatenate([values[r, rows_at, :], ones], axis=1))
            return 0

        lax.fori_loop(0, live(r), block, 0)


def home_call(groups, at, lengths, q, prompts, own, cache_keys, cache_values):
    requests, slots, _ = cache_keys.shape
    return pl.pallas_call(
        home_kernel,
        in_specs=[SMEM, SMEM, SMEM] + [VM] * 7 + [ANY, ANY],
        out_specs=VM,
        out_shape=jax.ShapeDtypeStruct(own.shape, F32),
        scratch_shapes=[
            pltpu.VMEM(cache_keys.shape, BF16),
            pltpu.VMEM(cache_values.shape, BF16),
            pltpu.SemaphoreType.DMA((2, requests, slots // KB)),
        ],
        compiler_params=params(24),
        name="home_attention",
    )(groups, at, lengths, q, *prompts, own, cache_keys, cache_values)


def merge_kernel(home_ref, a_ref, b_ref, c_ref, out_ref, *, requests):
    hd = a_ref.shape[1]
    qrows = home_ref.shape[0] // requests
    tree = out_ref.shape[0] // requests
    total = None
    for ref in (a_ref, b_ref, c_ref):
        both = ref[pl.ds(requests * qrows, 2 * requests), :].astype(F32)
        t = both[:requests] + both[requests:]
        total = t if total is None else total + t
    diagonal = lax.broadcasted_iota(jnp.int32, (qrows, hd), 0) == lax.broadcasted_iota(
        jnp.int32, (qrows, hd), 1
    )
    for r in range(requests):
        at = pl.ds(r * qrows, qrows)
        num = home_ref[at, pl.ds(0, hd)]
        for ref in (a_ref, b_ref, c_ref):
            num = num + ref[at, :].astype(F32)
        den = home_ref[at, pl.ds(hd, hd)] + jnp.sum(
            jnp.where(diagonal, jnp.broadcast_to(total[r : r + 1], (qrows, hd)), 0.0),
            axis=1,
            keepdims=True,
        )
        out = (num / den).astype(BF16)
        for g in range(qrows // tree):
            out_ref[pl.ds(r * tree, tree), pl.ds(g * hd, hd)] = out[g * tree : (g + 1) * tree]


def merge_call(home, a, b, c, requests, rows):
    hd = a.shape[1]
    return pl.pallas_call(
        lambda *refs: merge_kernel(*refs, requests=requests),
        in_specs=[VM] * 4,
        out_specs=VM,
        out_shape=jax.ShapeDtypeStruct((rows, home.shape[0] // rows * hd), BF16),
        compiler_params=params(8),
        name="merge",
    )(home, a, b, c)


def columns_kernel(mdl_ref, w_hbm, mine_ref, send_ref, sems):
    count, _, cols = mine_ref.shape
    copies = []
    for i in range(count):
        for j, ref in enumerate((mine_ref, send_ref)):
            side = lax.rem(mdl_ref[0] + j, 2)
            start = pl.multiple_of((2 * i + side) * cols, 128)
            c = pltpu.make_async_copy(w_hbm.at[:, pl.ds(start, cols)], ref.at[i], sems.at[j, i])
            c.start()
            copies.append(c)
    for c in copies:
        c.wait()


def columns_call(mdl, w_out, count):
    cols = w_out.shape[1] // (2 * count)
    return pl.pallas_call(
        columns_kernel,
        in_specs=[SMEM, ANY],
        out_specs=[VM, VM],
        out_shape=[jax.ShapeDtypeStruct((count, w_out.shape[0], cols), BF16)] * 2,
        scratch_shapes=[pltpu.SemaphoreType.DMA((2, count))],
        compiler_params=params(8),
        name="out_columns",
    )(mdl, w_out)


def out_kernel(mdl_ref, mine_ref, other_ref, wa, wb, *outs, shifts):
    for shift, out in zip(shifts, outs):
        i = lax.rem(mdl_ref[0] // 2 + shift, wa.shape[0])
        out[...] = (dot(mine_ref[...], wa[i]) + dot(other_ref[...], wb[i])).astype(out.dtype)


def out_call(mdl, mine, other, w_mine, w_other, shifts, dtype):
    shape = (mine.shape[0], w_other.shape[2])
    return pl.pallas_call(
        lambda *refs: out_kernel(*refs, shifts=shifts),
        in_specs=[SMEM] + [VM] * 4,
        out_specs=[VM] * len(shifts),
        out_shape=[jax.ShapeDtypeStruct(shape, dtype)] * len(shifts),
        compiler_params=params(12),
        name="out_proj",
    )(mdl, mine, other, w_mine, w_other)


def last_kernel(acc_ref, at_ref, own_ref, a_ref, b_ref, c_ref, tok_hbm, out_ref, rows_ref, tok, sums, kept, sem):
    cols = own_ref.shape[1]
    requests, most = acc_ref.shape
    tree = own_ref.shape[0] // requests
    get = pltpu.make_async_copy(
        tok_hbm.at[:, pl.ds(pl.multiple_of(at_ref[0] * cols, 128), cols)], tok, sem
    )
    get.start()
    total = own_ref[...] + a_ref[...].astype(F32) + b_ref[...].astype(F32) + c_ref[...].astype(F32)
    rounded = total.astype(BF16)
    out_ref[...] = rounded
    get.wait()
    sums[...] = tok[...].astype(F32) + rounded.astype(F32)
    for r in range(requests):
        for k in range(most):
            slot = acc_ref[r, k]
            row = sums[pl.ds(r * tree + jnp.maximum(slot, 0), 1), :]
            kept[r, pl.ds(k, 1), :] = jnp.where(slot >= 0, row, 0.0)
    rows_ref[...] = kept[...].astype(BF16)


def last_call(accepted, column, own, a, b, c, tokens):
    rows, cols = own.shape
    requests, most = accepted.shape
    return pl.pallas_call(
        last_kernel,
        in_specs=[SMEM, SMEM, VM, VM, VM, VM, ANY],
        out_specs=[VM, VM],
        out_shape=[
            jax.ShapeDtypeStruct((rows, cols), BF16),
            jax.ShapeDtypeStruct((requests, most, cols), BF16),
        ],
        scratch_shapes=[
            pltpu.VMEM((rows, cols), BF16),
            pltpu.VMEM((rows, cols), F32),
            pltpu.VMEM((requests, most, cols), F32),
            pltpu.SemaphoreType.DMA,
        ],
        compiler_params=params(8),
        name="last_sums",
    )(accepted, column, own, a, b, c, tokens)


def shards(
    tokens, norm_gain, w_query, w_key, w_value, w_out, prompt_keys, prompt_values, cache_keys,
    cache_values, cache_length, request_group, ancestors, accepted,
):
    requests, tree = ancestors.shape[:2]
    rows = tokens.shape[0]
    hd = prompt_keys.shape[3]
    n_tok = lax.axis_size("tok")
    n_mdl = lax.axis_size("mdl")
    n_y = 4
    n_x = n_mdl // 2
    tok = lax.axis_index("tok")
    mdl = lax.axis_index("mdl")

    def along_y(v, n):
        perm = [(t, t // n_y * n_y + (t + n) % n_y) for t in range(n_tok)]
        return lax.ppermute(v, "tok", perm)

    def along_z(v, n):
        return lax.ppermute(v, "tok", [(t, (t + n * n_y) % n_tok) for t in range(n_tok)])

    def along_x(v, n):
        return lax.ppermute(v, "mdl", [(m, (m + 2 * n) % n_mdl) for m in range(n_mdl)])

    def other_core(v):
        return lax.ppermute(v, "mdl", [(m, m ^ 1) for m in range(n_mdl)])

    tok_at = jnp.reshape(tok, (1,)).astype(jnp.int32)
    mdl_at = jnp.reshape(mdl, (1,)).astype(jnp.int32)

    squeeze = lambda v: v.reshape(v.shape[0], v.shape[1], v.shape[3])
    groups_n = prompt_keys.shape[0]
    kv = jnp.concatenate([squeeze(prompt_keys), squeeze(prompt_values)], axis=0)
    kv_r = along_y(kv, 1)
    kv_l = along_y(kv, -1)

    exponent = np.arange(hd // 2, dtype=np.float64) * (2.0 / hd)
    inverse = jnp.asarray(np.tile(THETA**-exponent, 2)[None, :], dtype=F32)
    table = ancestors.reshape(rows, tree)
    q, normed, cosine, sine = query_call(
        cache_length, tokens, norm_gain[None, :], w_query, table, inverse
    )
    shifts = (2, 1, -1)
    q_far = [along_z(q, n) for n in shifts]
    own = tree_call(normed, w_key, w_value, cosine, sine, q, table)

    k_o = along_y(kv_r[:groups_n], 1)
    v_o = along_y(kv_l[groups_n:], -1)
    prompts = (kv, kv_r, kv_l, k_o, v_o)

    w_mine, w_send = columns_call(mdl_at, w_out, n_x)
    w_other = other_core(w_send)

    back = []
    for n, qf in zip(shifts, q_far):
        part = remote_call(request_group, tok_at, qf, prompts, requests, n * n_y, n_tok)
        back.append(along_z(part, -n))
    home = home_call(
        request_group, tok_at, cache_length, q, prompts, own, squeeze(cache_keys),
        squeeze(cache_values),
    )
    attended = merge_call(home, *back, requests, rows)

    attended_other = other_core(attended)
    sent = []
    for group in ((2,), (1, -1), (0,)):
        outs = out_call(
            mdl_at, attended, attended_other, w_mine, w_other, [n % n_x for n in group],
            F32 if group == (0,) else BF16,
        )
        sent += [along_x(o, n) if n else o for o, n in zip(outs, group)]
    far, up, down, own_sum = sent
    return tuple(last_call(accepted, mdl_at, own_sum, far, up, down, tokens))


def solution(mesh):
    placed = (
        P("tok", None),
        P(),
        P(None, "mdl"),
        P(None, "mdl"),
        P(None, "mdl"),
        P("mdl", None),
        P(None, "tok", "mdl", None),
        P(None, "tok", "mdl", None),
        P("tok", None, "mdl", None),
        P("tok", None, "mdl", None),
        P("tok"),
        P(),
        P("tok", None, None),
        P("tok", None),
    )

    return jax.shard_map(
        shards,
        mesh=mesh,
        in_specs=placed,
        out_specs=(P("tok", "mdl"), P("tok", None, "mdl")),
        check_vma=False,
    )
```

```python
import math

import jax
import jax.numpy as jnp
import numpy as np
from jax import lax
from jax.experimental import pallas as pl
from jax.experimental.pallas import tpu as pltpu
from jax.sharding import PartitionSpec as P


PROMPT = 4096
THETA = 100000000.0
EPS = 1e-05

F32 = jnp.float32
BF16 = jnp.bfloat16

HBM = pl.BlockSpec(memory_space=pltpu.HBM)
SMEM = pl.BlockSpec(memory_space=pltpu.SMEM)
VM = pl.BlockSpec(memory_space=pltpu.VMEM)
CHUNKS = 5
KB = 256
PIECES = 2
LANES = 8
NT = (((1,), (1,)), ((), ()))


def params(mib):
    return pltpu.CompilerParams(vmem_limit_bytes=mib * 1024 * 1024)


def dot(a, b):
    return jnp.dot(a, b, preferred_element_type=F32)


def dot_nt(a, b):
    return lax.dot_general(a, b, NT, preferred_element_type=F32)


def rotate(x, cosine, sine):
    return x * cosine + pltpu.roll(x, x.shape[1] // 2, 1) * sine


def query_kernel(
    len_hbm, tok_hbm, gain_hbm, wq_hbm, anc_hbm, inv_hbm, q_ref, normed_hbm, turn_hbm,
    lengths, tok, gain, wq, table, inverse, normed_ref, turn, sems, wsems, osems,
):
    rows, width = tok.shape
    requests = lengths.shape[0]
    tree = rows // requests
    firsts = [
        pltpu.make_async_copy(source, target, sems.at[i])
        for i, (source, target) in enumerate(
            ((anc_hbm, table), (len_hbm, lengths), (inv_hbm, inverse), (gain_hbm, gain), (tok_hbm, tok))
        )
    ]
    for c in firsts:
        c.start()
    part = width // CHUNKS
    copies = []
    for i in range(CHUNKS):
        at = pl.ds(i * part, part)
        c = pltpu.make_async_copy(wq_hbm.at[at], wq.at[at], wsems.at[i])
        c.start()
        copies.append(c)
    for c in firsts[:3]:
        c.wait()
    depth = jnp.sum(table[...], axis=1, keepdims=True).astype(F32) - 1.0
    places = jnp.concatenate(
        [
            depth[r * tree : (r + 1) * tree] + (PROMPT + lengths[r]).astype(F32)
            for r in range(requests)
        ],
        axis=0,
    )
    angles = places * inverse[...]
    lane = lax.broadcasted_iota(jnp.int32, angles.shape, 1)
    cosine = jnp.cos(angles)
    sine = jnp.sin(angles)
    sine = jnp.where(lane < angles.shape[1] // 2, -sine, sine)
    turn[0] = cosine
    turn[1] = sine
    put_turn = pltpu.make_async_copy(turn, turn_hbm, osems.at[0])
    put_turn.start()
    for c in firsts[3:]:
        c.wait()
    gains = gain[...].astype(F32)
    gains = jnp.concatenate([gains[i : i + 1] for i in range(gain.shape[0])], axis=1)

    def norm(i, _):
        at = pl.ds(pl.multiple_of(i * 32, 32), 32)
        wide = tok[at, :].astype(F32)
        scale = lax.rsqrt(jnp.mean(wide * wide, axis=1, keepdims=True) + EPS)
        normed_ref[at, :] = (wide * scale * gains).astype(BF16)
        return 0

    lax.fori_loop(0, rows // 32, norm, 0)
    put_normed = pltpu.make_async_copy(normed_ref, normed_hbm, osems.at[1])
    put_normed.start()
    acc = None
    for i in range(CHUNKS):
        copies[i].wait()
        d = dot(normed_ref[:, i * part : (i + 1) * part], wq[i * part : (i + 1) * part, :])
        acc = d if acc is None else acc + d
    hd = inverse.shape[1]
    heads = acc.shape[1] // hd
    fold = hd**-0.5 * math.log2(math.e)
    for g in range(heads):
        turned = (rotate(acc[:, g * hd : (g + 1) * hd], cosine, sine) * fold).astype(BF16)
        for r in range(requests):
            q_ref[pl.ds((r * heads + g) * tree, tree), :] = turned[r * tree : (r + 1) * tree]
    put_turn.wait()
    put_normed.wait()


def query_call(lengths, tokens, gain, w_query, ancestors, inverse):
    rows, width = tokens.shape
    hd = inverse.shape[1]
    heads = w_query.shape[1] // hd
    return pl.pallas_call(
        query_kernel,
        in_specs=[HBM] * 6,
        out_specs=[VM, HBM, HBM],
        out_shape=[
            jax.ShapeDtypeStruct((rows * heads, hd), BF16),
            pltpu.HBM((rows, width), BF16),
            pltpu.HBM((2, rows, hd), F32),
        ],
        scratch_shapes=[
            pltpu.SMEM(lengths.shape, jnp.int32),
            pltpu.VMEM((rows, width), BF16),
            pltpu.VMEM(gain.shape, BF16),
            pltpu.VMEM(w_query.shape, BF16),
            pltpu.VMEM(ancestors.shape, jnp.int32),
            pltpu.VMEM(inverse.shape, F32),
            pltpu.VMEM((rows, width), BF16),
            pltpu.VMEM((2, rows, hd), F32),
            pltpu.SemaphoreType.DMA((5,)),
            pltpu.SemaphoreType.DMA((CHUNKS,)),
            pltpu.SemaphoreType.DMA((2,)),
        ],
        compiler_params=params(24),
        name="query_proj",
    )(lengths, tokens, gain, w_query, ancestors, inverse)


def tree_kernel(
    normed_hbm, wk_hbm, wv_hbm, turn_hbm, q_ref, anc_hbm, out_hbm,
    normed_ref, w, turn, anc_ref, out_ref, sems, osems,
):
    rows, tree = anc_ref.shape
    hd = q_ref.shape[1]
    group = q_ref.shape[0] // rows
    qrows = group * tree
    part = w.shape[0] // CHUNKS
    copies = []
    for i in range(CHUNKS):
        at = pl.ds(i * part, part)
        three = (
            pltpu.make_async_copy(normed_hbm.at[:, at], normed_ref.at[:, at], sems.at[0, i]),
            pltpu.make_async_copy(wk_hbm.at[at], w.at[at, pl.ds(0, hd)], sems.at[1, i]),
            pltpu.make_async_copy(wv_hbm.at[at], w.at[at, pl.ds(hd, hd)], sems.at[2, i]),
        )
        for c in three:
            c.start()
        copies.append(three)
    get_turn = pltpu.make_async_copy(turn_hbm, turn, osems.at[rows // tree])
    get_anc = pltpu.make_async_copy(anc_hbm, anc_ref, osems.at[rows // tree + 1])
    get_turn.start()
    get_anc.start()
    both = None
    for i in range(CHUNKS):
        for c in copies[i]:
            c.wait()
        d = dot(normed_ref[:, i * part : (i + 1) * part], w[i * part : (i + 1) * part, :])
        both = d if both is None else both + d
    get_turn.wait()
    get_anc.wait()
    new_keys = rotate(both[:, :hd], turn[0], turn[1]).astype(BF16)
    new_values = both[:, hd:].astype(BF16)
    ones = jnp.ones((tree, hd), BF16)
    puts = []
    for r in range(rows // tree):
        at = slice(r * tree, (r + 1) * tree)
        here = pl.ds(r * qrows, qrows)
        scores = dot_nt(q_ref[here, :], new_keys[at])
        seen = jnp.concatenate([anc_ref[at, :]] * group, axis=0)
        weights = jnp.where(seen > 0, jnp.exp2(scores), 0.0).astype(BF16)
        out_ref[here, :] = dot(weights, jnp.concatenate([new_values[at], ones], axis=1))
        put = pltpu.make_async_copy(out_ref.at[here], out_hbm.at[here], osems.at[r])
        put.start()
        puts.append(put)
    for put in puts:
        put.wait()


def tree_call(normed, w_key, w_value, turn, q, ancestors):
    rows, tree = ancestors.shape
    hd = q.shape[1]
    return pl.pallas_call(
        tree_kernel,
        in_specs=[HBM, HBM, HBM, HBM, VM, HBM],
        out_specs=HBM,
        out_shape=pltpu.HBM((q.shape[0], 2 * hd), F32),
        scratch_shapes=[
            pltpu.VMEM(normed.shape, BF16),
            pltpu.VMEM((normed.shape[1], 2 * hd), BF16),
            pltpu.VMEM(turn.shape, F32),
            pltpu.VMEM(ancestors.shape, jnp.int32),
            pltpu.VMEM((q.shape[0], 2 * hd), F32),
            pltpu.SemaphoreType.DMA((3, CHUNKS)),
            pltpu.SemaphoreType.DMA((rows // tree + 2,)),
        ],
        compiler_params=params(16),
        name="tree_attention",
    )(normed, w_key, w_value, turn, q, ancestors)


def join_kernel(a_hbm, b_hbm, out_ref, sems):
    n = a_hbm.shape[0]
    copies = [
        pltpu.make_async_copy(ref, out_ref.at[pl.ds(i * n, n)], sems.at[i])
        for i, ref in enumerate((a_hbm, b_hbm))
    ]
    for c in copies:
        c.start()
    for c in copies:
        c.wait()


def join_call(a, b):
    return pl.pallas_call(
        join_kernel,
        in_specs=[HBM, HBM],
        out_specs=VM,
        out_shape=jax.ShapeDtypeStruct((2 * a.shape[0],) + a.shape[1:], a.dtype),
        scratch_shapes=[pltpu.SemaphoreType.DMA((2,))],
        compiler_params=params(4),
        name="join",
    )(a, b)


def halves_kernel(right_ref, left_ref, k_ref, v_ref):
    n = k_ref.shape[0]
    k_ref[...] = right_ref[pl.ds(0, n)]
    v_ref[...] = left_ref[pl.ds(n, n)]


def halves_call(right, left):
    half = jax.ShapeDtypeStruct((right.shape[0] // 2,) + right.shape[1:], right.dtype)
    return pl.pallas_call(
        halves_kernel,
        in_specs=[VM, VM],
        out_specs=[VM, VM],
        out_shape=[half, half],
        compiler_params=params(8),
        name="halves",
    )(right, left)


def prompt_sum(q, g, pieces, ones):
    weights, values = [], []
    for kref, koff, vref, voff in pieces:
        weights.append(jnp.exp2(dot_nt(q, kref[koff + g])).astype(BF16))
        values.append(jnp.concatenate([vref[voff + g], ones], axis=1))
    return dot(jnp.concatenate(weights, axis=1), jnp.concatenate(values, axis=0))


def near_pieces(kv, kv_r, kv_l):
    n = kv.shape[0] // 2
    return [(kv, 0, kv, n), (kv_r, 0, kv_r, n), (kv_l, 0, kv_l, n)]


def source_of(at_ref, requests, shift, n_tok):
    return lax.rem(at_ref[0] + n_tok - shift, n_tok) * requests


def near_kernel(group_ref, at_ref, kv, kv_r, kv_l, *refs, requests, shifts, n_tok):
    hd = kv.shape[2]
    qrows = refs[0].shape[0] // requests
    pieces = near_pieces(kv, kv_r, kv_l)
    ones = jnp.ones((kv.shape[1], hd), BF16)
    for shift, q_ref, out_ref in zip(shifts, refs[: len(shifts)], refs[len(shifts) :]):
        base = source_of(at_ref, requests, shift, n_tok)
        for r in range(requests):
            at = pl.ds(r * qrows, qrows)
            out_ref[at, :] = prompt_sum(q_ref[at, :], group_ref[base + r], pieces, ones)


def near_call(groups, at, qs, kv, kv_r, kv_l, requests, shifts, n_tok):
    rows, hd = qs[0].shape
    n = len(shifts)
    return pl.pallas_call(
        lambda *refs: near_kernel(*refs, requests=requests, shifts=shifts, n_tok=n_tok),
        in_specs=[SMEM, SMEM] + [VM] * (3 + n),
        out_specs=[VM] * n,
        out_shape=[jax.ShapeDtypeStruct((rows, 2 * hd), F32)] * n,
        compiler_params=params(16),
        name="prompt_near",
    )(groups, at, kv, kv_r, kv_l, *qs)


def far_kernel(group_ref, at_ref, k_o, v_o, *refs, requests, shifts, n_tok):
    hd = k_o.shape[2]
    n = len(shifts)
    ones = jnp.ones((k_o.shape[1], hd), BF16)
    for shift, q_ref, near_ref, out_ref in zip(shifts, refs[:n], refs[n : 2 * n], refs[2 * n :]):
        qrows = q_ref.shape[0] // requests
        diagonal = lax.broadcasted_iota(jnp.int32, (qrows, hd), 0) == lax.broadcasted_iota(
            jnp.int32, (qrows, hd), 1
        )
        base = source_of(at_ref, requests, shift, n_tok)
        totals = []
        for r in range(requests):
            at = pl.ds(r * qrows, qrows)
            acc = near_ref[at, :] + prompt_sum(
                q_ref[at, :], group_ref[base + r], [(k_o, 0, v_o, 0)], ones
            )
            out_ref[at, :] = acc[:, :hd].astype(BF16)
            totals.append(jnp.sum(jnp.where(diagonal, acc[:, hd:], 0.0), axis=0, keepdims=True))
        total = jnp.concatenate(totals, axis=0)
        high = total.astype(BF16)
        low = (total - high.astype(F32)).astype(BF16)
        out_ref[pl.ds(requests * qrows, 2 * requests), :] = jnp.concatenate([high, low], axis=0)


def far_call(groups, at, nears, qs, k_o, v_o, requests, shifts, n_tok):
    rows, hd = qs[0].shape
    n = len(shifts)
    return pl.pallas_call(
        lambda *refs: far_kernel(*refs, requests=requests, shifts=shifts, n_tok=n_tok),
        in_specs=[SMEM, SMEM] + [VM] * (2 + 2 * n),
        out_specs=[VM] * n,
        out_shape=[jax.ShapeDtypeStruct((rows + 2 * requests, hd), BF16)] * n,
        compiler_params=params(16),
        name="prompt_far",
    )(groups, at, k_o, v_o, *qs, *nears)


def home_kernel(
    group_ref, at_ref, len_ref, q_ref, kv, kv_r, kv_l, k_o, v_o, own_hbm, ck_hbm, cv_hbm, out_ref,
    own_ref, keys, values, where_ref, sems, own_sem,
):
    requests, slots, hd = keys.shape
    qrows = q_ref.shape[0] // requests
    piece = slots // PIECES

    def copies(r, i):
        at = pl.ds(i * piece, piece)
        return (
            pltpu.make_async_copy(ck_hbm.at[r, at], keys.at[r, at], sems.at[0, r, i]),
            pltpu.make_async_copy(cv_hbm.at[r, at], values.at[r, at], sems.at[1, r, i]),
        )

    def each_copy(act):
        for i in range(PIECES):
            for r in range(requests):
                if i == 0:
                    for c in copies(r, i):
                        act(c)
                else:

                    @pl.when(len_ref[r] > i * piece)
                    def _(r=r, i=i):
                        for c in copies(r, i):
                            act(c)

    get_own = pltpu.make_async_copy(own_hbm, own_ref, own_sem)
    get_own.start()
    each_copy(lambda c: c.start())
    count = 0
    for r in range(requests):

        def note(b, n, r=r):
            where_ref[0, n] = r
            where_ref[1, n] = b * KB
            return n + 1

        count = lax.fori_loop(0, (len_ref[r] + KB - 1) // KB, note, count)
    for j in range(LANES):
        where_ref[0, count + j] = requests - 1
        where_ref[1, count + j] = 0
    pieces = near_pieces(kv, kv_r, kv_l) + [(k_o, 0, v_o, 0)]
    ones = jnp.ones((KB, hd), BF16)
    get_own.wait()
    for r in range(requests):
        at = pl.ds(r * qrows, qrows)
        out_ref[at, :] = own_ref[at, :] + prompt_sum(
            q_ref[at, :], group_ref[at_ref[0] * requests + r], pieces, ones
        )
    column = lax.broadcasted_iota(jnp.int32, (qrows, KB), 1)
    each_copy(lambda c: c.wait())

    def step(i, _):
        parts = []
        for j in range(LANES):
            n = i * LANES + j
            r = where_ref[0, n]
            first = pl.multiple_of(where_ref[1, n], KB)
            at = pl.ds(pl.multiple_of(r * qrows, qrows), qrows)
            limit = jnp.where(n < count, len_ref[r] - first, 0)
            s = dot_nt(q_ref[at, :], keys[r, pl.ds(first, KB), :])
            p = jnp.where(column < limit, jnp.exp2(s), 0.0).astype(BF16)
            both = jnp.concatenate([values[r, pl.ds(first, KB), :], ones], axis=1)
            parts.append((at, dot(p, both)))
        for at, d in parts:
            out_ref[at, :] += d
        return 0

    lax.fori_loop(0, (count + LANES - 1) // LANES, step, 0)


def home_call(groups, at, lengths, q, prompts, own, cache_keys, cache_values):
    requests, slots, _ = cache_keys.shape
    return pl.pallas_call(
        home_kernel,
        in_specs=[SMEM, SMEM, SMEM] + [VM] * 6 + [HBM] * 3,
        out_specs=VM,
        out_shape=jax.ShapeDtypeStruct(own.shape, F32),
        scratch_shapes=[
            pltpu.VMEM(own.shape, F32),
            pltpu.VMEM(cache_keys.shape, BF16),
            pltpu.VMEM(cache_values.shape, BF16),
            pltpu.SMEM((2, requests * slots // KB + LANES), jnp.int32),
            pltpu.SemaphoreType.DMA((2, requests, PIECES)),
            pltpu.SemaphoreType.DMA,
        ],
        compiler_params=params(20),
        name="home_attention",
    )(groups, at, lengths, q, *prompts, own, cache_keys, cache_values)


def merge_kernel(home_ref, a_ref, b_ref, c_ref, out_ref, *, requests):
    hd = a_ref.shape[1]
    qrows = home_ref.shape[0] // requests
    tree = out_ref.shape[0] // requests
    total = None
    for ref in (a_ref, b_ref, c_ref):
        both = ref[pl.ds(requests * qrows, 2 * requests), :].astype(F32)
        t = both[:requests] + both[requests:]
        total = t if total is None else total + t
    diagonal = lax.broadcasted_iota(jnp.int32, (qrows, hd), 0) == lax.broadcasted_iota(
        jnp.int32, (qrows, hd), 1
    )
    for r in range(requests):
        at = pl.ds(r * qrows, qrows)
        num = home_ref[at, pl.ds(0, hd)]
        for ref in (a_ref, b_ref, c_ref):
            num = num + ref[at, :].astype(F32)
        den = home_ref[at, pl.ds(hd, hd)] + jnp.sum(
            jnp.where(diagonal, jnp.broadcast_to(total[r : r + 1], (qrows, hd)), 0.0),
            axis=1,
            keepdims=True,
        )
        out = (num / den).astype(BF16)
        for g in range(qrows // tree):
            out_ref[pl.ds(r * tree, tree), pl.ds(g * hd, hd)] = out[g * tree : (g + 1) * tree]


def merge_call(home, a, b, c, requests, rows):
    hd = a.shape[1]
    return pl.pallas_call(
        lambda *refs: merge_kernel(*refs, requests=requests),
        in_specs=[VM] * 4,
        out_specs=VM,
        out_shape=jax.ShapeDtypeStruct((rows, home.shape[0] // rows * hd), BF16),
        compiler_params=params(8),
        name="merge",
    )(home, a, b, c)


def columns_kernel(mdl_ref, w_hbm, mine_ref, send_ref, sems):
    count, _, cols = mine_ref.shape
    copies = []
    for i in range(count):
        there = lax.rem(mdl_ref[0] // 2 + i, count)
        for j, ref in enumerate((mine_ref, send_ref)):
            side = lax.rem(mdl_ref[0] + j, 2)
            start = pl.multiple_of((2 * there + side) * cols, 128)
            c = pltpu.make_async_copy(w_hbm.at[:, pl.ds(start, cols)], ref.at[i], sems.at[j, i])
            c.start()
            copies.append(c)
    for c in copies:
        c.wait()


def columns_call(mdl, w_out, count):
    cols = w_out.shape[1] // (2 * count)
    return pl.pallas_call(
        columns_kernel,
        in_specs=[SMEM, HBM],
        out_specs=[VM, VM],
        out_shape=[jax.ShapeDtypeStruct((count, w_out.shape[0], cols), BF16)] * 2,
        scratch_shapes=[pltpu.SemaphoreType.DMA((2, count))],
        compiler_params=params(8),
        name="out_columns",
    )(mdl, w_out)


def out_kernel(mine_ref, other_ref, *refs):
    n = len(refs) // 3
    for wa, wb, out in zip(refs[:n], refs[n : 2 * n], refs[2 * n :]):
        out[...] = (dot(mine_ref[...], wa[0]) + dot(other_ref[...], wb[0])).astype(out.dtype)


def out_call(mine, other, w_mine, w_other, shifts, dtype):
    rows, inner = mine.shape
    cols = w_other.shape[2]
    whole = pl.BlockSpec((rows, inner), lambda i: (0, 0))
    chunks = [pl.BlockSpec((1, inner, cols), lambda i, n=n: (n, 0, 0)) for n in shifts]
    return pl.pallas_call(
        out_kernel,
        grid=(1,),
        in_specs=[whole, whole] + chunks * 2,
        out_specs=[pl.BlockSpec((rows, cols), lambda i: (0, 0))] * len(shifts),
        out_shape=[jax.ShapeDtypeStruct((rows, cols), dtype)] * len(shifts),
        compiler_params=params(16),
        name="out_proj",
    )(mine, other, *([w_mine] * len(shifts)), *([w_other] * len(shifts)))


def last_kernel(acc_ref, at_ref, own_ref, a_ref, b_ref, c_ref, tok_hbm, out_ref, rows_ref, tok, sums, kept, sem):
    cols = own_ref.shape[1]
    requests, most = acc_ref.shape
    tree = own_ref.shape[0] // requests
    get = pltpu.make_async_copy(
        tok_hbm.at[:, pl.ds(pl.multiple_of(at_ref[0] * cols, 128), cols)], tok, sem
    )
    get.start()
    total = own_ref[...] + a_ref[...].astype(F32) + b_ref[...].astype(F32) + c_ref[...].astype(F32)
    rounded = total.astype(BF16)
    out_ref[...] = rounded
    get.wait()
    sums[...] = tok[...].astype(F32) + rounded.astype(F32)
    for r in range(requests):
        for k in range(most):
            slot = acc_ref[r, k]
            row = sums[pl.ds(r * tree + jnp.maximum(slot, 0), 1), :]
            kept[r, pl.ds(k, 1), :] = jnp.where(slot >= 0, row, 0.0)
    rows_ref[...] = kept[...].astype(BF16)


def last_call(accepted, column, own, a, b, c, tokens):
    rows, cols = own.shape
    requests, most = accepted.shape
    return pl.pallas_call(
        last_kernel,
        in_specs=[SMEM, SMEM, VM, VM, VM, VM, HBM],
        out_specs=[VM, VM],
        out_shape=[
            jax.ShapeDtypeStruct((rows, cols), BF16),
            jax.ShapeDtypeStruct((requests, most, cols), BF16),
        ],
        scratch_shapes=[
            pltpu.VMEM((rows, cols), BF16),
            pltpu.VMEM((rows, cols), F32),
            pltpu.VMEM((requests, most, cols), F32),
            pltpu.SemaphoreType.DMA,
        ],
        compiler_params=params(8),
        name="last_sums",
    )(accepted, column, own, a, b, c, tokens)


def shards(
    tokens, norm_gain, w_query, w_key, w_value, w_out, prompt_keys, prompt_values, cache_keys,
    cache_values, cache_length, request_group, ancestors, accepted,
):
    requests, tree = ancestors.shape[:2]
    rows = tokens.shape[0]
    hd = prompt_keys.shape[3]
    n_tok = lax.axis_size("tok")
    n_mdl = lax.axis_size("mdl")
    n_y = 4
    n_z = n_tok // n_y
    n_x = n_mdl // 2
    tok = lax.axis_index("tok")
    mdl = lax.axis_index("mdl")

    def along_y(v, n):
        perm = [(t, t // n_y * n_y + (t + n) % n_y) for t in range(n_tok)]
        return lax.ppermute(v, "tok", perm)

    def along_z(v, n):
        return lax.ppermute(v, "tok", [(t, (t + n * n_y) % n_tok) for t in range(n_tok)])

    def along_x(v, n):
        return lax.ppermute(v, "mdl", [(m, (m + 2 * n) % n_mdl) for m in range(n_mdl)])

    def other_core(v):
        return lax.ppermute(v, "mdl", [(m, m ^ 1) for m in range(n_mdl)])

    def in_hbm(v):
        return pltpu.with_memory_space_constraint(v, pltpu.HBM)

    tok_at = jnp.reshape(tok, (1,)).astype(jnp.int32)
    mdl_at = jnp.reshape(mdl, (1,)).astype(jnp.int32)

    squeeze = lambda v: v.reshape(v.shape[0], v.shape[1], v.shape[3])
    kv = join_call(in_hbm(squeeze(prompt_keys)), in_hbm(squeeze(prompt_values)))
    kv_r = along_y(kv, 1)
    kv_l = along_y(kv, -1)

    exponent = np.arange(hd // 2, dtype=np.float64) * (2.0 / hd)
    inverse = jnp.asarray(np.tile(THETA**-exponent, 2)[None, :], dtype=F32)
    table = ancestors.reshape(rows, tree)
    q, normed, turn = query_call(
        *map(
            in_hbm,
            (cache_length, tokens, norm_gain.reshape(-1, hd), w_query, table, inverse),
        )
    )
    shifts = (2, 1, -1)
    q_far = [along_z(q, n) for n in shifts]
    own = tree_call(*map(in_hbm, (normed, w_key, w_value, turn)), q, in_hbm(table))

    k_half, v_half = halves_call(kv_r, kv_l)
    k_o = along_y(k_half, 1)
    v_o = along_y(v_half, -1)
    prompts = (kv, kv_r, kv_l, k_o, v_o)

    w_mine, w_send = columns_call(mdl_at, in_hbm(w_out), n_x)
    w_other = other_core(w_send)

    turns = [n % n_z * n_y for n in shifts]
    nears = near_call(
        request_group, tok_at, q_far, kv, in_hbm(kv_r), in_hbm(kv_l), requests, turns, n_tok
    )
    parts = far_call(request_group, tok_at, nears, q_far, k_o, v_o, requests, turns, n_tok)
    back = [along_z(part, -n) for n, part in zip(shifts, parts)]
    home = home_call(
        request_group, tok_at, cache_length, q, prompts, in_hbm(own),
        in_hbm(squeeze(cache_keys)), in_hbm(squeeze(cache_values)),
    )
    attended = merge_call(home, *back, requests, rows)

    attended_other = other_core(attended)
    sent = []
    for group in ((2,), (1, -1), (0,)):
        outs = out_call(
            attended, attended_other, w_mine, w_other, [n % n_x for n in group],
            F32 if group == (0,) else BF16,
        )
        sent += [along_x(o, n) if n else o for o, n in zip(outs, group)]
    far, up, down, own_sum = sent
    return tuple(last_call(accepted, mdl_at, own_sum, far, up, down, in_hbm(tokens)))


def solution(mesh):
    placed = (
        P("tok", None),
        P(),
        P(None, "mdl"),
        P(None, "mdl"),
        P(None, "mdl"),
        P("mdl", None),
        P(None, "tok", "mdl", None),
        P(None, "tok", "mdl", None),
        P("tok", None, "mdl", None),
        P("tok", None, "mdl", None),
        P("tok"),
        P(),
        P("tok", None, None),
        P("tok", None),
    )

    return jax.shard_map(
        shards,
        mesh=mesh,
        in_specs=placed,
        out_specs=(P("tok", "mdl"), P("tok", None, "mdl")),
        check_vma=False,
    )
```

```python
import math

import jax
import jax.numpy as jnp
import numpy as np
from jax import lax
from jax.experimental import pallas as pl
from jax.experimental.pallas import tpu as pltpu
from jax.sharding import PartitionSpec as P


PROMPT = 4096
THETA = 100000000.0
EPS = 1e-05

F32 = jnp.float32
BF16 = jnp.bfloat16

HBM = pl.BlockSpec(memory_space=pltpu.HBM)
SMEM = pl.BlockSpec(memory_space=pltpu.SMEM)
VM = pl.BlockSpec(memory_space=pltpu.VMEM)
CHUNKS = 5
KB = 256
PIECES = 2
LANES = 8
NT = (((1,), (1,)), ((), ()))


def params(mib):
    return pltpu.CompilerParams(vmem_limit_bytes=mib * 1024 * 1024)


def dot(a, b):
    return jnp.dot(a, b, preferred_element_type=F32)


def dot_nt(a, b):
    return lax.dot_general(a, b, NT, preferred_element_type=F32)


def rotate(x, cosine, sine):
    return x * cosine + pltpu.roll(x, x.shape[1] // 2, 1) * sine


def project_kernel(
    len_hbm, tok_hbm, gain_hbm, wq_hbm, wk_hbm, wv_hbm, anc_hbm, inv_hbm, q_ref, k_ref, v_ref,
    lengths, tok, gain, w, table, inverse, sems, csems,
):
    rows, width = tok.shape
    requests = lengths.shape[0]
    tree = rows // requests
    hd = inverse.shape[1]
    inner = wq_hbm.shape[1]
    part = width // CHUNKS
    firsts = [
        pltpu.make_async_copy(source, target, sems.at[i])
        for i, (source, target) in enumerate(
            ((anc_hbm, table), (len_hbm, lengths), (inv_hbm, inverse), (gain_hbm, gain))
        )
    ]
    for c in firsts:
        c.start()
    copies = []
    for i in range(CHUNKS):
        at = pl.ds(i * part, part)
        four = (
            pltpu.make_async_copy(tok_hbm.at[:, at], tok.at[:, at], csems.at[0, i]),
            pltpu.make_async_copy(wq_hbm.at[at], w.at[at, pl.ds(0, inner)], csems.at[1, i]),
            pltpu.make_async_copy(wk_hbm.at[at], w.at[at, pl.ds(inner, hd)], csems.at[2, i]),
            pltpu.make_async_copy(wv_hbm.at[at], w.at[at, pl.ds(inner + hd, hd)], csems.at[3, i]),
        )
        for c in four:
            c.start()
        copies.append(four)
    for c in firsts:
        c.wait()
    depth = jnp.sum(table[...], axis=1, keepdims=True).astype(F32) - 1.0
    places = jnp.concatenate(
        [
            depth[r * tree : (r + 1) * tree] + (PROMPT + lengths[r]).astype(F32)
            for r in range(requests)
        ],
        axis=0,
    )
    angles = places * inverse[...]
    lane = lax.broadcasted_iota(jnp.int32, angles.shape, 1)
    cosine = jnp.cos(angles)
    sine = jnp.sin(angles)
    sine = jnp.where(lane < hd // 2, -sine, sine)
    gains = gain[...].astype(F32)
    step = part // gain.shape[1]
    acc = None
    squares = None
    for i in range(CHUNKS):
        for c in copies[i]:
            c.wait()
        wide = tok[:, i * part : (i + 1) * part].astype(F32)
        own_gain = jnp.concatenate([gains[j : j + 1] for j in range(i * step, (i + 1) * step)], axis=1)
        d = dot((wide * own_gain).astype(BF16), w[i * part : (i + 1) * part, :])
        acc = d if acc is None else acc + d
        square = wide * wide
        for j in range(step):
            t = square[:, j * gain.shape[1] : (j + 1) * gain.shape[1]]
            squares = t if squares is None else squares + t
    scale = lax.rsqrt(jnp.sum(squares, axis=1, keepdims=True) * (1.0 / width) + EPS)
    heads = inner // hd
    scaled = scale * (hd**-0.5 * math.log2(math.e))
    for g in range(heads):
        turned = rotate(acc[:, g * hd : (g + 1) * hd] * scaled, cosine, sine).astype(BF16)
        for r in range(requests):
            q_ref[pl.ds((r * heads + g) * tree, tree), :] = turned[r * tree : (r + 1) * tree]
    k_ref[...] = rotate(acc[:, inner : inner + hd] * scale, cosine, sine).astype(BF16)
    v_ref[...] = (acc[:, inner + hd :] * scale).astype(BF16)


def project_call(lengths, tokens, gain, w_query, w_key, w_value, ancestors, inverse):
    rows, width = tokens.shape
    hd = inverse.shape[1]
    inner = w_query.shape[1]
    return pl.pallas_call(
        project_kernel,
        in_specs=[HBM] * 8,
        out_specs=[VM, VM, VM],
        out_shape=[
            jax.ShapeDtypeStruct((rows * inner // hd, hd), BF16),
            jax.ShapeDtypeStruct((rows, hd), BF16),
            jax.ShapeDtypeStruct((rows, hd), BF16),
        ],
        scratch_shapes=[
            pltpu.SMEM(lengths.shape, jnp.int32),
            pltpu.VMEM((rows, width), BF16),
            pltpu.VMEM(gain.shape, BF16),
            pltpu.VMEM((width, inner + 2 * hd), BF16),
            pltpu.VMEM(ancestors.shape, jnp.int32),
            pltpu.VMEM(inverse.shape, F32),
            pltpu.SemaphoreType.DMA((4,)),
            pltpu.SemaphoreType.DMA((4, CHUNKS)),
        ],
        compiler_params=params(28),
        name="projections",
    )(lengths, tokens, gain, w_query, w_key, w_value, ancestors, inverse)


def join_kernel(a_hbm, b_hbm, out_ref, sems):
    n = a_hbm.shape[0]
    copies = [
        pltpu.make_async_copy(ref, out_ref.at[pl.ds(i * n, n)], sems.at[i])
        for i, ref in enumerate((a_hbm, b_hbm))
    ]
    for c in copies:
        c.start()
    for c in copies:
        c.wait()


def join_call(a, b):
    return pl.pallas_call(
        join_kernel,
        in_specs=[HBM, HBM],
        out_specs=VM,
        out_shape=jax.ShapeDtypeStruct((2 * a.shape[0],) + a.shape[1:], a.dtype),
        scratch_shapes=[pltpu.SemaphoreType.DMA((2,))],
        compiler_params=params(4),
        name="join",
    )(a, b)


def halves_kernel(right_ref, left_ref, k_ref, v_ref):
    n = k_ref.shape[0]
    k_ref[...] = right_ref[pl.ds(0, n)]
    v_ref[...] = left_ref[pl.ds(n, n)]


def halves_call(right, left):
    half = jax.ShapeDtypeStruct((right.shape[0] // 2,) + right.shape[1:], right.dtype)
    return pl.pallas_call(
        halves_kernel,
        in_specs=[VM, VM],
        out_specs=[VM, VM],
        out_shape=[half, half],
        compiler_params=params(8),
        name="halves",
    )(right, left)


def prompt_sum(q, g, pieces, ones):
    weights, values = [], []
    for kref, koff, vref, voff in pieces:
        weights.append(jnp.exp2(dot_nt(q, kref[koff + g])).astype(BF16))
        values.append(jnp.concatenate([vref[voff + g], ones], axis=1))
    return dot(jnp.concatenate(weights, axis=1), jnp.concatenate(values, axis=0))


def near_pieces(kv, kv_r, kv_l):
    n = kv.shape[0] // 2
    return [(kv, 0, kv, n), (kv_r, 0, kv_r, n), (kv_l, 0, kv_l, n)]


def source_of(at_ref, requests, shift, n_tok):
    return lax.rem(at_ref[0] + n_tok - shift, n_tok) * requests


def near_kernel(group_ref, at_ref, kv, kv_r, kv_l, *refs, requests, shifts, n_tok):
    hd = kv.shape[2]
    qrows = refs[0].shape[0] // requests
    pieces = near_pieces(kv, kv_r, kv_l)
    ones = jnp.ones((kv.shape[1], hd), BF16)
    for shift, q_ref, out_ref in zip(shifts, refs[: len(shifts)], refs[len(shifts) :]):
        base = source_of(at_ref, requests, shift, n_tok)
        for r in range(requests):
            at = pl.ds(r * qrows, qrows)
            out_ref[at, :] = prompt_sum(q_ref[at, :], group_ref[base + r], pieces, ones)


def near_call(groups, at, qs, kv, kv_r, kv_l, requests, shifts, n_tok):
    rows, hd = qs[0].shape
    n = len(shifts)
    return pl.pallas_call(
        lambda *refs: near_kernel(*refs, requests=requests, shifts=shifts, n_tok=n_tok),
        in_specs=[SMEM, SMEM] + [VM] * (3 + n),
        out_specs=[VM] * n,
        out_shape=[jax.ShapeDtypeStruct((rows, 2 * hd), F32)] * n,
        compiler_params=params(16),
        name="prompt_near",
    )(groups, at, kv, kv_r, kv_l, *qs)


def far_kernel(group_ref, at_ref, k_o, v_o, *refs, requests, shifts, n_tok):
    hd = k_o.shape[2]
    n = len(shifts)
    ones = jnp.ones((k_o.shape[1], hd), BF16)
    for shift, q_ref, near_ref, out_ref in zip(shifts, refs[:n], refs[n : 2 * n], refs[2 * n :]):
        qrows = q_ref.shape[0] // requests
        diagonal = lax.broadcasted_iota(jnp.int32, (qrows, hd), 0) == lax.broadcasted_iota(
            jnp.int32, (qrows, hd), 1
        )
        base = source_of(at_ref, requests, shift, n_tok)
        totals = []
        for r in range(requests):
            at = pl.ds(r * qrows, qrows)
            acc = near_ref[at, :] + prompt_sum(
                q_ref[at, :], group_ref[base + r], [(k_o, 0, v_o, 0)], ones
            )
            out_ref[at, :] = acc[:, :hd].astype(BF16)
            totals.append(jnp.sum(jnp.where(diagonal, acc[:, hd:], 0.0), axis=0, keepdims=True))
        total = jnp.concatenate(totals, axis=0)
        high = total.astype(BF16)
        low = (total - high.astype(F32)).astype(BF16)
        out_ref[pl.ds(requests * qrows, 2 * requests), :] = jnp.concatenate([high, low], axis=0)


def far_call(groups, at, nears, qs, k_o, v_o, requests, shifts, n_tok):
    rows, hd = qs[0].shape
    n = len(shifts)
    return pl.pallas_call(
        lambda *refs: far_kernel(*refs, requests=requests, shifts=shifts, n_tok=n_tok),
        in_specs=[SMEM, SMEM] + [VM] * (2 + 2 * n),
        out_specs=[VM] * n,
        out_shape=[jax.ShapeDtypeStruct((rows + 2 * requests, hd), BF16)] * n,
        compiler_params=params(16),
        name="prompt_far",
    )(groups, at, k_o, v_o, *qs, *nears)


def home_kernel(
    group_ref, at_ref, len_ref, q_ref, kv, kv_r, kv_l, k_o, v_o, new_k, new_v, anc_hbm, ck_hbm,
    cv_hbm, out_ref, anc_ref, keys, values, where_ref, sems, anc_sem,
):
    requests, slots, hd = keys.shape
    qrows = q_ref.shape[0] // requests
    piece = slots // PIECES

    def copies(r, i):
        at = pl.ds(i * piece, piece)
        return (
            pltpu.make_async_copy(ck_hbm.at[r, at], keys.at[r, at], sems.at[0, r, i]),
            pltpu.make_async_copy(cv_hbm.at[r, at], values.at[r, at], sems.at[1, r, i]),
        )

    def each_copy(act):
        for i in range(PIECES):
            for r in range(requests):
                if i == 0:
                    for c in copies(r, i):
                        act(c)
                else:

                    @pl.when(len_ref[r] > i * piece)
                    def _(r=r, i=i):
                        for c in copies(r, i):
                            act(c)

    get_anc = pltpu.make_async_copy(anc_hbm, anc_ref, anc_sem)
    get_anc.start()
    tree = anc_ref.shape[1]
    each_copy(lambda c: c.start())
    count = 0
    for r in range(requests):

        def note(b, n, r=r):
            where_ref[0, n] = r
            where_ref[1, n] = b * KB
            return n + 1

        count = lax.fori_loop(0, (len_ref[r] + KB - 1) // KB, note, count)
    for j in range(LANES):
        where_ref[0, count + j] = requests - 1
        where_ref[1, count + j] = 0
    pieces = near_pieces(kv, kv_r, kv_l) + [(k_o, 0, v_o, 0)]
    ones = jnp.ones((KB, hd), BF16)
    get_anc.wait()
    for r in range(requests):
        at = pl.ds(r * qrows, qrows)
        mine = pl.ds(r * tree, tree)
        q = q_ref[at, :]
        seen = jnp.concatenate([anc_ref[mine, :]] * (qrows // tree), axis=0)
        p = jnp.where(seen > 0, jnp.exp2(dot_nt(q, new_k[mine, :])), 0.0).astype(BF16)
        out_ref[at, :] = prompt_sum(
            q, group_ref[at_ref[0] * requests + r], pieces, ones
        ) + dot(p, jnp.concatenate([new_v[mine, :], ones[:tree]], axis=1))
    column = lax.broadcasted_iota(jnp.int32, (qrows, KB), 1)
    each_copy(lambda c: c.wait())

    def step(i, _):
        parts = []
        for j in range(LANES):
            n = i * LANES + j
            r = where_ref[0, n]
            first = pl.multiple_of(where_ref[1, n], KB)
            at = pl.ds(pl.multiple_of(r * qrows, qrows), qrows)
            limit = jnp.where(n < count, len_ref[r] - first, 0)
            s = dot_nt(q_ref[at, :], keys[r, pl.ds(first, KB), :])
            p = jnp.where(column < limit, jnp.exp2(s), 0.0).astype(BF16)
            both = jnp.concatenate([values[r, pl.ds(first, KB), :], ones], axis=1)
            parts.append((at, dot(p, both)))
        for at, d in parts:
            out_ref[at, :] += d
        return 0

    lax.fori_loop(0, (count + LANES - 1) // LANES, step, 0)


def home_call(groups, at, lengths, q, prompts, new_k, new_v, ancestors, cache_keys, cache_values):
    requests, slots, hd = cache_keys.shape
    return pl.pallas_call(
        home_kernel,
        in_specs=[SMEM, SMEM, SMEM] + [VM] * 8 + [HBM] * 3,
        out_specs=VM,
        out_shape=jax.ShapeDtypeStruct((q.shape[0], 2 * hd), F32),
        scratch_shapes=[
            pltpu.VMEM(ancestors.shape, jnp.int32),
            pltpu.VMEM(cache_keys.shape, BF16),
            pltpu.VMEM(cache_values.shape, BF16),
            pltpu.SMEM((2, requests * slots // KB + LANES), jnp.int32),
            pltpu.SemaphoreType.DMA((2, requests, PIECES)),
            pltpu.SemaphoreType.DMA,
        ],
        compiler_params=params(20),
        name="home_attention",
    )(groups, at, lengths, q, *prompts, new_k, new_v, ancestors, cache_keys, cache_values)


def merge_kernel(home_ref, a_ref, b_ref, c_ref, out_ref, *, requests):
    hd = a_ref.shape[1]
    qrows = home_ref.shape[0] // requests
    tree = out_ref.shape[0] // requests
    total = None
    for ref in (a_ref, b_ref, c_ref):
        both = ref[pl.ds(requests * qrows, 2 * requests), :].astype(F32)
        t = both[:requests] + both[requests:]
        total = t if total is None else total + t
    diagonal = lax.broadcasted_iota(jnp.int32, (qrows, hd), 0) == lax.broadcasted_iota(
        jnp.int32, (qrows, hd), 1
    )
    for r in range(requests):
        at = pl.ds(r * qrows, qrows)
        num = home_ref[at, pl.ds(0, hd)]
        for ref in (a_ref, b_ref, c_ref):
            num = num + ref[at, :].astype(F32)
        den = home_ref[at, pl.ds(hd, hd)] + jnp.sum(
            jnp.where(diagonal, jnp.broadcast_to(total[r : r + 1], (qrows, hd)), 0.0),
            axis=1,
            keepdims=True,
        )
        out = (num / den).astype(BF16)
        for g in range(qrows // tree):
            out_ref[pl.ds(r * tree, tree), pl.ds(g * hd, hd)] = out[g * tree : (g + 1) * tree]


def merge_call(home, a, b, c, requests, rows):
    hd = a.shape[1]
    return pl.pallas_call(
        lambda *refs: merge_kernel(*refs, requests=requests),
        in_specs=[VM] * 4,
        out_specs=VM,
        out_shape=jax.ShapeDtypeStruct((rows, home.shape[0] // rows * hd), BF16),
        compiler_params=params(8),
        name="merge",
    )(home, a, b, c)


def pick(acc_ref, x, tree):
    rows = []
    slot = lax.broadcasted_iota(jnp.int32, (tree, acc_ref.shape[1]), 0)
    for r in range(acc_ref.shape[0]):
        chosen = (slot == acc_ref[r : r + 1, :]).astype(F32).astype(BF16)
        rows.append(
            lax.dot_general(
                chosen, x[r * tree : (r + 1) * tree], (((0,), (0,)), ((), ())),
                preferred_element_type=F32,
            )
        )
    return rows


def columns_kernel(mdl_ref, acc_ref, w_hbm, tok_hbm, mine_ref, send_ref, tok_out, tok, sems, sem):
    count, _, cols = mine_ref.shape
    get = pltpu.make_async_copy(
        tok_hbm.at[:, pl.ds(pl.multiple_of(mdl_ref[0] * cols, 128), cols)], tok, sem
    )
    get.start()
    copies = []
    for i in range(count):
        there = lax.rem(mdl_ref[0] // 2 + i, count)
        for j, ref in enumerate((mine_ref, send_ref)):
            side = lax.rem(mdl_ref[0] + j, 2)
            start = pl.multiple_of((2 * there + side) * cols, 128)
            c = pltpu.make_async_copy(w_hbm.at[:, pl.ds(start, cols)], ref.at[i], sems.at[j, i])
            c.start()
            copies.append(c)
    get.wait()
    for r, row in enumerate(pick(acc_ref, tok[...], tok.shape[0] // acc_ref.shape[0])):
        tok_out[r] = row
    for c in copies:
        c.wait()


def columns_call(mdl, accepted, w_out, tokens, count):
    cols = w_out.shape[1] // (2 * count)
    return pl.pallas_call(
        columns_kernel,
        in_specs=[SMEM, VM, HBM, HBM],
        out_specs=[VM, VM, VM],
        out_shape=[jax.ShapeDtypeStruct((count, w_out.shape[0], cols), BF16)] * 2
        + [jax.ShapeDtypeStruct(accepted.shape + (cols,), F32)],
        scratch_shapes=[
            pltpu.VMEM((tokens.shape[0], cols), BF16),
            pltpu.SemaphoreType.DMA((2, count)),
            pltpu.SemaphoreType.DMA,
        ],
        compiler_params=params(12),
        name="out_columns",
    )(mdl, accepted, w_out, tokens)


def first_kernel(mine_ref, w_ref, out_ref):
    out_ref[...] = dot(mine_ref[...], w_ref[0])


def out_first(mine, w_mine, shift):
    rows, inner = mine.shape
    cols = w_mine.shape[2]
    return pl.pallas_call(
        first_kernel,
        grid=(1,),
        in_specs=[
            pl.BlockSpec((rows, inner), lambda i: (0, 0)),
            pl.BlockSpec((1, inner, cols), lambda i: (shift, 0, 0)),
        ],
        out_specs=pl.BlockSpec((rows, cols), lambda i: (0, 0)),
        out_shape=jax.ShapeDtypeStruct((rows, cols), F32),
        compiler_params=params(12),
        name="out_first",
    )(mine, w_mine)


def second_kernel(first_ref, other_ref, w_ref, out_ref):
    out_ref[...] = (first_ref[...] + dot(other_ref[...], w_ref[0])).astype(BF16)


def out_second(first, other, w_other, shift):
    rows, inner = other.shape
    cols = w_other.shape[2]
    flat = lambda i: (0, 0)
    return pl.pallas_call(
        second_kernel,
        grid=(1,),
        in_specs=[
            pl.BlockSpec((rows, cols), flat),
            pl.BlockSpec((rows, inner), flat),
            pl.BlockSpec((1, inner, cols), lambda i: (shift, 0, 0)),
        ],
        out_specs=pl.BlockSpec((rows, cols), flat),
        out_shape=jax.ShapeDtypeStruct((rows, cols), BF16),
        compiler_params=params(12),
        name="out_second",
    )(first, other, w_other)


def out_kernel(mine_ref, other_ref, *refs):
    n = len(refs) // 3
    for wa, wb, out in zip(refs[:n], refs[n : 2 * n], refs[2 * n :]):
        out[...] = (dot(mine_ref[...], wa[0]) + dot(other_ref[...], wb[0])).astype(out.dtype)


def out_call(mine, other, w_mine, w_other, shifts, dtype):
    rows, inner = mine.shape
    cols = w_other.shape[2]
    whole = pl.BlockSpec((rows, inner), lambda i: (0, 0))
    chunks = [pl.BlockSpec((1, inner, cols), lambda i, n=n: (n, 0, 0)) for n in shifts]
    return pl.pallas_call(
        out_kernel,
        grid=(1,),
        in_specs=[whole, whole] + chunks * 2,
        out_specs=[pl.BlockSpec((rows, cols), lambda i: (0, 0))] * len(shifts),
        out_shape=[jax.ShapeDtypeStruct((rows, cols), dtype)] * len(shifts),
        compiler_params=params(16),
        name="out_proj",
    )(mine, other, *([w_mine] * len(shifts)), *([w_other] * len(shifts)))


def last_kernel(acc_ref, own_ref, a_ref, b_ref, c_ref, tok_ref, out_ref, rows_ref):
    total = own_ref[...] + a_ref[...].astype(F32) + b_ref[...].astype(F32) + c_ref[...].astype(F32)
    rounded = total.astype(BF16)
    out_ref[...] = rounded
    for r, row in enumerate(pick(acc_ref, rounded, own_ref.shape[0] // acc_ref.shape[0])):
        rows_ref[r] = (tok_ref[r] + row).astype(BF16)


def last_call(accepted, own, a, b, c, picked):
    rows, cols = own.shape
    return pl.pallas_call(
        last_kernel,
        in_specs=[VM] * 6,
        out_specs=[VM, VM],
        out_shape=[
            jax.ShapeDtypeStruct((rows, cols), BF16),
            jax.ShapeDtypeStruct(picked.shape, BF16),
        ],
        compiler_params=params(8),
        name="last_sums",
    )(accepted, own, a, b, c, picked)


def shards(
    tokens, norm_gain, w_query, w_key, w_value, w_out, prompt_keys, prompt_values, cache_keys,
    cache_values, cache_length, request_group, ancestors, accepted,
):
    requests, tree = ancestors.shape[:2]
    rows = tokens.shape[0]
    hd = prompt_keys.shape[3]
    n_tok = lax.axis_size("tok")
    n_mdl = lax.axis_size("mdl")
    n_y = 4
    n_z = n_tok // n_y
    n_x = n_mdl // 2
    tok = lax.axis_index("tok")
    mdl = lax.axis_index("mdl")

    def along_y(v, n):
        perm = [(t, t // n_y * n_y + (t + n) % n_y) for t in range(n_tok)]
        return lax.ppermute(v, "tok", perm)

    def along_z(v, n):
        return lax.ppermute(v, "tok", [(t, (t + n * n_y) % n_tok) for t in range(n_tok)])

    def along_x(v, n):
        return lax.ppermute(v, "mdl", [(m, (m + 2 * n) % n_mdl) for m in range(n_mdl)])

    def other_core(v):
        return lax.ppermute(v, "mdl", [(m, m ^ 1) for m in range(n_mdl)])

    def in_hbm(v):
        return pltpu.with_memory_space_constraint(v, pltpu.HBM)

    tok_at = jnp.reshape(tok, (1,)).astype(jnp.int32)
    mdl_at = jnp.reshape(mdl, (1,)).astype(jnp.int32)

    squeeze = lambda v: v.reshape(v.shape[0], v.shape[1], v.shape[3])
    kv = join_call(in_hbm(squeeze(prompt_keys)), in_hbm(squeeze(prompt_values)))
    kv_r = along_y(kv, 1)
    kv_l = along_y(kv, -1)

    exponent = np.arange(hd // 2, dtype=np.float64) * (2.0 / hd)
    inverse = jnp.asarray(np.tile(THETA**-exponent, 2)[None, :], dtype=F32)
    table = ancestors.reshape(rows, tree)
    q, new_k, new_v = project_call(
        *map(
            in_hbm,
            (
                cache_length, tokens, norm_gain.reshape(-1, hd), w_query, w_key, w_value, table,
                inverse,
            ),
        )
    )
    shifts = (2, 1, -1)
    q_far = [along_z(q, n) for n in shifts]

    w_mine, w_send, picked = columns_call(mdl_at, accepted, in_hbm(w_out), in_hbm(tokens), n_x)
    w_other = other_core(w_send)

    k_half, v_half = halves_call(kv_r, kv_l)
    k_o = along_y(k_half, 1)
    v_o = along_y(v_half, -1)
    prompts = (kv, kv_r, kv_l, k_o, v_o)

    turns = [n % n_z * n_y for n in shifts]
    nears = near_call(
        request_group, tok_at, q_far, kv, in_hbm(kv_r), in_hbm(kv_l), requests, turns, n_tok
    )
    parts = []
    for some in (slice(0, 1), slice(1, 3)):
        parts += far_call(
            request_group, tok_at, nears[some], q_far[some], k_o, v_o, requests, turns[some],
            n_tok,
        )
    back = [along_z(part, -n) for n, part in zip(shifts, parts)]
    home = home_call(
        request_group, tok_at, cache_length, q, prompts, new_k, new_v, in_hbm(table),
        in_hbm(squeeze(cache_keys)), in_hbm(squeeze(cache_values)),
    )
    attended = merge_call(home, *back, requests, rows)

    attended_other = other_core(attended)
    first = out_first(attended, w_mine, 2)
    far = along_x(out_second(first, attended_other, w_other, 2), 2)
    up, down = out_call(attended, attended_other, w_mine, w_other, (1, n_x - 1), BF16)
    up = along_x(up, 1)
    down = along_x(down, -1)
    (own_sum,) = out_call(attended, attended_other, w_mine, w_other, (0,), F32)
    return tuple(last_call(accepted, own_sum, far, up, down, picked))


def solution(mesh):
    placed = (
        P("tok", None),
        P(),
        P(None, "mdl"),
        P(None, "mdl"),
        P(None, "mdl"),
        P("mdl", None),
        P(None, "tok", "mdl", None),
        P(None, "tok", "mdl", None),
        P("tok", None, "mdl", None),
        P("tok", None, "mdl", None),
        P("tok"),
        P(),
        P("tok", None, None),
        P("tok", None),
    )

    return jax.shard_map(
        shards,
        mesh=mesh,
        in_specs=placed,
        out_specs=(P("tok", "mdl"), P("tok", None, "mdl")),
        check_vma=False,
    )
```

```python
import math

import jax
import jax.numpy as jnp
import numpy as np
from jax import lax
from jax.experimental import pallas as pl
from jax.experimental.pallas import tpu as pltpu
from jax.sharding import PartitionSpec as P


PROMPT = 4096
THETA = 100000000.0
EPS = 1e-05

F32 = jnp.float32
BF16 = jnp.bfloat16

HBM = pl.BlockSpec(memory_space=pltpu.HBM)
SMEM = pl.BlockSpec(memory_space=pltpu.SMEM)
VM = pl.BlockSpec(memory_space=pltpu.VMEM)
CHUNKS = 4
AHEAD = 1
KB = 256
PIECES = 2
LANES = 8
NT = (((1,), (1,)), ((), ()))


def params(mib):
    return pltpu.CompilerParams(vmem_limit_bytes=mib * 1024 * 1024)


def dot(a, b):
    return jnp.dot(a, b, preferred_element_type=F32)


def dot_nt(a, b):
    return lax.dot_general(a, b, NT, preferred_element_type=F32)


def rotate(x, cosine, sine):
    return x * cosine + pltpu.roll(x, x.shape[1] // 2, 1) * sine


def project_kernel(
    len_hbm, tok_hbm, gain_hbm, wq_hbm, wk_hbm, wv_hbm, anc_hbm, inv_hbm, q_ref, k_ref, v_ref,
    lengths, tok, gain, w, table, inverse, sems, csems,
):
    rows, width = tok.shape
    requests = lengths.shape[0]
    tree = rows // requests
    hd = inverse.shape[1]
    inner = wq_hbm.shape[1]
    part = width // CHUNKS
    firsts = [
        pltpu.make_async_copy(source, target, sems.at[i])
        for i, (source, target) in enumerate(
            ((anc_hbm, table), (len_hbm, lengths), (inv_hbm, inverse), (gain_hbm, gain))
        )
    ]
    for c in firsts:
        c.start()
    get_tok = pltpu.make_async_copy(tok_hbm, tok, sems.at[4])
    get_tok.start()
    copies = []
    for i in range(CHUNKS):
        at = pl.ds(i * part, part)
        copies.append(
            (
                pltpu.make_async_copy(wq_hbm.at[at], w.at[at, pl.ds(0, inner)], csems.at[0, i]),
                pltpu.make_async_copy(wk_hbm.at[at], w.at[at, pl.ds(inner, hd)], csems.at[1, i]),
                pltpu.make_async_copy(wv_hbm.at[at], w.at[at, pl.ds(inner + hd, hd)], csems.at[2, i]),
            )
        )

    def begin(i):
        if i < CHUNKS:
            for c in copies[i]:
                c.start()

    for i in range(AHEAD):
        begin(i)
    for c in firsts:
        c.wait()
    depth = jnp.sum(table[...], axis=1, keepdims=True).astype(F32) - 1.0
    places = jnp.concatenate(
        [
            depth[r * tree : (r + 1) * tree] + (PROMPT + lengths[r]).astype(F32)
            for r in range(requests)
        ],
        axis=0,
    )
    angles = places * inverse[...]
    lane = lax.broadcasted_iota(jnp.int32, angles.shape, 1)
    cosine = jnp.cos(angles)
    sine = jnp.sin(angles)
    sine = jnp.where(lane < hd // 2, -sine, sine)
    gains = gain[...].astype(F32)
    gains = jnp.concatenate([gains[i : i + 1] for i in range(gain.shape[0])], axis=1)
    get_tok.wait()
    begin(AHEAD)

    wide = tok[...].astype(F32)
    scale = lax.rsqrt(jnp.mean(wide * wide, axis=1, keepdims=True) + EPS)
    acc = None
    for i in range(CHUNKS):
        for c in copies[i]:
            c.wait()
        begin(AHEAD + 1 + i)
        at = slice(i * part, (i + 1) * part)
        normed = (tok[:, at].astype(F32) * scale * gains[:, at]).astype(BF16)
        d = dot(normed, w[at, :])
        acc = d if acc is None else acc + d
    heads = inner // hd
    fold = hd**-0.5 * math.log2(math.e)
    for g in range(heads):
        turned = rotate(acc[:, g * hd : (g + 1) * hd], cosine, sine)
        turned = (turned * fold).astype(BF16)
        for r in range(requests):
            q_ref[pl.ds((r * heads + g) * tree, tree), :] = turned[r * tree : (r + 1) * tree]
    k_ref[...] = rotate(acc[:, inner : inner + hd], cosine, sine).astype(BF16)
    v_ref[...] = acc[:, inner + hd :].astype(BF16)


def project_call(lengths, tokens, gain, w_query, w_key, w_value, ancestors, inverse):
    rows, width = tokens.shape
    hd = inverse.shape[1]
    inner = w_query.shape[1]
    return pl.pallas_call(
        project_kernel,
        in_specs=[HBM] * 8,
        out_specs=[VM, VM, VM],
        out_shape=[
            jax.ShapeDtypeStruct((rows * inner // hd, hd), BF16),
            jax.ShapeDtypeStruct((rows, hd), BF16),
            jax.ShapeDtypeStruct((rows, hd), BF16),
        ],
        scratch_shapes=[
            pltpu.SMEM(lengths.shape, jnp.int32),
            pltpu.VMEM((rows, width), BF16),
            pltpu.VMEM(gain.shape, BF16),
            pltpu.VMEM((width, inner + 2 * hd), BF16),
            pltpu.VMEM(ancestors.shape, jnp.int32),
            pltpu.VMEM(inverse.shape, F32),
            pltpu.SemaphoreType.DMA((5,)),
            pltpu.SemaphoreType.DMA((3, CHUNKS)),
        ],
        compiler_params=params(28),
        name="projections",
    )(lengths, tokens, gain, w_query, w_key, w_value, ancestors, inverse)


def join_kernel(a_hbm, b_hbm, out_ref, sems):
    n = a_hbm.shape[0]
    copies = [
        pltpu.make_async_copy(ref, out_ref.at[pl.ds(i * n, n)], sems.at[i])
        for i, ref in enumerate((a_hbm, b_hbm))
    ]
    for c in copies:
        c.start()
    for c in copies:
        c.wait()


def join_call(a, b):
    return pl.pallas_call(
        join_kernel,
        in_specs=[HBM, HBM],
        out_specs=VM,
        out_shape=jax.ShapeDtypeStruct((2 * a.shape[0],) + a.shape[1:], a.dtype),
        scratch_shapes=[pltpu.SemaphoreType.DMA((2,))],
        compiler_params=params(4),
        name="join",
    )(a, b)


def halves_kernel(right_hbm, left_hbm, k_ref, v_ref, sems):
    n = k_ref.shape[0]
    copies = (
        pltpu.make_async_copy(right_hbm.at[pl.ds(0, n)], k_ref, sems.at[0]),
        pltpu.make_async_copy(left_hbm.at[pl.ds(n, n)], v_ref, sems.at[1]),
    )
    for c in copies:
        c.start()
    for c in copies:
        c.wait()


def halves_call(right, left):
    half = jax.ShapeDtypeStruct((right.shape[0] // 2,) + right.shape[1:], right.dtype)
    return pl.pallas_call(
        halves_kernel,
        in_specs=[pl.BlockSpec(memory_space=pl.ANY)] * 2,
        out_specs=[VM, VM],
        out_shape=[half, half],
        scratch_shapes=[pltpu.SemaphoreType.DMA((2,))],
        compiler_params=params(4),
        name="halves",
    )(right, left)


def prompt_sum(q, g, pieces, ones):
    weights, values = [], []
    for kref, koff, vref, voff in pieces:
        weights.append(jnp.exp2(dot_nt(q, kref[koff + g])).astype(BF16))
        values.append(jnp.concatenate([vref[voff + g], ones], axis=1))
    return dot(jnp.concatenate(weights, axis=1), jnp.concatenate(values, axis=0))


def near_pieces(kv, kv_r, kv_l):
    n = kv.shape[0] // 2
    return [(kv, 0, kv, n), (kv_r, 0, kv_r, n), (kv_l, 0, kv_l, n)]


def source_of(at_ref, requests, shift, n_tok):
    return lax.rem(at_ref[0] + n_tok - shift, n_tok) * requests


def near_kernel(group_ref, at_ref, kv, kv_r, kv_l, *refs, requests, shifts, n_tok):
    hd = kv.shape[2]
    qrows = refs[0].shape[0] // requests
    pieces = near_pieces(kv, kv_r, kv_l)
    ones = jnp.ones((kv.shape[1], hd), BF16)
    for shift, q_ref, out_ref in zip(shifts, refs[: len(shifts)], refs[len(shifts) :]):
        base = source_of(at_ref, requests, shift, n_tok)
        for r in range(requests):
            at = pl.ds(r * qrows, qrows)
            out_ref[at, :] = prompt_sum(q_ref[at, :], group_ref[base + r], pieces, ones)


def near_call(groups, at, qs, kv, kv_r, kv_l, requests, shifts, n_tok):
    rows, hd = qs[0].shape
    n = len(shifts)
    return pl.pallas_call(
        lambda *refs: near_kernel(*refs, requests=requests, shifts=shifts, n_tok=n_tok),
        in_specs=[SMEM, SMEM] + [VM] * (3 + n),
        out_specs=[VM] * n,
        out_shape=[jax.ShapeDtypeStruct((rows, 2 * hd), F32)] * n,
        compiler_params=params(16),
        name="prompt_near",
    )(groups, at, kv, kv_r, kv_l, *qs)


def far_kernel(group_ref, at_ref, k_o, v_o, *refs, requests, shifts, n_tok):
    hd = k_o.shape[2]
    n = len(shifts)
    ones = jnp.ones((k_o.shape[1], hd), BF16)
    for shift, q_ref, near_ref, out_ref in zip(shifts, refs[:n], refs[n : 2 * n], refs[2 * n :]):
        qrows = q_ref.shape[0] // requests
        diagonal = lax.broadcasted_iota(jnp.int32, (qrows, hd), 0) == lax.broadcasted_iota(
            jnp.int32, (qrows, hd), 1
        )
        base = source_of(at_ref, requests, shift, n_tok)
        totals = []
        for r in range(requests):
            at = pl.ds(r * qrows, qrows)
            acc = near_ref[at, :] + prompt_sum(
                q_ref[at, :], group_ref[base + r], [(k_o, 0, v_o, 0)], ones
            )
            out_ref[at, :] = acc[:, :hd].astype(BF16)
            totals.append(jnp.sum(jnp.where(diagonal, acc[:, hd:], 0.0), axis=0, keepdims=True))
        total = jnp.concatenate(totals, axis=0)
        high = total.astype(BF16)
        low = (total - high.astype(F32)).astype(BF16)
        out_ref[pl.ds(requests * qrows, 2 * requests), :] = jnp.concatenate([high, low], axis=0)


def far_call(groups, at, nears, qs, k_o, v_o, requests, shifts, n_tok):
    rows, hd = qs[0].shape
    n = len(shifts)
    return pl.pallas_call(
        lambda *refs: far_kernel(*refs, requests=requests, shifts=shifts, n_tok=n_tok),
        in_specs=[SMEM, SMEM] + [VM] * (2 + 2 * n),
        out_specs=[VM] * n,
        out_shape=[jax.ShapeDtypeStruct((rows + 2 * requests, hd), BF16)] * n,
        compiler_params=params(16),
        name="prompt_far",
    )(groups, at, k_o, v_o, *qs, *nears)


def home_kernel(
    group_ref, at_ref, len_ref, q_ref, kv, kv_r, kv_l, k_o, v_o, new_k, new_v, anc_hbm, ck_hbm,
    cv_hbm, out_ref, anc_ref, keys, values, where_ref, sems, anc_sem,
):
    requests, slots, hd = keys.shape
    qrows = q_ref.shape[0] // requests
    piece = slots // PIECES

    def copies(r, i):
        at = pl.ds(i * piece, piece)
        return (
            pltpu.make_async_copy(ck_hbm.at[r, at], keys.at[r, at], sems.at[0, r, i]),
            pltpu.make_async_copy(cv_hbm.at[r, at], values.at[r, at], sems.at[1, r, i]),
        )

    def each_copy(act):
        for i in range(PIECES):
            for r in range(requests):
                if i == 0:
                    for c in copies(r, i):
                        act(c)
                else:

                    @pl.when(len_ref[r] > i * piece)
                    def _(r=r, i=i):
                        for c in copies(r, i):
                            act(c)

    get_anc = pltpu.make_async_copy(anc_hbm, anc_ref, anc_sem)
    get_anc.start()
    tree = anc_ref.shape[1]
    each_copy(lambda c: c.start())
    count = 0
    for r in range(requests):

        def note(b, n, r=r):
            where_ref[0, n] = r
            where_ref[1, n] = b * KB
            return n + 1

        count = lax.fori_loop(0, (len_ref[r] + KB - 1) // KB, note, count)
    for j in range(LANES):
        where_ref[0, count + j] = requests - 1
        where_ref[1, count + j] = 0
    pieces = near_pieces(kv, kv_r, kv_l) + [(k_o, 0, v_o, 0)]
    ones = jnp.ones((KB, hd), BF16)
    get_anc.wait()
    for r in range(requests):
        at = pl.ds(r * qrows, qrows)
        mine = pl.ds(r * tree, tree)
        q = q_ref[at, :]
        seen = jnp.concatenate([anc_ref[mine, :]] * (qrows // tree), axis=0)
        p = jnp.where(seen > 0, jnp.exp2(dot_nt(q, new_k[mine, :])), 0.0).astype(BF16)
        out_ref[at, :] = prompt_sum(
            q, group_ref[at_ref[0] * requests + r], pieces, ones
        ) + dot(p, jnp.concatenate([new_v[mine, :], ones[:tree]], axis=1))
    column = lax.broadcasted_iota(jnp.int32, (qrows, KB), 1)
    each_copy(lambda c: c.wait())

    def step(i, _):
        parts = []
        for j in range(LANES):
            n = i * LANES + j
            r = where_ref[0, n]
            first = pl.multiple_of(where_ref[1, n], KB)
            at = pl.ds(pl.multiple_of(r * qrows, qrows), qrows)
            limit = jnp.where(n < count, len_ref[r] - first, 0)
            s = dot_nt(q_ref[at, :], keys[r, pl.ds(first, KB), :])
            p = jnp.where(column < limit, jnp.exp2(s), 0.0).astype(BF16)
            both = jnp.concatenate([values[r, pl.ds(first, KB), :], ones], axis=1)
            parts.append((at, dot(p, both)))
        for at, d in parts:
            out_ref[at, :] += d
        return 0

    lax.fori_loop(0, (count + LANES - 1) // LANES, step, 0)


def home_call(groups, at, lengths, q, prompts, new_k, new_v, ancestors, cache_keys, cache_values):
    requests, slots, hd = cache_keys.shape
    return pl.pallas_call(
        home_kernel,
        in_specs=[SMEM, SMEM, SMEM] + [VM] * 8 + [HBM] * 3,
        out_specs=VM,
        out_shape=jax.ShapeDtypeStruct((q.shape[0], 2 * hd), F32),
        scratch_shapes=[
            pltpu.VMEM(ancestors.shape, jnp.int32),
            pltpu.VMEM(cache_keys.shape, BF16),
            pltpu.VMEM(cache_values.shape, BF16),
            pltpu.SMEM((2, requests * slots // KB + LANES), jnp.int32),
            pltpu.SemaphoreType.DMA((2, requests, PIECES)),
            pltpu.SemaphoreType.DMA,
        ],
        compiler_params=params(20),
        name="home_attention",
    )(groups, at, lengths, q, *prompts, new_k, new_v, ancestors, cache_keys, cache_values)


def merge_kernel(home_ref, a_ref, b_ref, c_ref, out_ref, *, requests):
    hd = a_ref.shape[1]
    qrows = home_ref.shape[0] // requests
    tree = out_ref.shape[0] // requests
    total = None
    for ref in (a_ref, b_ref, c_ref):
        both = ref[pl.ds(requests * qrows, 2 * requests), :].astype(F32)
        t = both[:requests] + both[requests:]
        total = t if total is None else total + t
    diagonal = lax.broadcasted_iota(jnp.int32, (qrows, hd), 0) == lax.broadcasted_iota(
        jnp.int32, (qrows, hd), 1
    )
    for r in range(requests):
        at = pl.ds(r * qrows, qrows)
        num = home_ref[at, pl.ds(0, hd)]
        for ref in (a_ref, b_ref, c_ref):
            num = num + ref[at, :].astype(F32)
        den = home_ref[at, pl.ds(hd, hd)] + jnp.sum(
            jnp.where(diagonal, jnp.broadcast_to(total[r : r + 1], (qrows, hd)), 0.0),
            axis=1,
            keepdims=True,
        )
        out = (num / den).astype(BF16)
        for g in range(qrows // tree):
            out_ref[pl.ds(r * tree, tree), pl.ds(g * hd, hd)] = out[g * tree : (g + 1) * tree]


def merge_call(home, a, b, c, requests, rows):
    hd = a.shape[1]
    return pl.pallas_call(
        lambda *refs: merge_kernel(*refs, requests=requests),
        in_specs=[VM] * 4,
        out_specs=VM,
        out_shape=jax.ShapeDtypeStruct((rows, home.shape[0] // rows * hd), BF16),
        compiler_params=params(8),
        name="merge",
    )(home, a, b, c)


def pick(acc_ref, x, tree):
    rows = []
    slot = lax.broadcasted_iota(jnp.int32, (tree, acc_ref.shape[1]), 0)
    for r in range(acc_ref.shape[0]):
        chosen = (slot == acc_ref[r : r + 1, :]).astype(F32).astype(BF16)
        rows.append(
            lax.dot_general(
                chosen, x[r * tree : (r + 1) * tree], (((0,), (0,)), ((), ())),
                preferred_element_type=F32,
            )
        )
    return rows


def columns_kernel(
    mdl_ref, acc_ref, w_hbm, tok_hbm, mine_ref, send_ref, tok_out, tok, rows_ref, sems, sem, put_sem
):
    count, _, cols = mine_ref.shape
    get = pltpu.make_async_copy(
        tok_hbm.at[:, pl.ds(pl.multiple_of(mdl_ref[0] * cols, 128), cols)], tok, sem
    )
    get.start()
    copies = []
    for i in range(count):
        there = lax.rem(mdl_ref[0] // 2 + i, count)
        for j, ref in enumerate((mine_ref, send_ref)):
            side = lax.rem(mdl_ref[0] + j, 2)
            start = pl.multiple_of((2 * there + side) * cols, 128)
            c = pltpu.make_async_copy(w_hbm.at[:, pl.ds(start, cols)], ref.at[i], sems.at[j, i])
            c.start()
            copies.append(c)
    get.wait()
    for r, row in enumerate(pick(acc_ref, tok[...], tok.shape[0] // acc_ref.shape[0])):
        rows_ref[r] = row
    put = pltpu.make_async_copy(rows_ref, tok_out, put_sem)
    put.start()
    for c in copies:
        c.wait()
    put.wait()


def columns_call(mdl, accepted, w_out, tokens, count):
    cols = w_out.shape[1] // (2 * count)
    return pl.pallas_call(
        columns_kernel,
        in_specs=[SMEM, VM, HBM, HBM],
        out_specs=[VM, VM, HBM],
        out_shape=[jax.ShapeDtypeStruct((count, w_out.shape[0], cols), BF16)] * 2
        + [pltpu.HBM(accepted.shape + (cols,), F32)],
        scratch_shapes=[
            pltpu.VMEM((tokens.shape[0], cols), BF16),
            pltpu.VMEM(accepted.shape + (cols,), F32),
            pltpu.SemaphoreType.DMA((2, count)),
            pltpu.SemaphoreType.DMA,
            pltpu.SemaphoreType.DMA,
        ],
        compiler_params=params(12),
        name="out_columns",
    )(mdl, accepted, w_out, tokens)


def first_kernel(mine_ref, w_ref, other_hbm, out_ref, other_ref, sem, *, shift):
    get = pltpu.make_async_copy(other_hbm.at[shift], other_ref, sem)
    get.start()
    out_ref[...] = dot(mine_ref[...], w_ref[0])
    get.wait()


def out_first(mine, w_mine, w_other, shift):
    rows, inner = mine.shape
    cols = w_mine.shape[2]
    flat = lambda i: (0, 0)
    return pl.pallas_call(
        lambda *refs: first_kernel(*refs, shift=shift),
        grid=(1,),
        in_specs=[
            pl.BlockSpec((rows, inner), flat),
            pl.BlockSpec((1, inner, cols), lambda i: (shift, 0, 0)),
            HBM,
        ],
        out_specs=[pl.BlockSpec((rows, cols), flat), pl.BlockSpec((inner, cols), flat)],
        out_shape=[
            jax.ShapeDtypeStruct((rows, cols), F32),
            jax.ShapeDtypeStruct((inner, cols), BF16),
        ],
        scratch_shapes=[pltpu.SemaphoreType.DMA],
        compiler_params=params(12),
        name="out_first",
    )(mine, w_mine, w_other)


def second_kernel(first_ref, other_ref, w_ref, out_ref):
    out_ref[...] = (first_ref[...] + dot(other_ref[...], w_ref[...])).astype(BF16)


def out_second(first, other, w):
    return pl.pallas_call(
        second_kernel,
        in_specs=[VM] * 3,
        out_specs=VM,
        out_shape=jax.ShapeDtypeStruct(first.shape, BF16),
        compiler_params=params(12),
        name="out_second",
    )(first, other, w)


def out_kernel(mine_ref, other_ref, *refs):
    n = len(refs) // 3
    for wa, wb, out in zip(refs[:n], refs[n : 2 * n], refs[2 * n :]):
        out[...] = (dot(mine_ref[...], wa[0]) + dot(other_ref[...], wb[0])).astype(out.dtype)


def out_call(mine, other, w_mine, w_other, shifts, dtype):
    rows, inner = mine.shape
    cols = w_other.shape[2]
    whole = pl.BlockSpec((rows, inner), lambda i: (0, 0))
    chunks = [pl.BlockSpec((1, inner, cols), lambda i, n=n: (n, 0, 0)) for n in shifts]
    return pl.pallas_call(
        out_kernel,
        grid=(1,),
        in_specs=[whole, whole] + chunks * 2,
        out_specs=[pl.BlockSpec((rows, cols), lambda i: (0, 0))] * len(shifts),
        out_shape=[jax.ShapeDtypeStruct((rows, cols), dtype)] * len(shifts),
        compiler_params=params(16),
        name="out_proj",
    )(mine, other, *([w_mine] * len(shifts)), *([w_other] * len(shifts)))


def last_kernel(acc_ref, own_ref, a_ref, b_ref, c_ref, tok_ref, out_ref, rows_ref):
    total = own_ref[...] + a_ref[...].astype(F32) + b_ref[...].astype(F32) + c_ref[...].astype(F32)
    rounded = total.astype(BF16)
    out_ref[...] = rounded
    for r, row in enumerate(pick(acc_ref, rounded, own_ref.shape[0] // acc_ref.shape[0])):
        rows_ref[r] = (tok_ref[r] + row).astype(BF16)


def last_call(accepted, own, a, b, c, picked):
    rows, cols = own.shape
    return pl.pallas_call(
        last_kernel,
        in_specs=[VM] * 6,
        out_specs=[VM, VM],
        out_shape=[
            jax.ShapeDtypeStruct((rows, cols), BF16),
            jax.ShapeDtypeStruct(picked.shape, BF16),
        ],
        compiler_params=params(8),
        name="last_sums",
    )(accepted, own, a, b, c, picked)


def shards(
    tokens, norm_gain, w_query, w_key, w_value, w_out, prompt_keys, prompt_values, cache_keys,
    cache_values, cache_length, request_group, ancestors, accepted,
):
    requests, tree = ancestors.shape[:2]
    rows = tokens.shape[0]
    hd = prompt_keys.shape[3]
    n_tok = lax.axis_size("tok")
    n_mdl = lax.axis_size("mdl")
    n_y = 4
    n_z = n_tok // n_y
    n_x = n_mdl // 2
    tok = lax.axis_index("tok")
    mdl = lax.axis_index("mdl")

    def along_y(v, n):
        perm = [(t, t // n_y * n_y + (t + n) % n_y) for t in range(n_tok)]
        return lax.ppermute(v, "tok", perm)

    def along_z(v, n):
        return lax.ppermute(v, "tok", [(t, (t + n * n_y) % n_tok) for t in range(n_tok)])

    def along_x(v, n):
        return lax.ppermute(v, "mdl", [(m, (m + 2 * n) % n_mdl) for m in range(n_mdl)])

    def other_core(v):
        return lax.ppermute(v, "mdl", [(m, m ^ 1) for m in range(n_mdl)])

    def in_hbm(v):
        return pltpu.with_memory_space_constraint(v, pltpu.HBM)

    tok_at = jnp.reshape(tok, (1,)).astype(jnp.int32)
    mdl_at = jnp.reshape(mdl, (1,)).astype(jnp.int32)

    squeeze = lambda v: v.reshape(v.shape[0], v.shape[1], v.shape[3])
    kv = join_call(in_hbm(squeeze(prompt_keys)), in_hbm(squeeze(prompt_values)))
    kv_r = along_y(kv, 1)
    kv_l = along_y(kv, -1)

    exponent = np.arange(hd // 2, dtype=np.float64) * (2.0 / hd)
    inverse = jnp.asarray(np.tile(THETA**-exponent, 2)[None, :], dtype=F32)
    table = ancestors.reshape(rows, tree)
    q, new_k, new_v = project_call(
        *map(
            in_hbm,
            (
                cache_length, tokens, norm_gain.reshape(-1, hd), w_query, w_key, w_value, table,
                inverse,
            ),
        )
    )
    shifts = (2, 1, -1)
    q_far = [along_z(q, n) for n in shifts]

    w_mine, w_send, picked = columns_call(mdl_at, accepted, in_hbm(w_out), in_hbm(tokens), n_x)
    w_other = other_core(w_send)

    k_half, v_half = halves_call(kv_r, kv_l)
    k_o = along_y(k_half, 1)
    v_o = along_y(v_half, -1)
    prompts = (kv, kv_r, kv_l, k_o, v_o)

    turns = [n % n_z * n_y for n in shifts]
    nears = near_call(
        request_group, tok_at, q_far, kv, in_hbm(kv_r), in_hbm(kv_l), requests, turns, n_tok
    )
    parts = []
    for some in (slice(0, 1), slice(1, 3)):
        parts += far_call(
            request_group, tok_at, nears[some], q_far[some], k_o, v_o, requests, turns[some],
            n_tok,
        )
    back = [along_z(part, -n) for n, part in zip(shifts, parts)]
    home = home_call(
        request_group, tok_at, cache_length, q, prompts, new_k, new_v, in_hbm(table),
        in_hbm(squeeze(cache_keys)), in_hbm(squeeze(cache_values)),
    )
    attended = merge_call(home, *back, requests, rows)

    attended_other = other_core(attended)
    first, w_second = out_first(attended, w_mine, in_hbm(w_other), 2)
    far = along_x(out_second(first, attended_other, w_second), 2)
    up, down = out_call(attended, attended_other, w_mine, w_other, (1, n_x - 1), BF16)
    up = along_x(up, 1)
    down = along_x(down, -1)
    (own_sum,) = out_call(attended, attended_other, w_mine, w_other, (0,), F32)
    return tuple(last_call(accepted, own_sum, far, up, down, picked))


def solution(mesh):
    placed = (
        P("tok", None),
        P(),
        P(None, "mdl"),
        P(None, "mdl"),
        P(None, "mdl"),
        P("mdl", None),
        P(None, "tok", "mdl", None),
        P(None, "tok", "mdl", None),
        P("tok", None, "mdl", None),
        P("tok", None, "mdl", None),
        P("tok"),
        P(),
        P("tok", None, None),
        P("tok", None),
    )

    return jax.shard_map(
        shards,
        mesh=mesh,
        in_specs=placed,
        out_specs=(P("tok", "mdl"), P("tok", None, "mdl")),
        check_vma=False,
    )
```

```python
import math

import jax
import jax.numpy as jnp
import numpy as np
from jax import lax
from jax.experimental import pallas as pl
from jax.experimental.pallas import tpu as pltpu
from jax.sharding import PartitionSpec as P


PROMPT = 4096
THETA = 100000000.0
EPS = 1e-05

F32 = jnp.float32
BF16 = jnp.bfloat16

HBM = pl.BlockSpec(memory_space=pltpu.HBM)
SMEM = pl.BlockSpec(memory_space=pltpu.SMEM)
VM = pl.BlockSpec(memory_space=pltpu.VMEM)
CHUNKS = 4
AHEAD = 1
KB = 256
PIECES = 2
LANES = 8
NT = (((1,), (1,)), ((), ()))


def params(mib):
    return pltpu.CompilerParams(vmem_limit_bytes=mib * 1024 * 1024)


def dot(a, b):
    return jnp.dot(a, b, preferred_element_type=F32)


def dot_nt(a, b):
    return lax.dot_general(a, b, NT, preferred_element_type=F32)


def rotate(x, cosine, sine):
    return x * cosine + pltpu.roll(x, x.shape[1] // 2, 1) * sine


def project_kernel(
    len_hbm, tok_hbm, gain_hbm, wq_hbm, wk_hbm, wv_hbm, anc_hbm, inv_hbm, q_ref, k_ref, v_ref,
    lengths, tok, gain, w, table, inverse, sems, csems,
):
    rows, width = tok.shape
    requests = lengths.shape[0]
    tree = rows // requests
    hd = inverse.shape[1]
    inner = wq_hbm.shape[1]
    part = width // CHUNKS
    firsts = [
        pltpu.make_async_copy(source, target, sems.at[i])
        for i, (source, target) in enumerate(
            ((anc_hbm, table), (len_hbm, lengths), (inv_hbm, inverse), (gain_hbm, gain))
        )
    ]
    for c in firsts:
        c.start()
    get_tok = pltpu.make_async_copy(tok_hbm, tok, sems.at[4])
    get_tok.start()
    copies = []
    for i in range(CHUNKS):
        at = pl.ds(i * part, part)
        copies.append(
            (
                pltpu.make_async_copy(wq_hbm.at[at], w.at[at, pl.ds(0, inner)], csems.at[0, i]),
                pltpu.make_async_copy(wk_hbm.at[at], w.at[at, pl.ds(inner, hd)], csems.at[1, i]),
                pltpu.make_async_copy(wv_hbm.at[at], w.at[at, pl.ds(inner + hd, hd)], csems.at[2, i]),
            )
        )

    def begin(i):
        if i < CHUNKS:
            for c in copies[i]:
                c.start()

    for i in range(AHEAD):
        begin(i)
    for c in firsts:
        c.wait()
    depth = jnp.sum(table[...], axis=1, keepdims=True).astype(F32) - 1.0
    places = jnp.concatenate(
        [
            depth[r * tree : (r + 1) * tree] + (PROMPT + lengths[r]).astype(F32)
            for r in range(requests)
        ],
        axis=0,
    )
    angles = places * inverse[...]
    lane = lax.broadcasted_iota(jnp.int32, angles.shape, 1)
    cosine = jnp.cos(angles)
    sine = jnp.sin(angles)
    sine = jnp.where(lane < hd // 2, -sine, sine)
    gains = gain[...].astype(F32)
    gains = jnp.concatenate([gains[i : i + 1] for i in range(gain.shape[0])], axis=1)
    get_tok.wait()
    begin(AHEAD)

    wide = tok[...].astype(F32)
    scale = lax.rsqrt(jnp.mean(wide * wide, axis=1, keepdims=True) + EPS)
    acc = None
    for i in range(CHUNKS):
        for c in copies[i]:
            c.wait()
        begin(AHEAD + 1 + i)
        at = slice(i * part, (i + 1) * part)
        normed = (tok[:, at].astype(F32) * scale * gains[:, at]).astype(BF16)
        d = dot(normed, w[at, :])
        acc = d if acc is None else acc + d
    heads = inner // hd
    fold = hd**-0.5 * math.log2(math.e)
    for g in range(heads):
        turned = rotate(acc[:, g * hd : (g + 1) * hd], cosine, sine)
        turned = (turned * fold).astype(BF16)
        for r in range(requests):
            q_ref[pl.ds((r * heads + g) * tree, tree), :] = turned[r * tree : (r + 1) * tree]
    k_ref[...] = rotate(acc[:, inner : inner + hd], cosine, sine).astype(BF16)
    v_ref[...] = acc[:, inner + hd :].astype(BF16)


def project_call(lengths, tokens, gain, w_query, w_key, w_value, ancestors, inverse):
    rows, width = tokens.shape
    hd = inverse.shape[1]
    inner = w_query.shape[1]
    return pl.pallas_call(
        project_kernel,
        in_specs=[HBM] * 8,
        out_specs=[VM, VM, VM],
        out_shape=[
            jax.ShapeDtypeStruct((rows * inner // hd, hd), BF16),
            jax.ShapeDtypeStruct((rows, hd), BF16),
            jax.ShapeDtypeStruct((rows, hd), BF16),
        ],
        scratch_shapes=[
            pltpu.SMEM(lengths.shape, jnp.int32),
            pltpu.VMEM((rows, width), BF16),
            pltpu.VMEM(gain.shape, BF16),
            pltpu.VMEM((width, inner + 2 * hd), BF16),
            pltpu.VMEM(ancestors.shape, jnp.int32),
            pltpu.VMEM(inverse.shape, F32),
            pltpu.SemaphoreType.DMA((5,)),
            pltpu.SemaphoreType.DMA((3, CHUNKS)),
        ],
        compiler_params=params(28),
        name="projections",
    )(lengths, tokens, gain, w_query, w_key, w_value, ancestors, inverse)


def prompt_sum(q, g, pieces, ones):
    weights, values = [], []
    for keys, vals in pieces:
        weights.append(jnp.exp2(dot_nt(q, keys[g])).astype(BF16))
        values.append(jnp.concatenate([vals[g], ones], axis=1))
    return dot(jnp.concatenate(weights, axis=1), jnp.concatenate(values, axis=0))


def source_of(at_ref, requests, shift, n_tok):
    return lax.rem(at_ref[0] + n_tok - shift, n_tok) * requests


def near_kernel(group_ref, at_ref, k, k_r, k_l, v, v_r, v_l, *refs, requests, shifts, n_tok):
    hd = k.shape[2]
    qrows = refs[0].shape[0] // requests
    pieces = [(k, v), (k_r, v_r), (k_l, v_l)]
    ones = jnp.ones((k.shape[1], hd), BF16)
    for shift, q_ref, out_ref in zip(shifts, refs[: len(shifts)], refs[len(shifts) :]):
        base = source_of(at_ref, requests, shift, n_tok)
        for r in range(requests):
            at = pl.ds(r * qrows, qrows)
            out_ref[at, :] = prompt_sum(q_ref[at, :], group_ref[base + r], pieces, ones)


def near_call(groups, at, qs, prompts, requests, shifts, n_tok):
    rows, hd = qs[0].shape
    n = len(shifts)
    return pl.pallas_call(
        lambda *refs: near_kernel(*refs, requests=requests, shifts=shifts, n_tok=n_tok),
        in_specs=[SMEM, SMEM] + [VM] * (6 + n),
        out_specs=[VM] * n,
        out_shape=[jax.ShapeDtypeStruct((rows, 2 * hd), F32)] * n,
        compiler_params=params(16),
        name="prompt_near",
    )(groups, at, *prompts, *qs)


def far_kernel(group_ref, at_ref, k_o, v_o, *refs, requests, shifts, n_tok):
    hd = k_o.shape[2]
    n = len(shifts)
    ones = jnp.ones((k_o.shape[1], hd), BF16)
    for shift, q_ref, near_ref, out_ref in zip(shifts, refs[:n], refs[n : 2 * n], refs[2 * n :]):
        qrows = q_ref.shape[0] // requests
        diagonal = lax.broadcasted_iota(jnp.int32, (qrows, hd), 0) == lax.broadcasted_iota(
            jnp.int32, (qrows, hd), 1
        )
        base = source_of(at_ref, requests, shift, n_tok)
        totals = []
        for r in range(requests):
            at = pl.ds(r * qrows, qrows)
            acc = near_ref[at, :] + prompt_sum(
                q_ref[at, :], group_ref[base + r], [(k_o, v_o)], ones
            )
            out_ref[at, :] = acc[:, :hd].astype(BF16)
            totals.append(jnp.sum(jnp.where(diagonal, acc[:, hd:], 0.0), axis=0, keepdims=True))
        total = jnp.concatenate(totals, axis=0)
        high = total.astype(BF16)
        low = (total - high.astype(F32)).astype(BF16)
        out_ref[pl.ds(requests * qrows, 2 * requests), :] = jnp.concatenate([high, low], axis=0)


def far_call(groups, at, nears, qs, k_o, v_o, requests, shifts, n_tok):
    rows, hd = qs[0].shape
    n = len(shifts)
    return pl.pallas_call(
        lambda *refs: far_kernel(*refs, requests=requests, shifts=shifts, n_tok=n_tok),
        in_specs=[SMEM, SMEM] + [VM] * (2 + 2 * n),
        out_specs=[VM] * n,
        out_shape=[jax.ShapeDtypeStruct((rows + 2 * requests, hd), BF16)] * n,
        compiler_params=params(16),
        name="prompt_far",
    )(groups, at, k_o, v_o, *qs, *nears)


def home_kernel(
    group_ref, at_ref, len_ref, q_ref, k, k_r, k_l, v, v_r, v_l, k_o, v_o, new_k, new_v, anc_hbm,
    ck_hbm, cv_hbm, out_ref, anc_ref, keys, values, where_ref, sems, anc_sem,
):
    requests, slots, hd = keys.shape
    qrows = q_ref.shape[0] // requests
    piece = slots // PIECES

    def copies(r, i):
        at = pl.ds(i * piece, piece)
        return (
            pltpu.make_async_copy(ck_hbm.at[r, at], keys.at[r, at], sems.at[0, r, i]),
            pltpu.make_async_copy(cv_hbm.at[r, at], values.at[r, at], sems.at[1, r, i]),
        )

    def each_copy(act):
        for i in range(PIECES):
            for r in range(requests):
                if i == 0:
                    for c in copies(r, i):
                        act(c)
                else:

                    @pl.when(len_ref[r] > i * piece)
                    def _(r=r, i=i):
                        for c in copies(r, i):
                            act(c)

    get_anc = pltpu.make_async_copy(anc_hbm, anc_ref, anc_sem)
    get_anc.start()
    tree = anc_ref.shape[1]
    each_copy(lambda c: c.start())
    count = 0
    for r in range(requests):

        def note(b, n, r=r):
            where_ref[0, n] = r
            where_ref[1, n] = b * KB
            return n + 1

        count = lax.fori_loop(0, (len_ref[r] + KB - 1) // KB, note, count)
    for j in range(LANES):
        where_ref[0, count + j] = requests - 1
        where_ref[1, count + j] = 0
    pieces = [(k, v), (k_r, v_r), (k_l, v_l), (k_o, v_o)]
    ones = jnp.ones((KB, hd), BF16)
    get_anc.wait()
    for r in range(requests):
        at = pl.ds(r * qrows, qrows)
        mine = pl.ds(r * tree, tree)
        q = q_ref[at, :]
        seen = jnp.concatenate([anc_ref[mine, :]] * (qrows // tree), axis=0)
        p = jnp.where(seen > 0, jnp.exp2(dot_nt(q, new_k[mine, :])), 0.0).astype(BF16)
        out_ref[at, :] = prompt_sum(
            q, group_ref[at_ref[0] * requests + r], pieces, ones
        ) + dot(p, jnp.concatenate([new_v[mine, :], ones[:tree]], axis=1))
    column = lax.broadcasted_iota(jnp.int32, (qrows, KB), 1)
    each_copy(lambda c: c.wait())

    def step(i, _):
        parts = []
        for j in range(LANES):
            n = i * LANES + j
            r = where_ref[0, n]
            first = pl.multiple_of(where_ref[1, n], KB)
            at = pl.ds(pl.multiple_of(r * qrows, qrows), qrows)
            limit = jnp.where(n < count, len_ref[r] - first, 0)
            s = dot_nt(q_ref[at, :], keys[r, pl.ds(first, KB), :])
            p = jnp.where(column < limit, jnp.exp2(s), 0.0).astype(BF16)
            both = jnp.concatenate([values[r, pl.ds(first, KB), :], ones], axis=1)
            parts.append((at, dot(p, both)))
        for at, d in parts:
            out_ref[at, :] += d
        return 0

    lax.fori_loop(0, (count + LANES - 1) // LANES, step, 0)


def home_call(groups, at, lengths, q, prompts, new_k, new_v, ancestors, cache_keys, cache_values):
    requests, slots, hd = cache_keys.shape
    return pl.pallas_call(
        home_kernel,
        in_specs=[SMEM, SMEM, SMEM] + [VM] * 11 + [HBM] * 3,
        out_specs=VM,
        out_shape=jax.ShapeDtypeStruct((q.shape[0], 2 * hd), F32),
        scratch_shapes=[
            pltpu.VMEM(ancestors.shape, jnp.int32),
            pltpu.VMEM(cache_keys.shape, BF16),
            pltpu.VMEM(cache_values.shape, BF16),
            pltpu.SMEM((2, requests * slots // KB + LANES), jnp.int32),
            pltpu.SemaphoreType.DMA((2, requests, PIECES)),
            pltpu.SemaphoreType.DMA,
        ],
        compiler_params=params(20),
        name="home_attention",
    )(groups, at, lengths, q, *prompts, new_k, new_v, ancestors, cache_keys, cache_values)


def merge_kernel(home_ref, a_ref, b_ref, c_ref, out_ref, *, requests):
    hd = a_ref.shape[1]
    qrows = home_ref.shape[0] // requests
    tree = out_ref.shape[0] // requests
    total = None
    for ref in (a_ref, b_ref, c_ref):
        both = ref[pl.ds(requests * qrows, 2 * requests), :].astype(F32)
        t = both[:requests] + both[requests:]
        total = t if total is None else total + t
    diagonal = lax.broadcasted_iota(jnp.int32, (qrows, hd), 0) == lax.broadcasted_iota(
        jnp.int32, (qrows, hd), 1
    )
    for r in range(requests):
        at = pl.ds(r * qrows, qrows)
        num = home_ref[at, pl.ds(0, hd)]
        for ref in (a_ref, b_ref, c_ref):
            num = num + ref[at, :].astype(F32)
        den = home_ref[at, pl.ds(hd, hd)] + jnp.sum(
            jnp.where(diagonal, jnp.broadcast_to(total[r : r + 1], (qrows, hd)), 0.0),
            axis=1,
            keepdims=True,
        )
        out = (num / den).astype(BF16)
        for g in range(qrows // tree):
            out_ref[pl.ds(r * tree, tree), pl.ds(g * hd, hd)] = out[g * tree : (g + 1) * tree]


def merge_call(home, a, b, c, requests, rows):
    hd = a.shape[1]
    return pl.pallas_call(
        lambda *refs: merge_kernel(*refs, requests=requests),
        in_specs=[VM] * 4,
        out_specs=VM,
        out_shape=jax.ShapeDtypeStruct((rows, home.shape[0] // rows * hd), BF16),
        compiler_params=params(8),
        name="merge",
    )(home, a, b, c)


def pick(acc_ref, x, tree):
    rows = []
    slot = lax.broadcasted_iota(jnp.int32, (tree, acc_ref.shape[1]), 0)
    for r in range(acc_ref.shape[0]):
        chosen = (slot == acc_ref[r : r + 1, :]).astype(F32).astype(BF16)
        rows.append(
            lax.dot_general(
                chosen, x[r * tree : (r + 1) * tree], (((0,), (0,)), ((), ())),
                preferred_element_type=F32,
            )
        )
    return rows


def columns_kernel(
    mdl_ref, acc_ref, w_hbm, tok_hbm, mine_ref, send_ref, tok_out, tok, rows_ref, sems, sem, put_sem
):
    count, _, cols = mine_ref.shape
    get = pltpu.make_async_copy(
        tok_hbm.at[:, pl.ds(pl.multiple_of(mdl_ref[0] * cols, 128), cols)], tok, sem
    )
    get.start()
    copies = []
    for i in range(count):
        there = lax.rem(mdl_ref[0] // 2 + i, count)
        for j, ref in enumerate((mine_ref, send_ref)):
            side = lax.rem(mdl_ref[0] + j, 2)
            start = pl.multiple_of((2 * there + side) * cols, 128)
            c = pltpu.make_async_copy(w_hbm.at[:, pl.ds(start, cols)], ref.at[i], sems.at[j, i])
            c.start()
            copies.append(c)
    get.wait()
    for r, row in enumerate(pick(acc_ref, tok[...], tok.shape[0] // acc_ref.shape[0])):
        rows_ref[r] = row
    put = pltpu.make_async_copy(rows_ref, tok_out, put_sem)
    put.start()
    for c in copies:
        c.wait()
    put.wait()


def columns_call(mdl, accepted, w_out, tokens, count):
    cols = w_out.shape[1] // (2 * count)
    return pl.pallas_call(
        columns_kernel,
        in_specs=[SMEM, VM, HBM, HBM],
        out_specs=[VM, VM, HBM],
        out_shape=[jax.ShapeDtypeStruct((count, w_out.shape[0], cols), BF16)] * 2
        + [pltpu.HBM(accepted.shape + (cols,), F32)],
        scratch_shapes=[
            pltpu.VMEM((tokens.shape[0], cols), BF16),
            pltpu.VMEM(accepted.shape + (cols,), F32),
            pltpu.SemaphoreType.DMA((2, count)),
            pltpu.SemaphoreType.DMA,
            pltpu.SemaphoreType.DMA,
        ],
        compiler_params=params(12),
        name="out_columns",
    )(mdl, accepted, w_out, tokens)


def first_kernel(mine_ref, w_ref, other_hbm, out_ref, other_ref, sem, *, shift):
    get = pltpu.make_async_copy(other_hbm.at[shift], other_ref, sem)
    get.start()
    out_ref[...] = dot(mine_ref[...], w_ref[0])
    get.wait()


def out_first(mine, w_mine, w_other, shift):
    rows, inner = mine.shape
    cols = w_mine.shape[2]
    flat = lambda i: (0, 0)
    return pl.pallas_call(
        lambda *refs: first_kernel(*refs, shift=shift),
        grid=(1,),
        in_specs=[
            pl.BlockSpec((rows, inner), flat),
            pl.BlockSpec((1, inner, cols), lambda i: (shift, 0, 0)),
            HBM,
        ],
        out_specs=[pl.BlockSpec((rows, cols), flat), pl.BlockSpec((inner, cols), flat)],
        out_shape=[
            jax.ShapeDtypeStruct((rows, cols), F32),
            jax.ShapeDtypeStruct((inner, cols), BF16),
        ],
        scratch_shapes=[pltpu.SemaphoreType.DMA],
        compiler_params=params(12),
        name="out_first",
    )(mine, w_mine, w_other)


def second_kernel(first_ref, other_ref, w_ref, out_ref):
    out_ref[...] = (first_ref[...] + dot(other_ref[...], w_ref[...])).astype(BF16)


def out_second(first, other, w):
    return pl.pallas_call(
        second_kernel,
        in_specs=[VM] * 3,
        out_specs=VM,
        out_shape=jax.ShapeDtypeStruct(first.shape, BF16),
        compiler_params=params(12),
        name="out_second",
    )(first, other, w)


def out_kernel(mine_ref, other_ref, *refs):
    n = len(refs) // 3
    for wa, wb, out in zip(refs[:n], refs[n : 2 * n], refs[2 * n :]):
        out[...] = (dot(mine_ref[...], wa[0]) + dot(other_ref[...], wb[0])).astype(out.dtype)


def out_call(mine, other, w_mine, w_other, shifts, dtype):
    rows, inner = mine.shape
    cols = w_other.shape[2]
    whole = pl.BlockSpec((rows, inner), lambda i: (0, 0))
    chunks = [pl.BlockSpec((1, inner, cols), lambda i, n=n: (n, 0, 0)) for n in shifts]
    return pl.pallas_call(
        out_kernel,
        grid=(1,),
        in_specs=[whole, whole] + chunks * 2,
        out_specs=[pl.BlockSpec((rows, cols), lambda i: (0, 0))] * len(shifts),
        out_shape=[jax.ShapeDtypeStruct((rows, cols), dtype)] * len(shifts),
        compiler_params=params(16),
        name="out_proj",
    )(mine, other, *([w_mine] * len(shifts)), *([w_other] * len(shifts)))


def last_kernel(acc_ref, own_ref, a_ref, b_ref, c_ref, tok_ref, out_ref, rows_ref):
    total = own_ref[...] + a_ref[...].astype(F32) + b_ref[...].astype(F32) + c_ref[...].astype(F32)
    rounded = total.astype(BF16)
    out_ref[...] = rounded
    for r, row in enumerate(pick(acc_ref, rounded, own_ref.shape[0] // acc_ref.shape[0])):
        rows_ref[r] = (tok_ref[r] + row).astype(BF16)


def last_call(accepted, own, a, b, c, picked):
    rows, cols = own.shape
    return pl.pallas_call(
        last_kernel,
        in_specs=[VM] * 6,
        out_specs=[VM, VM],
        out_shape=[
            jax.ShapeDtypeStruct((rows, cols), BF16),
            jax.ShapeDtypeStruct(picked.shape, BF16),
        ],
        compiler_params=params(8),
        name="last_sums",
    )(accepted, own, a, b, c, picked)


def shards(
    tokens, norm_gain, w_query, w_key, w_value, w_out, prompt_keys, prompt_values, cache_keys,
    cache_values, cache_length, request_group, ancestors, accepted,
):
    requests, tree = ancestors.shape[:2]
    rows = tokens.shape[0]
    hd = prompt_keys.shape[3]
    n_tok = lax.axis_size("tok")
    n_mdl = lax.axis_size("mdl")
    n_y = 4
    n_z = n_tok // n_y
    n_x = n_mdl // 2
    tok = lax.axis_index("tok")
    mdl = lax.axis_index("mdl")

    def along_y(v, n):
        perm = [(t, t // n_y * n_y + (t + n) % n_y) for t in range(n_tok)]
        return lax.ppermute(v, "tok", perm)

    def along_z(v, n):
        return lax.ppermute(v, "tok", [(t, (t + n * n_y) % n_tok) for t in range(n_tok)])

    def along_x(v, n):
        return lax.ppermute(v, "mdl", [(m, (m + 2 * n) % n_mdl) for m in range(n_mdl)])

    def other_core(v):
        return lax.ppermute(v, "mdl", [(m, m ^ 1) for m in range(n_mdl)])

    def in_hbm(v):
        return pltpu.with_memory_space_constraint(v, pltpu.HBM)

    tok_at = jnp.reshape(tok, (1,)).astype(jnp.int32)
    mdl_at = jnp.reshape(mdl, (1,)).astype(jnp.int32)

    squeeze = lambda v: v.reshape(v.shape[0], v.shape[1], v.shape[3])
    k, v = squeeze(prompt_keys), squeeze(prompt_values)
    k_r, k_l = along_y(k, 1), along_y(k, -1)
    v_r, v_l = along_y(v, 1), along_y(v, -1)

    exponent = np.arange(hd // 2, dtype=np.float64) * (2.0 / hd)
    inverse = jnp.asarray(np.tile(THETA**-exponent, 2)[None, :], dtype=F32)
    table = ancestors.reshape(rows, tree)
    q, new_k, new_v = project_call(
        *map(
            in_hbm,
            (
                cache_length, tokens, norm_gain.reshape(-1, hd), w_query, w_key, w_value, table,
                inverse,
            ),
        )
    )
    shifts = (2, 1, -1)
    q_far = [along_z(q, n) for n in shifts]

    w_mine, w_send, picked = columns_call(mdl_at, accepted, in_hbm(w_out), in_hbm(tokens), n_x)
    w_other = other_core(w_send)

    k_o = along_y(k_r, 1)
    v_o = along_y(v_l, -1)
    near = tuple(map(in_hbm, (k, k_r, k_l, v, v_r, v_l)))

    turns = [n % n_z * n_y for n in shifts]
    nears, parts = [], []
    two = (slice(0, 1), slice(1, 3))
    for some in two:
        nears.append(
            near_call(request_group, tok_at, q_far[some], near, requests, turns[some], n_tok)
        )
    for i, some in enumerate(two):
        parts += far_call(
            request_group, tok_at, nears[i], q_far[some], k_o, v_o, requests, turns[some], n_tok
        )
    back = [along_z(part, -n) for n, part in zip(shifts, parts)]
    home = home_call(
        request_group, tok_at, cache_length, q, (k, k_r, k_l, v, v_r, v_l, k_o, v_o), new_k, new_v, in_hbm(table),
        in_hbm(squeeze(cache_keys)), in_hbm(squeeze(cache_values)),
    )
    attended = merge_call(home, *back, requests, rows)

    attended_other = other_core(attended)
    first, w_second = out_first(attended, w_mine, in_hbm(w_other), 2)
    far = along_x(out_second(first, attended_other, w_second), 2)
    up, down = out_call(attended, attended_other, w_mine, w_other, (1, n_x - 1), BF16)
    up = along_x(up, 1)
    down = along_x(down, -1)
    (own_sum,) = out_call(attended, attended_other, w_mine, w_other, (0,), F32)
    return tuple(last_call(accepted, own_sum, far, up, down, picked))


def solution(mesh):
    placed = (
        P("tok", None),
        P(),
        P(None, "mdl"),
        P(None, "mdl"),
        P(None, "mdl"),
        P("mdl", None),
        P(None, "tok", "mdl", None),
        P(None, "tok", "mdl", None),
        P("tok", None, "mdl", None),
        P("tok", None, "mdl", None),
        P("tok"),
        P(),
        P("tok", None, None),
        P("tok", None),
    )

    return jax.shard_map(
        shards,
        mesh=mesh,
        in_specs=placed,
        out_specs=(P("tok", "mdl"), P("tok", None, "mdl")),
        check_vma=False,
    )
```

```python
import math

import jax
import jax.numpy as jnp
import numpy as np
from jax import lax
from jax.experimental import pallas as pl
from jax.experimental.pallas import tpu as pltpu
from jax.sharding import PartitionSpec as P


PROMPT = 4096
THETA = 100000000.0
EPS = 1e-05

F32 = jnp.float32
BF16 = jnp.bfloat16

HBM = pl.BlockSpec(memory_space=pltpu.HBM)
SMEM = pl.BlockSpec(memory_space=pltpu.SMEM)
VM = pl.BlockSpec(memory_space=pltpu.VMEM)
CHUNKS = 4
AHEAD = 1
KB = 256
PIECES = 2
LANES = 8
NT = (((1,), (1,)), ((), ()))


def params(mib):
    return pltpu.CompilerParams(vmem_limit_bytes=mib * 1024 * 1024)


def dot(a, b):
    return jnp.dot(a, b, preferred_element_type=F32)


def dot_nt(a, b):
    return lax.dot_general(a, b, NT, preferred_element_type=F32)


def rotate(x, cosine, sine):
    return x * cosine + pltpu.roll(x, x.shape[1] // 2, 1) * sine


def project_kernel(
    len_hbm, tok_hbm, gain_hbm, wq_hbm, wk_hbm, wv_hbm, anc_hbm, inv_hbm, q_ref, k_ref, v_ref,
    lengths, tok, gain, w, table, inverse, sems, csems,
):
    rows, width = tok.shape
    requests = lengths.shape[0]
    tree = rows // requests
    hd = inverse.shape[1]
    inner = wq_hbm.shape[1]
    part = width // CHUNKS
    firsts = [
        pltpu.make_async_copy(source, target, sems.at[i])
        for i, (source, target) in enumerate(
            ((anc_hbm, table), (len_hbm, lengths), (inv_hbm, inverse), (gain_hbm, gain))
        )
    ]
    for c in firsts:
        c.start()
    get_tok = pltpu.make_async_copy(tok_hbm, tok, sems.at[4])
    get_tok.start()
    copies = []
    for i in range(CHUNKS):
        at = pl.ds(i * part, part)
        copies.append(
            (
                pltpu.make_async_copy(wq_hbm.at[at], w.at[at, pl.ds(0, inner)], csems.at[0, i]),
                pltpu.make_async_copy(wk_hbm.at[at], w.at[at, pl.ds(inner, hd)], csems.at[1, i]),
                pltpu.make_async_copy(wv_hbm.at[at], w.at[at, pl.ds(inner + hd, hd)], csems.at[2, i]),
            )
        )

    def begin(i):
        if i < CHUNKS:
            for c in copies[i]:
                c.start()

    for i in range(AHEAD):
        begin(i)
    for c in firsts:
        c.wait()
    depth = jnp.sum(table[...], axis=1, keepdims=True).astype(F32) - 1.0
    places = jnp.concatenate(
        [
            depth[r * tree : (r + 1) * tree] + (PROMPT + lengths[r]).astype(F32)
            for r in range(requests)
        ],
        axis=0,
    )
    angles = places * inverse[...]
    lane = lax.broadcasted_iota(jnp.int32, angles.shape, 1)
    cosine = jnp.cos(angles)
    sine = jnp.sin(angles)
    sine = jnp.where(lane < hd // 2, -sine, sine)
    gains = gain[...].astype(F32)
    gains = jnp.concatenate([gains[i : i + 1] for i in range(gain.shape[0])], axis=1)
    get_tok.wait()
    begin(AHEAD)

    wide = tok[...].astype(F32)
    scale = lax.rsqrt(jnp.mean(wide * wide, axis=1, keepdims=True) + EPS)
    acc = None
    for i in range(CHUNKS):
        for c in copies[i]:
            c.wait()
        begin(AHEAD + 1 + i)
        at = slice(i * part, (i + 1) * part)
        normed = (tok[:, at].astype(F32) * scale * gains[:, at]).astype(BF16)
        d = dot(normed, w[at, :])
        acc = d if acc is None else acc + d
    heads = inner // hd
    fold = hd**-0.5 * math.log2(math.e)
    for g in range(heads):
        turned = rotate(acc[:, g * hd : (g + 1) * hd], cosine, sine)
        turned = (turned * fold).astype(BF16)
        for r in range(requests):
            q_ref[pl.ds((r * heads + g) * tree, tree), :] = turned[r * tree : (r + 1) * tree]
    k_ref[...] = rotate(acc[:, inner : inner + hd], cosine, sine).astype(BF16)
    v_ref[...] = acc[:, inner + hd :].astype(BF16)


def project_call(lengths, tokens, gain, w_query, w_key, w_value, ancestors, inverse):
    rows, width = tokens.shape
    hd = inverse.shape[1]
    inner = w_query.shape[1]
    return pl.pallas_call(
        project_kernel,
        in_specs=[HBM] * 8,
        out_specs=[VM, VM, VM],
        out_shape=[
            jax.ShapeDtypeStruct((rows * inner // hd, hd), BF16),
            jax.ShapeDtypeStruct((rows, hd), BF16),
            jax.ShapeDtypeStruct((rows, hd), BF16),
        ],
        scratch_shapes=[
            pltpu.SMEM(lengths.shape, jnp.int32),
            pltpu.VMEM((rows, width), BF16),
            pltpu.VMEM(gain.shape, BF16),
            pltpu.VMEM((width, inner + 2 * hd), BF16),
            pltpu.VMEM(ancestors.shape, jnp.int32),
            pltpu.VMEM(inverse.shape, F32),
            pltpu.SemaphoreType.DMA((5,)),
            pltpu.SemaphoreType.DMA((3, CHUNKS)),
        ],
        compiler_params=params(28),
        name="projections",
    )(lengths, tokens, gain, w_query, w_key, w_value, ancestors, inverse)


def prompt_sum(q, g, pieces, ones):
    weights, values = [], []
    for keys, vals in pieces:
        weights.append(jnp.exp2(dot_nt(q, keys[g])).astype(BF16))
        values.append(jnp.concatenate([vals[g], ones], axis=1))
    return dot(jnp.concatenate(weights, axis=1), jnp.concatenate(values, axis=0))


def source_of(at_ref, requests, shift, n_tok):
    return lax.rem(at_ref[0] + n_tok - shift, n_tok) * requests


def near_kernel(group_ref, at_ref, k, k_r, k_l, v, v_r, v_l, *refs, requests, shifts, n_tok):
    hd = k.shape[2]
    qrows = refs[0].shape[0] // requests
    pieces = [(k, v), (k_r, v_r), (k_l, v_l)]
    ones = jnp.ones((k.shape[1], hd), BF16)
    for shift, q_ref, out_ref in zip(shifts, refs[: len(shifts)], refs[len(shifts) :]):
        base = source_of(at_ref, requests, shift, n_tok)
        for r in range(requests):
            at = pl.ds(r * qrows, qrows)
            out_ref[at, :] = prompt_sum(q_ref[at, :], group_ref[base + r], pieces, ones)


def near_call(groups, at, qs, prompts, requests, shifts, n_tok):
    rows, hd = qs[0].shape
    n = len(shifts)
    return pl.pallas_call(
        lambda *refs: near_kernel(*refs, requests=requests, shifts=shifts, n_tok=n_tok),
        in_specs=[SMEM, SMEM] + [VM] * (6 + n),
        out_specs=[VM] * n,
        out_shape=[jax.ShapeDtypeStruct((rows, 2 * hd), F32)] * n,
        compiler_params=params(16),
        name="prompt_near",
    )(groups, at, *prompts, *qs)


def far_kernel(group_ref, at_ref, k_o, v_o, *refs, requests, shifts, n_tok):
    hd = k_o.shape[2]
    n = len(shifts)
    ones = jnp.ones((k_o.shape[1], hd), BF16)
    for shift, q_ref, near_ref, out_ref in zip(shifts, refs[:n], refs[n : 2 * n], refs[2 * n :]):
        qrows = q_ref.shape[0] // requests
        diagonal = lax.broadcasted_iota(jnp.int32, (qrows, hd), 0) == lax.broadcasted_iota(
            jnp.int32, (qrows, hd), 1
        )
        base = source_of(at_ref, requests, shift, n_tok)
        totals = []
        for r in range(requests):
            at = pl.ds(r * qrows, qrows)
            acc = near_ref[at, :] + prompt_sum(
                q_ref[at, :], group_ref[base + r], [(k_o, v_o)], ones
            )
            out_ref[at, :] = acc[:, :hd].astype(BF16)
            totals.append(jnp.sum(jnp.where(diagonal, acc[:, hd:], 0.0), axis=0, keepdims=True))
        total = jnp.concatenate(totals, axis=0)
        high = total.astype(BF16)
        low = (total - high.astype(F32)).astype(BF16)
        out_ref[pl.ds(requests * qrows, 2 * requests), :] = jnp.concatenate([high, low], axis=0)


def far_call(groups, at, nears, qs, k_o, v_o, requests, shifts, n_tok):
    rows, hd = qs[0].shape
    n = len(shifts)
    return pl.pallas_call(
        lambda *refs: far_kernel(*refs, requests=requests, shifts=shifts, n_tok=n_tok),
        in_specs=[SMEM, SMEM] + [VM] * (2 + 2 * n),
        out_specs=[VM] * n,
        out_shape=[jax.ShapeDtypeStruct((rows + 2 * requests, hd), BF16)] * n,
        compiler_params=params(16),
        name="prompt_far",
    )(groups, at, k_o, v_o, *qs, *nears)


def home_kernel(
    group_ref, at_ref, len_ref, q_ref, k, k_r, k_l, v, v_r, v_l, k_o, v_o, new_k, new_v, anc_hbm,
    ck_hbm, cv_hbm, out_ref, anc_ref, keys, values, where_ref, sems, anc_sem,
):
    requests, slots, hd = keys.shape
    qrows = q_ref.shape[0] // requests
    piece = slots // PIECES

    def copies(r, i):
        at = pl.ds(i * piece, piece)
        return (
            pltpu.make_async_copy(ck_hbm.at[r, at], keys.at[r, at], sems.at[0, r, i]),
            pltpu.make_async_copy(cv_hbm.at[r, at], values.at[r, at], sems.at[1, r, i]),
        )

    def each_copy(act):
        for i in range(PIECES):
            for r in range(requests):
                if i == 0:
                    for c in copies(r, i):
                        act(c)
                else:

                    @pl.when(len_ref[r] > i * piece)
                    def _(r=r, i=i):
                        for c in copies(r, i):
                            act(c)

    get_anc = pltpu.make_async_copy(anc_hbm, anc_ref, anc_sem)
    get_anc.start()
    tree = anc_ref.shape[1]
    each_copy(lambda c: c.start())
    count = 0
    for r in range(requests):

        def note(b, n, r=r):
            where_ref[0, n] = r
            where_ref[1, n] = b * KB
            return n + 1

        count = lax.fori_loop(0, (len_ref[r] + KB - 1) // KB, note, count)
    for j in range(LANES):
        where_ref[0, count + j] = requests - 1
        where_ref[1, count + j] = 0
    pieces = [(k, v), (k_r, v_r), (k_l, v_l), (k_o, v_o)]
    ones = jnp.ones((KB, hd), BF16)
    get_anc.wait()
    for r in range(requests):
        at = pl.ds(r * qrows, qrows)
        mine = pl.ds(r * tree, tree)
        q = q_ref[at, :]
        seen = jnp.concatenate([anc_ref[mine, :]] * (qrows // tree), axis=0)
        p = jnp.where(seen > 0, jnp.exp2(dot_nt(q, new_k[mine, :])), 0.0).astype(BF16)
        out_ref[at, :] = prompt_sum(
            q, group_ref[at_ref[0] * requests + r], pieces, ones
        ) + dot(p, jnp.concatenate([new_v[mine, :], ones[:tree]], axis=1))
    column = lax.broadcasted_iota(jnp.int32, (qrows, KB), 1)
    each_copy(lambda c: c.wait())

    def step(i, _):
        parts = []
        for j in range(LANES):
            n = i * LANES + j
            r = where_ref[0, n]
            first = pl.multiple_of(where_ref[1, n], KB)
            at = pl.ds(pl.multiple_of(r * qrows, qrows), qrows)
            limit = jnp.where(n < count, len_ref[r] - first, 0)
            s = dot_nt(q_ref[at, :], keys[r, pl.ds(first, KB), :])
            p = jnp.where(column < limit, jnp.exp2(s), 0.0).astype(BF16)
            both = jnp.concatenate([values[r, pl.ds(first, KB), :], ones], axis=1)
            parts.append((at, dot(p, both)))
        for at, d in parts:
            out_ref[at, :] += d
        return 0

    lax.fori_loop(0, (count + LANES - 1) // LANES, step, 0)


def home_call(groups, at, lengths, q, prompts, new_k, new_v, ancestors, cache_keys, cache_values):
    requests, slots, hd = cache_keys.shape
    return pl.pallas_call(
        home_kernel,
        in_specs=[SMEM, SMEM, SMEM] + [VM] * 11 + [HBM] * 3,
        out_specs=VM,
        out_shape=jax.ShapeDtypeStruct((q.shape[0], 2 * hd), F32),
        scratch_shapes=[
            pltpu.VMEM(ancestors.shape, jnp.int32),
            pltpu.VMEM(cache_keys.shape, BF16),
            pltpu.VMEM(cache_values.shape, BF16),
            pltpu.SMEM((2, requests * slots // KB + LANES), jnp.int32),
            pltpu.SemaphoreType.DMA((2, requests, PIECES)),
            pltpu.SemaphoreType.DMA,
        ],
        compiler_params=params(20),
        name="home_attention",
    )(groups, at, lengths, q, *prompts, new_k, new_v, ancestors, cache_keys, cache_values)


def merge_kernel(home_ref, a_ref, b_ref, c_ref, out_ref, *, requests):
    hd = a_ref.shape[1]
    qrows = home_ref.shape[0] // requests
    tree = out_ref.shape[0] // requests
    total = None
    for ref in (a_ref, b_ref, c_ref):
        both = ref[pl.ds(requests * qrows, 2 * requests), :].astype(F32)
        t = both[:requests] + both[requests:]
        total = t if total is None else total + t
    diagonal = lax.broadcasted_iota(jnp.int32, (qrows, hd), 0) == lax.broadcasted_iota(
        jnp.int32, (qrows, hd), 1
    )
    for r in range(requests):
        at = pl.ds(r * qrows, qrows)
        num = home_ref[at, pl.ds(0, hd)]
        for ref in (a_ref, b_ref, c_ref):
            num = num + ref[at, :].astype(F32)
        den = home_ref[at, pl.ds(hd, hd)] + jnp.sum(
            jnp.where(diagonal, jnp.broadcast_to(total[r : r + 1], (qrows, hd)), 0.0),
            axis=1,
            keepdims=True,
        )
        out = (num / den).astype(BF16)
        for g in range(qrows // tree):
            out_ref[pl.ds(r * tree, tree), pl.ds(g * hd, hd)] = out[g * tree : (g + 1) * tree]


def merge_call(home, a, b, c, requests, rows):
    hd = a.shape[1]
    return pl.pallas_call(
        lambda *refs: merge_kernel(*refs, requests=requests),
        in_specs=[VM] * 4,
        out_specs=VM,
        out_shape=jax.ShapeDtypeStruct((rows, home.shape[0] // rows * hd), BF16),
        compiler_params=params(8),
        name="merge",
    )(home, a, b, c)


def pick(acc_ref, x, tree):
    rows = []
    slot = lax.broadcasted_iota(jnp.int32, (tree, acc_ref.shape[1]), 0)
    for r in range(acc_ref.shape[0]):
        chosen = (slot == acc_ref[r : r + 1, :]).astype(F32).astype(BF16)
        rows.append(
            lax.dot_general(
                chosen, x[r * tree : (r + 1) * tree], (((0,), (0,)), ((), ())),
                preferred_element_type=F32,
            )
        )
    return rows


def pick_kernel(mdl_ref, acc_ref, tok_hbm, out_ref, tok, sem):
    cols = tok.shape[1]
    get = pltpu.make_async_copy(
        tok_hbm.at[:, pl.ds(pl.multiple_of(mdl_ref[0] * cols, 128), cols)], tok, sem
    )
    get.start()
    get.wait()
    for r, row in enumerate(pick(acc_ref, tok[...], tok.shape[0] // acc_ref.shape[0])):
        out_ref[r] = row


def pick_call(mdl, accepted, tokens, cols):
    return pl.pallas_call(
        pick_kernel,
        in_specs=[SMEM, VM, HBM],
        out_specs=VM,
        out_shape=jax.ShapeDtypeStruct(accepted.shape + (cols,), F32),
        scratch_shapes=[pltpu.VMEM((tokens.shape[0], cols), BF16), pltpu.SemaphoreType.DMA],
        compiler_params=params(4),
        name="pick_tokens",
    )(mdl, accepted, tokens)


def columns_of(mdl_ref, w_hbm, shift, side, count, cols):
    there = lax.rem(mdl_ref[0] // 2 + shift, count)
    start = (2 * there + lax.rem(mdl_ref[0] + side, 2)) * cols
    return w_hbm.at[:, pl.ds(pl.multiple_of(start, 128), cols)]


def columns_kernel(mdl_ref, w_hbm, send_ref, sems):
    count, _, cols = send_ref.shape
    copies = [
        pltpu.make_async_copy(
            columns_of(mdl_ref, w_hbm, i, 1, count, cols), send_ref.at[i], sems.at[i]
        )
        for i in range(count)
    ]
    for c in copies:
        c.start()
    for c in copies:
        c.wait()


def columns_call(mdl, w_out, count):
    cols = w_out.shape[1] // (2 * count)
    return pl.pallas_call(
        columns_kernel,
        in_specs=[SMEM, HBM],
        out_specs=VM,
        out_shape=jax.ShapeDtypeStruct((count, w_out.shape[0], cols), BF16),
        scratch_shapes=[pltpu.SemaphoreType.DMA((count,))],
        compiler_params=params(6),
        name="out_columns",
    )(mdl, w_out)


def first_kernel(mdl_ref, mine_ref, w_hbm, other_hbm, out_ref, other_ref, w, sems, *, shift):
    count, _, cols = other_hbm.shape
    get = pltpu.make_async_copy(columns_of(mdl_ref, w_hbm, shift, 0, count, cols), w, sems.at[0])
    get_other = pltpu.make_async_copy(other_hbm.at[shift], other_ref, sems.at[1])
    get.start()
    get_other.start()
    get.wait()
    out_ref[...] = dot(mine_ref[...], w[...])
    get_other.wait()


def out_first(mdl, mine, w_out, w_other, shift):
    rows, inner = mine.shape
    cols = w_other.shape[2]
    return pl.pallas_call(
        lambda *refs: first_kernel(*refs, shift=shift),
        in_specs=[SMEM, VM, HBM, HBM],
        out_specs=[VM, VM],
        out_shape=[
            jax.ShapeDtypeStruct((rows, cols), F32),
            jax.ShapeDtypeStruct((inner, cols), BF16),
        ],
        scratch_shapes=[pltpu.VMEM((inner, cols), BF16), pltpu.SemaphoreType.DMA((2,))],
        compiler_params=params(12),
        name="out_first",
    )(mdl, mine, w_out, w_other)


def second_kernel(first_ref, other_ref, w_ref, out_ref):
    out_ref[...] = (first_ref[...] + dot(other_ref[...], w_ref[...])).astype(BF16)


def out_second(first, other, w):
    return pl.pallas_call(
        second_kernel,
        in_specs=[VM] * 3,
        out_specs=VM,
        out_shape=jax.ShapeDtypeStruct(first.shape, BF16),
        compiler_params=params(12),
        name="out_second",
    )(first, other, w)


def out_kernel(mdl_ref, mine_ref, other_ref, w_hbm, wo_hbm, *refs, shifts):
    outs = refs[: len(shifts)]
    wa, wb, sems = refs[len(shifts) :]
    count, _, cols = wo_hbm.shape
    copies = []
    for i, shift in enumerate(shifts):
        two = (
            pltpu.make_async_copy(
                columns_of(mdl_ref, w_hbm, shift, 0, count, cols), wa.at[i], sems.at[0, i]
            ),
            pltpu.make_async_copy(wo_hbm.at[shift], wb.at[i], sems.at[1, i]),
        )
        for c in two:
            c.start()
        copies.append(two)
    for i, out in enumerate(outs):
        for c in copies[i]:
            c.wait()
        d = dot(mine_ref[...], wa[i]) + dot(other_ref[...], wb[i])
        out[...] = d.astype(out.dtype)


def out_call(mdl, mine, other, w_out, w_other, shifts, dtype):
    rows, inner = mine.shape
    cols = w_other.shape[2]
    n = len(shifts)
    return pl.pallas_call(
        lambda *refs: out_kernel(*refs, shifts=shifts),
        in_specs=[SMEM, VM, VM, HBM, HBM],
        out_specs=[VM] * n,
        out_shape=[jax.ShapeDtypeStruct((rows, cols), dtype)] * n,
        scratch_shapes=[
            pltpu.VMEM((n, inner, cols), BF16),
            pltpu.VMEM((n, inner, cols), BF16),
            pltpu.SemaphoreType.DMA((2, n)),
        ],
        compiler_params=params(12),
        name="out_proj",
    )(mdl, mine, other, w_out, w_other)


def last_kernel(acc_ref, own_ref, a_ref, b_ref, c_ref, tok_ref, out_ref, rows_ref):
    total = own_ref[...] + a_ref[...].astype(F32) + b_ref[...].astype(F32) + c_ref[...].astype(F32)
    rounded = total.astype(BF16)
    out_ref[...] = rounded
    for r, row in enumerate(pick(acc_ref, rounded, own_ref.shape[0] // acc_ref.shape[0])):
        rows_ref[r] = (tok_ref[r] + row).astype(BF16)


def last_call(accepted, own, a, b, c, picked):
    rows, cols = own.shape
    return pl.pallas_call(
        last_kernel,
        in_specs=[VM] * 6,
        out_specs=[VM, VM],
        out_shape=[
            jax.ShapeDtypeStruct((rows, cols), BF16),
            jax.ShapeDtypeStruct(picked.shape, BF16),
        ],
        compiler_params=params(8),
        name="last_sums",
    )(accepted, own, a, b, c, picked)


def shards(
    tokens, norm_gain, w_query, w_key, w_value, w_out, prompt_keys, prompt_values, cache_keys,
    cache_values, cache_length, request_group, ancestors, accepted,
):
    requests, tree = ancestors.shape[:2]
    rows = tokens.shape[0]
    hd = prompt_keys.shape[3]
    n_tok = lax.axis_size("tok")
    n_mdl = lax.axis_size("mdl")
    n_y = 4
    n_z = n_tok // n_y
    n_x = n_mdl // 2
    tok = lax.axis_index("tok")
    mdl = lax.axis_index("mdl")

    def along_y(v, n):
        perm = [(t, t // n_y * n_y + (t + n) % n_y) for t in range(n_tok)]
        return lax.ppermute(v, "tok", perm)

    def along_z(v, n):
        return lax.ppermute(v, "tok", [(t, (t + n * n_y) % n_tok) for t in range(n_tok)])

    def along_x(v, n):
        return lax.ppermute(v, "mdl", [(m, (m + 2 * n) % n_mdl) for m in range(n_mdl)])

    def other_core(v):
        return lax.ppermute(v, "mdl", [(m, m ^ 1) for m in range(n_mdl)])

    def in_hbm(v):
        return pltpu.with_memory_space_constraint(v, pltpu.HBM)

    tok_at = jnp.reshape(tok, (1,)).astype(jnp.int32)
    mdl_at = jnp.reshape(mdl, (1,)).astype(jnp.int32)

    squeeze = lambda v: v.reshape(v.shape[0], v.shape[1], v.shape[3])
    k, v = squeeze(prompt_keys), squeeze(prompt_values)
    k_r, k_l = along_y(k, 1), along_y(k, -1)
    v_r, v_l = along_y(v, 1), along_y(v, -1)

    exponent = np.arange(hd // 2, dtype=np.float64) * (2.0 / hd)
    inverse = jnp.asarray(np.tile(THETA**-exponent, 2)[None, :], dtype=F32)
    table = ancestors.reshape(rows, tree)
    q, new_k, new_v = project_call(
        *map(
            in_hbm,
            (
                cache_length, tokens, norm_gain.reshape(-1, hd), w_query, w_key, w_value, table,
                inverse,
            ),
        )
    )
    shifts = (2, 1, -1)
    q_far = [along_z(q, n) for n in shifts]

    w_send = columns_call(mdl_at, in_hbm(w_out), n_x)
    w_other = in_hbm(other_core(w_send))

    k_o = along_y(k_r, 1)
    v_o = along_y(v_l, -1)
    near = tuple(map(in_hbm, (k, k_r, k_l, v, v_r, v_l)))

    turns = [n % n_z * n_y for n in shifts]
    nears = near_call(request_group, tok_at, q_far, near, requests, turns, n_tok)
    parts = []
    for some in (slice(0, 1), slice(1, 3)):
        parts += far_call(
            request_group, tok_at, nears[some], q_far[some], k_o, v_o, requests, turns[some],
            n_tok,
        )
    back = [along_z(part, -n) for n, part in zip(shifts, parts)]
    home = home_call(
        request_group, tok_at, cache_length, q, (k, k_r, k_l, v, v_r, v_l, k_o, v_o), new_k, new_v, in_hbm(table),
        in_hbm(squeeze(cache_keys)), in_hbm(squeeze(cache_values)),
    )
    attended = merge_call(home, *back, requests, rows)

    attended_other = other_core(attended)
    weights = (in_hbm(w_out), w_other)
    first, w_second = out_first(mdl_at, attended, *weights, 2)
    far = along_x(out_second(first, attended_other, w_second), 2)
    both = (mdl_at, attended, attended_other, *weights)
    up, down = out_call(*both, (1, n_x - 1), BF16)
    up = along_x(up, 1)
    down = along_x(down, -1)
    (own_sum,) = out_call(*both, (0,), F32)
    picked = pick_call(mdl_at, accepted, in_hbm(tokens), w_other.shape[2])
    return tuple(last_call(accepted, own_sum, far, up, down, picked))


def solution(mesh):
    placed = (
        P("tok", None),
        P(),
        P(None, "mdl"),
        P(None, "mdl"),
        P(None, "mdl"),
        P("mdl", None),
        P(None, "tok", "mdl", None),
        P(None, "tok", "mdl", None),
        P("tok", None, "mdl", None),
        P("tok", None, "mdl", None),
        P("tok"),
        P(),
        P("tok", None, None),
        P("tok", None),
    )

    return jax.shard_map(
        shards,
        mesh=mesh,
        in_specs=placed,
        out_specs=(P("tok", "mdl"), P("tok", None, "mdl")),
        check_vma=False,
    )
```

```python
import math

import jax
import jax.numpy as jnp
import numpy as np
from jax import lax
from jax.experimental import pallas as pl
from jax.experimental.pallas import tpu as pltpu
from jax.sharding import PartitionSpec as P


PROMPT = 4096
THETA = 100000000.0
EPS = 1e-05

F32 = jnp.float32
BF16 = jnp.bfloat16

HBM = pl.BlockSpec(memory_space=pltpu.HBM)
SMEM = pl.BlockSpec(memory_space=pltpu.SMEM)
VM = pl.BlockSpec(memory_space=pltpu.VMEM)
CHUNKS = 4
AHEAD = 1
KB = 256
PIECES = 2
LANES = 8
NT = (((1,), (1,)), ((), ()))


def params(mib):
    return pltpu.CompilerParams(vmem_limit_bytes=mib * 1024 * 1024)


def dot(a, b):
    return jnp.dot(a, b, preferred_element_type=F32)


def dot_nt(a, b):
    return lax.dot_general(a, b, NT, preferred_element_type=F32)


def rotate(x, cosine, sine):
    return x * cosine + pltpu.roll(x, x.shape[1] // 2, 1) * sine


def project_kernel(
    len_hbm, tok_hbm, gain_hbm, wq_hbm, wk_hbm, wv_hbm, anc_hbm, inv_hbm, q_ref, k_ref, v_ref,
    lengths, tok, gain, w, table, inverse, sems, csems,
):
    rows, width = tok.shape
    requests = lengths.shape[0]
    tree = rows // requests
    hd = inverse.shape[1]
    inner = wq_hbm.shape[1]
    part = width // CHUNKS
    firsts = [
        pltpu.make_async_copy(source, target, sems.at[i])
        for i, (source, target) in enumerate(
            ((anc_hbm, table), (len_hbm, lengths), (inv_hbm, inverse), (gain_hbm, gain))
        )
    ]
    for c in firsts:
        c.start()
    get_tok = pltpu.make_async_copy(tok_hbm, tok, sems.at[4])
    get_tok.start()
    copies = []
    for i in range(CHUNKS):
        at = pl.ds(i * part, part)
        copies.append(
            (
                pltpu.make_async_copy(wq_hbm.at[at], w.at[at, pl.ds(0, inner)], csems.at[0, i]),
                pltpu.make_async_copy(wk_hbm.at[at], w.at[at, pl.ds(inner, hd)], csems.at[1, i]),
                pltpu.make_async_copy(wv_hbm.at[at], w.at[at, pl.ds(inner + hd, hd)], csems.at[2, i]),
            )
        )

    def begin(i):
        if i < CHUNKS:
            for c in copies[i]:
                c.start()

    for i in range(AHEAD):
        begin(i)
    for c in firsts:
        c.wait()
    depth = jnp.sum(table[...], axis=1, keepdims=True).astype(F32) - 1.0
    places = jnp.concatenate(
        [
            depth[r * tree : (r + 1) * tree] + (PROMPT + lengths[r]).astype(F32)
            for r in range(requests)
        ],
        axis=0,
    )
    angles = places * inverse[...]
    lane = lax.broadcasted_iota(jnp.int32, angles.shape, 1)
    cosine = jnp.cos(angles)
    sine = jnp.sin(angles)
    sine = jnp.where(lane < hd // 2, -sine, sine)
    gains = gain[...].astype(F32)
    gains = jnp.concatenate([gains[i : i + 1] for i in range(gain.shape[0])], axis=1)
    get_tok.wait()
    begin(AHEAD)

    wide = tok[...].astype(F32)
    scale = lax.rsqrt(jnp.mean(wide * wide, axis=1, keepdims=True) + EPS)
    acc = None
    for i in range(CHUNKS):
        for c in copies[i]:
            c.wait()
        begin(AHEAD + 1 + i)
        at = slice(i * part, (i + 1) * part)
        normed = (tok[:, at].astype(F32) * scale * gains[:, at]).astype(BF16)
        d = dot(normed, w[at, :])
        acc = d if acc is None else acc + d
    heads = inner // hd
    fold = hd**-0.5 * math.log2(math.e)
    for g in range(heads):
        turned = rotate(acc[:, g * hd : (g + 1) * hd], cosine, sine)
        turned = (turned * fold).astype(BF16)
        for r in range(requests):
            q_ref[pl.ds((r * heads + g) * tree, tree), :] = turned[r * tree : (r + 1) * tree]
    k_ref[...] = rotate(acc[:, inner : inner + hd], cosine, sine).astype(BF16)
    v_ref[...] = acc[:, inner + hd :].astype(BF16)


def project_call(lengths, tokens, gain, w_query, w_key, w_value, ancestors, inverse):
    rows, width = tokens.shape
    hd = inverse.shape[1]
    inner = w_query.shape[1]
    return pl.pallas_call(
        project_kernel,
        in_specs=[HBM] * 8,
        out_specs=[VM, VM, VM],
        out_shape=[
            jax.ShapeDtypeStruct((rows * inner // hd, hd), BF16),
            jax.ShapeDtypeStruct((rows, hd), BF16),
            jax.ShapeDtypeStruct((rows, hd), BF16),
        ],
        scratch_shapes=[
            pltpu.SMEM(lengths.shape, jnp.int32),
            pltpu.VMEM((rows, width), BF16),
            pltpu.VMEM(gain.shape, BF16),
            pltpu.VMEM((width, inner + 2 * hd), BF16),
            pltpu.VMEM(ancestors.shape, jnp.int32),
            pltpu.VMEM(inverse.shape, F32),
            pltpu.SemaphoreType.DMA((5,)),
            pltpu.SemaphoreType.DMA((3, CHUNKS)),
        ],
        compiler_params=params(28),
        name="projections",
    )(lengths, tokens, gain, w_query, w_key, w_value, ancestors, inverse)


def prompt_sum(q, g, pieces, ones):
    weights, values = [], []
    for keys, vals in pieces:
        weights.append(jnp.exp2(dot_nt(q, keys[g])).astype(BF16))
        values.append(jnp.concatenate([vals[g], ones], axis=1))
    return dot(jnp.concatenate(weights, axis=1), jnp.concatenate(values, axis=0))


def source_of(at_ref, requests, shift, n_tok):
    return lax.rem(at_ref[0] + n_tok - shift, n_tok) * requests


def near_kernel(group_ref, at_ref, k, k_r, k_l, v, v_r, v_l, *refs, requests, shifts, n_tok):
    hd = k.shape[2]
    qrows = refs[0].shape[0] // requests
    pieces = [(k, v), (k_r, v_r), (k_l, v_l)]
    ones = jnp.ones((k.shape[1], hd), BF16)
    for shift, q_ref, out_ref in zip(shifts, refs[: len(shifts)], refs[len(shifts) :]):
        base = source_of(at_ref, requests, shift, n_tok)
        for r in range(requests):
            at = pl.ds(r * qrows, qrows)
            out_ref[at, :] = prompt_sum(q_ref[at, :], group_ref[base + r], pieces, ones)


def near_call(groups, at, qs, prompts, requests, shifts, n_tok):
    rows, hd = qs[0].shape
    n = len(shifts)
    return pl.pallas_call(
        lambda *refs: near_kernel(*refs, requests=requests, shifts=shifts, n_tok=n_tok),
        in_specs=[SMEM, SMEM] + [VM] * (6 + n),
        out_specs=[VM] * n,
        out_shape=[jax.ShapeDtypeStruct((rows, 2 * hd), F32)] * n,
        compiler_params=params(16),
        name="prompt_near",
    )(groups, at, *prompts, *qs)


def far_kernel(group_ref, at_ref, k_o, v_o, *refs, requests, shifts, n_tok):
    hd = k_o.shape[2]
    n = len(shifts)
    ones = jnp.ones((k_o.shape[1], hd), BF16)
    for shift, q_ref, near_ref, out_ref in zip(shifts, refs[:n], refs[n : 2 * n], refs[2 * n :]):
        qrows = q_ref.shape[0] // requests
        diagonal = lax.broadcasted_iota(jnp.int32, (qrows, hd), 0) == lax.broadcasted_iota(
            jnp.int32, (qrows, hd), 1
        )
        base = source_of(at_ref, requests, shift, n_tok)
        totals = []
        for r in range(requests):
            at = pl.ds(r * qrows, qrows)
            acc = near_ref[at, :] + prompt_sum(
                q_ref[at, :], group_ref[base + r], [(k_o, v_o)], ones
            )
            out_ref[at, :] = acc[:, :hd].astype(BF16)
            totals.append(jnp.sum(jnp.where(diagonal, acc[:, hd:], 0.0), axis=0, keepdims=True))
        total = jnp.concatenate(totals, axis=0)
        high = total.astype(BF16)
        low = (total - high.astype(F32)).astype(BF16)
        out_ref[pl.ds(requests * qrows, 2 * requests), :] = jnp.concatenate([high, low], axis=0)


def far_call(groups, at, nears, qs, k_o, v_o, requests, shifts, n_tok):
    rows, hd = qs[0].shape
    n = len(shifts)
    return pl.pallas_call(
        lambda *refs: far_kernel(*refs, requests=requests, shifts=shifts, n_tok=n_tok),
        in_specs=[SMEM, SMEM] + [VM] * (2 + 2 * n),
        out_specs=[VM] * n,
        out_shape=[jax.ShapeDtypeStruct((rows + 2 * requests, hd), BF16)] * n,
        compiler_params=params(16),
        name="prompt_far",
    )(groups, at, k_o, v_o, *qs, *nears)


def own_kernel(group_ref, at_ref, q_ref, k, k_r, k_l, v, v_r, v_l, out_hbm, acc_ref, sems):
    hd = k.shape[2]
    requests = sems.shape[0]
    qrows = q_ref.shape[0] // requests
    pieces = [(k, v), (k_r, v_r), (k_l, v_l)]
    ones = jnp.ones((k.shape[1], hd), BF16)
    puts = []
    for r in range(requests):
        at = pl.ds(r * qrows, qrows)
        acc_ref[at, :] = prompt_sum(
            q_ref[at, :], group_ref[at_ref[0] * requests + r], pieces, ones
        )
        put = pltpu.make_async_copy(acc_ref.at[at], out_hbm.at[at], sems.at[r])
        put.start()
        puts.append(put)
    for put in puts:
        put.wait()


def own_call(groups, at, q, prompts, requests):
    shape = (q.shape[0], 2 * q.shape[1])
    return pl.pallas_call(
        own_kernel,
        in_specs=[SMEM, SMEM] + [VM] * 7,
        out_specs=HBM,
        out_shape=pltpu.HBM(shape, F32),
        scratch_shapes=[pltpu.VMEM(shape, F32), pltpu.SemaphoreType.DMA((requests,))],
        compiler_params=params(12),
        name="own_near",
    )(groups, at, q, *prompts)


def home_kernel(
    group_ref, at_ref, len_ref, q_ref, k_o, v_o, new_k, new_v, anc_hbm, own_hbm, ck_hbm, cv_hbm,
    out_ref, anc_ref, own_ref, keys, values, where_ref, sems, anc_sem, own_sem,
):
    requests, slots, hd = keys.shape
    qrows = q_ref.shape[0] // requests
    piece = slots // PIECES

    def copies(r, i):
        at = pl.ds(i * piece, piece)
        return (
            pltpu.make_async_copy(ck_hbm.at[r, at], keys.at[r, at], sems.at[0, r, i]),
            pltpu.make_async_copy(cv_hbm.at[r, at], values.at[r, at], sems.at[1, r, i]),
        )

    def each_copy(act):
        for i in range(PIECES):
            for r in range(requests):
                if i == 0:
                    for c in copies(r, i):
                        act(c)
                else:

                    @pl.when(len_ref[r] > i * piece)
                    def _(r=r, i=i):
                        for c in copies(r, i):
                            act(c)

    get_anc = pltpu.make_async_copy(anc_hbm, anc_ref, anc_sem)
    get_anc.start()
    get_own = pltpu.make_async_copy(own_hbm, own_ref, own_sem)
    get_own.start()
    tree = anc_ref.shape[1]
    each_copy(lambda c: c.start())
    count = 0
    for r in range(requests):

        def note(b, n, r=r):
            where_ref[0, n] = r
            where_ref[1, n] = b * KB
            return n + 1

        count = lax.fori_loop(0, (len_ref[r] + KB - 1) // KB, note, count)
    for j in range(LANES):
        where_ref[0, count + j] = requests - 1
        where_ref[1, count + j] = 0
    pieces = [(k_o, v_o)]
    ones = jnp.ones((KB, hd), BF16)
    get_anc.wait()
    get_own.wait()
    for r in range(requests):
        at = pl.ds(r * qrows, qrows)
        mine = pl.ds(r * tree, tree)
        q = q_ref[at, :]
        seen = jnp.concatenate([anc_ref[mine, :]] * (qrows // tree), axis=0)
        p = jnp.where(seen > 0, jnp.exp2(dot_nt(q, new_k[mine, :])), 0.0).astype(BF16)
        out_ref[at, :] = own_ref[at, :] + prompt_sum(
            q, group_ref[at_ref[0] * requests + r], pieces, ones
        ) + dot(p, jnp.concatenate([new_v[mine, :], ones[:tree]], axis=1))
    column = lax.broadcasted_iota(jnp.int32, (qrows, KB), 1)
    each_copy(lambda c: c.wait())

    def step(i, _):
        parts = []
        for j in range(LANES):
            n = i * LANES + j
            r = where_ref[0, n]
            first = pl.multiple_of(where_ref[1, n], KB)
            at = pl.ds(pl.multiple_of(r * qrows, qrows), qrows)
            limit = jnp.where(n < count, len_ref[r] - first, 0)
            s = dot_nt(q_ref[at, :], keys[r, pl.ds(first, KB), :])
            p = jnp.where(column < limit, jnp.exp2(s), 0.0).astype(BF16)
            both = jnp.concatenate([values[r, pl.ds(first, KB), :], ones], axis=1)
            parts.append((at, dot(p, both)))
        for at, d in parts:
            out_ref[at, :] += d
        return 0

    lax.fori_loop(0, (count + LANES - 1) // LANES, step, 0)


def home_call(groups, at, lengths, q, far, new_k, new_v, ancestors, own, cache_keys, cache_values):
    requests, slots, hd = cache_keys.shape
    return pl.pallas_call(
        home_kernel,
        in_specs=[SMEM, SMEM, SMEM] + [VM] * 5 + [HBM] * 4,
        out_specs=VM,
        out_shape=jax.ShapeDtypeStruct((q.shape[0], 2 * hd), F32),
        scratch_shapes=[
            pltpu.VMEM(ancestors.shape, jnp.int32),
            pltpu.VMEM(own.shape, F32),
            pltpu.VMEM(cache_keys.shape, BF16),
            pltpu.VMEM(cache_values.shape, BF16),
            pltpu.SMEM((2, requests * slots // KB + LANES), jnp.int32),
            pltpu.SemaphoreType.DMA((2, requests, PIECES)),
            pltpu.SemaphoreType.DMA,
            pltpu.SemaphoreType.DMA,
        ],
        compiler_params=params(20),
        name="home_attention",
    )(groups, at, lengths, q, *far, new_k, new_v, ancestors, own, cache_keys, cache_values)


def merge_kernel(home_ref, a_ref, b_ref, c_ref, out_ref, *, requests):
    hd = a_ref.shape[1]
    qrows = home_ref.shape[0] // requests
    tree = out_ref.shape[0] // requests
    total = None
    for ref in (a_ref, b_ref, c_ref):
        both = ref[pl.ds(requests * qrows, 2 * requests), :].astype(F32)
        t = both[:requests] + both[requests:]
        total = t if total is None else total + t
    diagonal = lax.broadcasted_iota(jnp.int32, (qrows, hd), 0) == lax.broadcasted_iota(
        jnp.int32, (qrows, hd), 1
    )
    for r in range(requests):
        at = pl.ds(r * qrows, qrows)
        num = home_ref[at, pl.ds(0, hd)]
        for ref in (a_ref, b_ref, c_ref):
            num = num + ref[at, :].astype(F32)
        den = home_ref[at, pl.ds(hd, hd)] + jnp.sum(
            jnp.where(diagonal, jnp.broadcast_to(total[r : r + 1], (qrows, hd)), 0.0),
            axis=1,
            keepdims=True,
        )
        out = (num / den).astype(BF16)
        for g in range(qrows // tree):
            out_ref[pl.ds(r * tree, tree), pl.ds(g * hd, hd)] = out[g * tree : (g + 1) * tree]


def merge_call(home, a, b, c, requests, rows):
    hd = a.shape[1]
    return pl.pallas_call(
        lambda *refs: merge_kernel(*refs, requests=requests),
        in_specs=[VM] * 4,
        out_specs=VM,
        out_shape=jax.ShapeDtypeStruct((rows, home.shape[0] // rows * hd), BF16),
        compiler_params=params(8),
        name="merge",
    )(home, a, b, c)


def pick(acc_ref, x, tree):
    rows = []
    slot = lax.broadcasted_iota(jnp.int32, (tree, acc_ref.shape[1]), 0)
    for r in range(acc_ref.shape[0]):
        chosen = (slot == acc_ref[r : r + 1, :]).astype(F32).astype(BF16)
        rows.append(
            lax.dot_general(
                chosen, x[r * tree : (r + 1) * tree], (((0,), (0,)), ((), ())),
                preferred_element_type=F32,
            )
        )
    return rows


def pick_kernel(mdl_ref, acc_ref, tok_hbm, out_ref, tok, sem):
    cols = tok.shape[1]
    get = pltpu.make_async_copy(
        tok_hbm.at[:, pl.ds(pl.multiple_of(mdl_ref[0] * cols, 128), cols)], tok, sem
    )
    get.start()
    get.wait()
    for r, row in enumerate(pick(acc_ref, tok[...], tok.shape[0] // acc_ref.shape[0])):
        out_ref[r] = row


def pick_call(mdl, accepted, tokens, cols):
    return pl.pallas_call(
        pick_kernel,
        in_specs=[SMEM, VM, HBM],
        out_specs=VM,
        out_shape=jax.ShapeDtypeStruct(accepted.shape + (cols,), F32),
        scratch_shapes=[pltpu.VMEM((tokens.shape[0], cols), BF16), pltpu.SemaphoreType.DMA],
        compiler_params=params(4),
        name="pick_tokens",
    )(mdl, accepted, tokens)


def columns_of(mdl_ref, w_hbm, shift, side, count, cols):
    there = lax.rem(mdl_ref[0] // 2 + shift, count)
    start = (2 * there + lax.rem(mdl_ref[0] + side, 2)) * cols
    return w_hbm.at[:, pl.ds(pl.multiple_of(start, 128), cols)]


def columns_kernel(mdl_ref, w_hbm, send_ref, sems):
    count, _, cols = send_ref.shape
    copies = [
        pltpu.make_async_copy(
            columns_of(mdl_ref, w_hbm, i, 1, count, cols), send_ref.at[i], sems.at[i]
        )
        for i in range(count)
    ]
    for c in copies:
        c.start()
    for c in copies:
        c.wait()


def columns_call(mdl, w_out, count):
    cols = w_out.shape[1] // (2 * count)
    return pl.pallas_call(
        columns_kernel,
        in_specs=[SMEM, HBM],
        out_specs=VM,
        out_shape=jax.ShapeDtypeStruct((count, w_out.shape[0], cols), BF16),
        scratch_shapes=[pltpu.SemaphoreType.DMA((count,))],
        compiler_params=params(6),
        name="out_columns",
    )(mdl, w_out)


def first_kernel(mdl_ref, mine_ref, w_hbm, other_hbm, out_ref, other_ref, w, sems, *, shift):
    count, _, cols = other_hbm.shape
    get = pltpu.make_async_copy(columns_of(mdl_ref, w_hbm, shift, 0, count, cols), w, sems.at[0])
    get_other = pltpu.make_async_copy(other_hbm.at[shift], other_ref, sems.at[1])
    get.start()
    get_other.start()
    get.wait()
    out_ref[...] = dot(mine_ref[...], w[...])
    get_other.wait()


def out_first(mdl, mine, w_out, w_other, shift):
    rows, inner = mine.shape
    cols = w_other.shape[2]
    return pl.pallas_call(
        lambda *refs: first_kernel(*refs, shift=shift),
        in_specs=[SMEM, VM, HBM, HBM],
        out_specs=[VM, VM],
        out_shape=[
            jax.ShapeDtypeStruct((rows, cols), F32),
            jax.ShapeDtypeStruct((inner, cols), BF16),
        ],
        scratch_shapes=[pltpu.VMEM((inner, cols), BF16), pltpu.SemaphoreType.DMA((2,))],
        compiler_params=params(12),
        name="out_first",
    )(mdl, mine, w_out, w_other)


def second_kernel(first_ref, other_ref, w_ref, out_ref):
    out_ref[...] = (first_ref[...] + dot(other_ref[...], w_ref[...])).astype(BF16)


def out_second(first, other, w):
    return pl.pallas_call(
        second_kernel,
        in_specs=[VM] * 3,
        out_specs=VM,
        out_shape=jax.ShapeDtypeStruct(first.shape, BF16),
        compiler_params=params(12),
        name="out_second",
    )(first, other, w)


def out_kernel(mdl_ref, mine_ref, other_ref, w_hbm, wo_hbm, *refs, shifts):
    outs = refs[: len(shifts)]
    wa, wb, sems = refs[len(shifts) :]
    count, _, cols = wo_hbm.shape
    copies = []
    for i, shift in enumerate(shifts):
        two = (
            pltpu.make_async_copy(
                columns_of(mdl_ref, w_hbm, shift, 0, count, cols), wa.at[i], sems.at[0, i]
            ),
            pltpu.make_async_copy(wo_hbm.at[shift], wb.at[i], sems.at[1, i]),
        )
        for c in two:
            c.start()
        copies.append(two)
    for i, out in enumerate(outs):
        for c in copies[i]:
            c.wait()
        d = dot(mine_ref[...], wa[i]) + dot(other_ref[...], wb[i])
        out[...] = d.astype(out.dtype)


def out_call(mdl, mine, other, w_out, w_other, shifts, dtype):
    rows, inner = mine.shape
    cols = w_other.shape[2]
    n = len(shifts)
    return pl.pallas_call(
        lambda *refs: out_kernel(*refs, shifts=shifts),
        in_specs=[SMEM, VM, VM, HBM, HBM],
        out_specs=[VM] * n,
        out_shape=[jax.ShapeDtypeStruct((rows, cols), dtype)] * n,
        scratch_shapes=[
            pltpu.VMEM((n, inner, cols), BF16),
            pltpu.VMEM((n, inner, cols), BF16),
            pltpu.SemaphoreType.DMA((2, n)),
        ],
        compiler_params=params(12),
        name="out_proj",
    )(mdl, mine, other, w_out, w_other)


def last_kernel(acc_ref, own_ref, a_ref, b_ref, c_ref, tok_ref, out_ref, rows_ref):
    total = own_ref[...] + a_ref[...].astype(F32) + b_ref[...].astype(F32) + c_ref[...].astype(F32)
    rounded = total.astype(BF16)
    out_ref[...] = rounded
    for r, row in enumerate(pick(acc_ref, rounded, own_ref.shape[0] // acc_ref.shape[0])):
        rows_ref[r] = (tok_ref[r] + row).astype(BF16)


def last_call(accepted, own, a, b, c, picked):
    rows, cols = own.shape
    return pl.pallas_call(
        last_kernel,
        in_specs=[VM] * 6,
        out_specs=[VM, VM],
        out_shape=[
            jax.ShapeDtypeStruct((rows, cols), BF16),
            jax.ShapeDtypeStruct(picked.shape, BF16),
        ],
        compiler_params=params(8),
        name="last_sums",
    )(accepted, own, a, b, c, picked)


def shards(
    tokens, norm_gain, w_query, w_key, w_value, w_out, prompt_keys, prompt_values, cache_keys,
    cache_values, cache_length, request_group, ancestors, accepted,
):
    requests, tree = ancestors.shape[:2]
    rows = tokens.shape[0]
    hd = prompt_keys.shape[3]
    n_tok = lax.axis_size("tok")
    n_mdl = lax.axis_size("mdl")
    n_y = 4
    n_z = n_tok // n_y
    n_x = n_mdl // 2
    tok = lax.axis_index("tok")
    mdl = lax.axis_index("mdl")

    def along_y(v, n):
        perm = [(t, t // n_y * n_y + (t + n) % n_y) for t in range(n_tok)]
        return lax.ppermute(v, "tok", perm)

    def along_z(v, n):
        return lax.ppermute(v, "tok", [(t, (t + n * n_y) % n_tok) for t in range(n_tok)])

    def along_x(v, n):
        return lax.ppermute(v, "mdl", [(m, (m + 2 * n) % n_mdl) for m in range(n_mdl)])

    def other_core(v):
        return lax.ppermute(v, "mdl", [(m, m ^ 1) for m in range(n_mdl)])

    def in_hbm(v):
        return pltpu.with_memory_space_constraint(v, pltpu.HBM)

    tok_at = jnp.reshape(tok, (1,)).astype(jnp.int32)
    mdl_at = jnp.reshape(mdl, (1,)).astype(jnp.int32)

    squeeze = lambda v: v.reshape(v.shape[0], v.shape[1], v.shape[3])
    k, v = squeeze(prompt_keys), squeeze(prompt_values)
    k_r, k_l = along_y(k, 1), along_y(k, -1)
    v_r, v_l = along_y(v, 1), along_y(v, -1)

    exponent = np.arange(hd // 2, dtype=np.float64) * (2.0 / hd)
    inverse = jnp.asarray(np.tile(THETA**-exponent, 2)[None, :], dtype=F32)
    table = ancestors.reshape(rows, tree)
    q, new_k, new_v = project_call(
        *map(
            in_hbm,
            (
                cache_length, tokens, norm_gain.reshape(-1, hd), w_query, w_key, w_value, table,
                inverse,
            ),
        )
    )
    shifts = (2, 1, -1)
    q_far = [along_z(q, n) for n in shifts]

    w_send = columns_call(mdl_at, in_hbm(w_out), n_x)
    w_other = in_hbm(other_core(w_send))

    k_o = along_y(k_r, 1)
    v_o = along_y(v_l, -1)
    near = tuple(map(in_hbm, (k, k_r, k_l, v, v_r, v_l)))

    own = own_call(request_group, tok_at, q, near, requests)

    turns = [n % n_z * n_y for n in shifts]
    nears = near_call(request_group, tok_at, q_far, near, requests, turns, n_tok)
    parts = []
    for some in (slice(0, 1), slice(1, 3)):
        parts += far_call(
            request_group, tok_at, nears[some], q_far[some], k_o, v_o, requests, turns[some],
            n_tok,
        )
    back = [along_z(part, -n) for n, part in zip(shifts, parts)]
    home = home_call(
        request_group, tok_at, cache_length, q, (k_o, v_o), new_k, new_v, in_hbm(table),
        in_hbm(own), in_hbm(squeeze(cache_keys)), in_hbm(squeeze(cache_values)),
    )
    attended = merge_call(home, *back, requests, rows)

    attended_other = other_core(attended)
    weights = (in_hbm(w_out), w_other)
    first, w_second = out_first(mdl_at, attended, *weights, 2)
    far = along_x(out_second(first, attended_other, w_second), 2)
    both = (mdl_at, attended, attended_other, *weights)
    up, down = out_call(*both, (1, n_x - 1), BF16)
    up = along_x(up, 1)
    down = along_x(down, -1)
    (own_sum,) = out_call(*both, (0,), F32)
    picked = pick_call(mdl_at, accepted, in_hbm(tokens), w_other.shape[2])
    return tuple(last_call(accepted, own_sum, far, up, down, picked))


def solution(mesh):
    placed = (
        P("tok", None),
        P(),
        P(None, "mdl"),
        P(None, "mdl"),
        P(None, "mdl"),
        P("mdl", None),
        P(None, "tok", "mdl", None),
        P(None, "tok", "mdl", None),
        P("tok", None, "mdl", None),
        P("tok", None, "mdl", None),
        P("tok"),
        P(),
        P("tok", None, None),
        P("tok", None),
    )

    return jax.shard_map(
        shards,
        mesh=mesh,
        in_specs=placed,
        out_specs=(P("tok", "mdl"), P("tok", None, "mdl")),
        check_vma=False,
    )
```

```python
import math

import jax
import jax.numpy as jnp
import numpy as np
from jax import lax
from jax.experimental import pallas as pl
from jax.experimental.pallas import tpu as pltpu
from jax.sharding import PartitionSpec as P


PROMPT = 4096
THETA = 100000000.0
EPS = 1e-05

F32 = jnp.float32
BF16 = jnp.bfloat16

HBM = pl.BlockSpec(memory_space=pltpu.HBM)
SMEM = pl.BlockSpec(memory_space=pltpu.SMEM)
VM = pl.BlockSpec(memory_space=pltpu.VMEM)
CHUNKS = 4
AHEAD = 1
KB = 256
PIECES = 2
LANES = 8
NT = (((1,), (1,)), ((), ()))


def params(mib):
    return pltpu.CompilerParams(vmem_limit_bytes=mib * 1024 * 1024)


def dot(a, b):
    return jnp.dot(a, b, preferred_element_type=F32)


def dot_nt(a, b):
    return lax.dot_general(a, b, NT, preferred_element_type=F32)


def rotate(x, cosine, sine):
    return x * cosine + pltpu.roll(x, x.shape[1] // 2, 1) * sine


def project_kernel(
    len_hbm, tok_hbm, gain_hbm, wq_hbm, wk_hbm, wv_hbm, anc_hbm, inv_hbm, q_ref, k_ref, v_ref,
    lengths, tok, gain, w, table, inverse, sems, csems,
):
    rows, width = tok.shape
    requests = lengths.shape[0]
    tree = rows // requests
    hd = inverse.shape[1]
    inner = wq_hbm.shape[1]
    part = width // CHUNKS
    firsts = [
        pltpu.make_async_copy(source, target, sems.at[i])
        for i, (source, target) in enumerate(
            ((anc_hbm, table), (len_hbm, lengths), (inv_hbm, inverse), (gain_hbm, gain))
        )
    ]
    for c in firsts:
        c.start()
    get_tok = pltpu.make_async_copy(tok_hbm, tok, sems.at[4])
    get_tok.start()
    copies = []
    for i in range(CHUNKS):
        at = pl.ds(i * part, part)
        copies.append(
            (
                pltpu.make_async_copy(wq_hbm.at[at], w.at[at, pl.ds(0, inner)], csems.at[0, i]),
                pltpu.make_async_copy(wk_hbm.at[at], w.at[at, pl.ds(inner, hd)], csems.at[1, i]),
                pltpu.make_async_copy(wv_hbm.at[at], w.at[at, pl.ds(inner + hd, hd)], csems.at[2, i]),
            )
        )

    def begin(i):
        if i < CHUNKS:
            for c in copies[i]:
                c.start()

    for i in range(AHEAD):
        begin(i)
    for c in firsts:
        c.wait()
    depth = jnp.sum(table[...], axis=1, keepdims=True).astype(F32) - 1.0
    places = jnp.concatenate(
        [
            depth[r * tree : (r + 1) * tree] + (PROMPT + lengths[r]).astype(F32)
            for r in range(requests)
        ],
        axis=0,
    )
    angles = places * inverse[...]
    lane = lax.broadcasted_iota(jnp.int32, angles.shape, 1)
    cosine = jnp.cos(angles)
    sine = jnp.sin(angles)
    sine = jnp.where(lane < hd // 2, -sine, sine)
    gains = gain[...].astype(F32)
    gains = jnp.concatenate([gains[i : i + 1] for i in range(gain.shape[0])], axis=1)
    get_tok.wait()
    begin(AHEAD)

    wide = tok[...].astype(F32)
    scale = lax.rsqrt(jnp.mean(wide * wide, axis=1, keepdims=True) + EPS)
    acc = None
    for i in range(CHUNKS):
        for c in copies[i]:
            c.wait()
        begin(AHEAD + 1 + i)
        at = slice(i * part, (i + 1) * part)
        normed = (tok[:, at].astype(F32) * scale * gains[:, at]).astype(BF16)
        d = dot(normed, w[at, :])
        acc = d if acc is None else acc + d
    heads = inner // hd
    fold = hd**-0.5 * math.log2(math.e)
    for g in range(heads):
        turned = rotate(acc[:, g * hd : (g + 1) * hd], cosine, sine)
        turned = (turned * fold).astype(BF16)
        for r in range(requests):
            q_ref[pl.ds((r * heads + g) * tree, tree), :] = turned[r * tree : (r + 1) * tree]
    k_ref[...] = rotate(acc[:, inner : inner + hd], cosine, sine).astype(BF16)
    v_ref[...] = acc[:, inner + hd :].astype(BF16)


def project_call(lengths, tokens, gain, w_query, w_key, w_value, ancestors, inverse):
    rows, width = tokens.shape
    hd = inverse.shape[1]
    inner = w_query.shape[1]
    return pl.pallas_call(
        project_kernel,
        in_specs=[HBM] * 8,
        out_specs=[VM, VM, VM],
        out_shape=[
            jax.ShapeDtypeStruct((rows * inner // hd, hd), BF16),
            jax.ShapeDtypeStruct((rows, hd), BF16),
            jax.ShapeDtypeStruct((rows, hd), BF16),
        ],
        scratch_shapes=[
            pltpu.SMEM(lengths.shape, jnp.int32),
            pltpu.VMEM((rows, width), BF16),
            pltpu.VMEM(gain.shape, BF16),
            pltpu.VMEM((width, inner + 2 * hd), BF16),
            pltpu.VMEM(ancestors.shape, jnp.int32),
            pltpu.VMEM(inverse.shape, F32),
            pltpu.SemaphoreType.DMA((5,)),
            pltpu.SemaphoreType.DMA((3, CHUNKS)),
        ],
        compiler_params=params(28),
        name="projections",
    )(lengths, tokens, gain, w_query, w_key, w_value, ancestors, inverse)


def prompt_sum(q, g, pieces, ones):
    weights, values = [], []
    for keys, vals in pieces:
        weights.append(jnp.exp2(dot_nt(q, keys[g])).astype(BF16))
        values.append(jnp.concatenate([vals[g], ones], axis=1))
    return dot(jnp.concatenate(weights, axis=1), jnp.concatenate(values, axis=0))


def source_of(at_ref, requests, shift, n_tok):
    return lax.rem(at_ref[0] + n_tok - shift, n_tok) * requests


def near_kernel(group_ref, at_ref, k, k_r, k_l, v, v_r, v_l, *refs, requests, shifts, n_tok):
    hd = k.shape[2]
    qrows = refs[0].shape[0] // requests
    pieces = [(k, v), (k_r, v_r), (k_l, v_l)]
    ones = jnp.ones((k.shape[1], hd), BF16)
    for shift, q_ref, out_ref in zip(shifts, refs[: len(shifts)], refs[len(shifts) :]):
        base = source_of(at_ref, requests, shift, n_tok)
        for r in range(requests):
            at = pl.ds(r * qrows, qrows)
            out_ref[at, :] = prompt_sum(q_ref[at, :], group_ref[base + r], pieces, ones)


def near_call(groups, at, qs, prompts, requests, shifts, n_tok):
    rows, hd = qs[0].shape
    n = len(shifts)
    return pl.pallas_call(
        lambda *refs: near_kernel(*refs, requests=requests, shifts=shifts, n_tok=n_tok),
        in_specs=[SMEM, SMEM] + [VM] * (6 + n),
        out_specs=[VM] * n,
        out_shape=[jax.ShapeDtypeStruct((rows, 2 * hd), F32)] * n,
        compiler_params=params(16),
        name="prompt_near",
    )(groups, at, *prompts, *qs)


def far_kernel(group_ref, at_ref, k_o, v_o, *refs, requests, shifts, n_tok):
    hd = k_o.shape[2]
    n = len(shifts)
    ones = jnp.ones((k_o.shape[1], hd), BF16)
    for shift, q_ref, near_ref, out_ref in zip(shifts, refs[:n], refs[n : 2 * n], refs[2 * n :]):
        qrows = q_ref.shape[0] // requests
        diagonal = lax.broadcasted_iota(jnp.int32, (qrows, hd), 0) == lax.broadcasted_iota(
            jnp.int32, (qrows, hd), 1
        )
        base = source_of(at_ref, requests, shift, n_tok)
        totals = []
        for r in range(requests):
            at = pl.ds(r * qrows, qrows)
            acc = near_ref[at, :] + prompt_sum(
                q_ref[at, :], group_ref[base + r], [(k_o, v_o)], ones
            )
            out_ref[at, :] = acc[:, :hd].astype(BF16)
            totals.append(jnp.sum(jnp.where(diagonal, acc[:, hd:], 0.0), axis=0, keepdims=True))
        total = jnp.concatenate(totals, axis=0)
        high = total.astype(BF16)
        low = (total - high.astype(F32)).astype(BF16)
        out_ref[pl.ds(requests * qrows, 2 * requests), :] = jnp.concatenate([high, low], axis=0)


def far_call(groups, at, nears, qs, k_o, v_o, requests, shifts, n_tok):
    rows, hd = qs[0].shape
    n = len(shifts)
    return pl.pallas_call(
        lambda *refs: far_kernel(*refs, requests=requests, shifts=shifts, n_tok=n_tok),
        in_specs=[SMEM, SMEM] + [VM] * (2 + 2 * n),
        out_specs=[VM] * n,
        out_shape=[jax.ShapeDtypeStruct((rows + 2 * requests, hd), BF16)] * n,
        compiler_params=params(16),
        name="prompt_far",
    )(groups, at, k_o, v_o, *qs, *nears)


def home_kernel(
    group_ref, at_ref, len_ref, q_ref, k, k_r, k_l, v, v_r, v_l, k_o, v_o, new_k, new_v, anc_hbm,
    ck_hbm, cv_hbm, out_ref, anc_ref, keys, values, where_ref, sems, anc_sem,
):
    requests, slots, hd = keys.shape
    qrows = q_ref.shape[0] // requests
    piece = slots // PIECES

    def copies(r, i):
        at = pl.ds(i * piece, piece)
        return (
            pltpu.make_async_copy(ck_hbm.at[r, at], keys.at[r, at], sems.at[0, r, i]),
            pltpu.make_async_copy(cv_hbm.at[r, at], values.at[r, at], sems.at[1, r, i]),
        )

    def each_copy(act):
        for i in range(PIECES):
            for r in range(requests):
                if i == 0:
                    for c in copies(r, i):
                        act(c)
                else:

                    @pl.when(len_ref[r] > i * piece)
                    def _(r=r, i=i):
                        for c in copies(r, i):
                            act(c)

    get_anc = pltpu.make_async_copy(anc_hbm, anc_ref, anc_sem)
    get_anc.start()
    tree = anc_ref.shape[1]
    each_copy(lambda c: c.start())
    count = 0
    for r in range(requests):

        def note(b, n, r=r):
            where_ref[0, n] = r
            where_ref[1, n] = b * KB
            return n + 1

        count = lax.fori_loop(0, (len_ref[r] + KB - 1) // KB, note, count)
    for j in range(LANES):
        where_ref[0, count + j] = requests - 1
        where_ref[1, count + j] = 0
    pieces = [(k, v), (k_r, v_r), (k_l, v_l), (k_o, v_o)]
    ones = jnp.ones((KB, hd), BF16)
    get_anc.wait()
    for r in range(requests):
        at = pl.ds(r * qrows, qrows)
        mine = pl.ds(r * tree, tree)
        q = q_ref[at, :]
        seen = jnp.concatenate([anc_ref[mine, :]] * (qrows // tree), axis=0)
        p = jnp.where(seen > 0, jnp.exp2(dot_nt(q, new_k[mine, :])), 0.0).astype(BF16)
        out_ref[at, :] = prompt_sum(
            q, group_ref[at_ref[0] * requests + r], pieces, ones
        ) + dot(p, jnp.concatenate([new_v[mine, :], ones[:tree]], axis=1))
    column = lax.broadcasted_iota(jnp.int32, (qrows, KB), 1)
    each_copy(lambda c: c.wait())

    def step(i, _):
        parts = []
        for j in range(LANES):
            n = i * LANES + j
            r = where_ref[0, n]
            first = pl.multiple_of(where_ref[1, n], KB)
            at = pl.ds(pl.multiple_of(r * qrows, qrows), qrows)
            limit = jnp.where(n < count, len_ref[r] - first, 0)
            s = dot_nt(q_ref[at, :], keys[r, pl.ds(first, KB), :])
            p = jnp.where(column < limit, jnp.exp2(s), 0.0).astype(BF16)
            both = jnp.concatenate([values[r, pl.ds(first, KB), :], ones], axis=1)
            parts.append((at, dot(p, both)))
        for at, d in parts:
            out_ref[at, :] += d
        return 0

    lax.fori_loop(0, (count + LANES - 1) // LANES, step, 0)


def home_call(groups, at, lengths, q, prompts, new_k, new_v, ancestors, cache_keys, cache_values):
    requests, slots, hd = cache_keys.shape
    return pl.pallas_call(
        home_kernel,
        in_specs=[SMEM, SMEM, SMEM] + [VM] * 11 + [HBM] * 3,
        out_specs=VM,
        out_shape=jax.ShapeDtypeStruct((q.shape[0], 2 * hd), F32),
        scratch_shapes=[
            pltpu.VMEM(ancestors.shape, jnp.int32),
            pltpu.VMEM(cache_keys.shape, BF16),
            pltpu.VMEM(cache_values.shape, BF16),
            pltpu.SMEM((2, requests * slots // KB + LANES), jnp.int32),
            pltpu.SemaphoreType.DMA((2, requests, PIECES)),
            pltpu.SemaphoreType.DMA,
        ],
        compiler_params=params(20),
        name="home_attention",
    )(groups, at, lengths, q, *prompts, new_k, new_v, ancestors, cache_keys, cache_values)


def merge_kernel(home_ref, a_ref, b_ref, c_ref, out_ref, *, requests):
    hd = a_ref.shape[1]
    qrows = home_ref.shape[0] // requests
    tree = out_ref.shape[0] // requests
    total = None
    for ref in (a_ref, b_ref, c_ref):
        both = ref[pl.ds(requests * qrows, 2 * requests), :].astype(F32)
        t = both[:requests] + both[requests:]
        total = t if total is None else total + t
    diagonal = lax.broadcasted_iota(jnp.int32, (qrows, hd), 0) == lax.broadcasted_iota(
        jnp.int32, (qrows, hd), 1
    )
    for r in range(requests):
        at = pl.ds(r * qrows, qrows)
        num = home_ref[at, pl.ds(0, hd)]
        for ref in (a_ref, b_ref, c_ref):
            num = num + ref[at, :].astype(F32)
        den = home_ref[at, pl.ds(hd, hd)] + jnp.sum(
            jnp.where(diagonal, jnp.broadcast_to(total[r : r + 1], (qrows, hd)), 0.0),
            axis=1,
            keepdims=True,
        )
        out = (num / den).astype(BF16)
        for g in range(qrows // tree):
            out_ref[pl.ds(r * tree, tree), pl.ds(g * hd, hd)] = out[g * tree : (g + 1) * tree]


def merge_call(home, a, b, c, requests, rows):
    hd = a.shape[1]
    return pl.pallas_call(
        lambda *refs: merge_kernel(*refs, requests=requests),
        in_specs=[VM] * 4,
        out_specs=VM,
        out_shape=jax.ShapeDtypeStruct((rows, home.shape[0] // rows * hd), BF16),
        compiler_params=params(8),
        name="merge",
    )(home, a, b, c)


def pick(acc_ref, x, tree):
    rows = []
    slot = lax.broadcasted_iota(jnp.int32, (tree, acc_ref.shape[1]), 0)
    for r in range(acc_ref.shape[0]):
        chosen = (slot == acc_ref[r : r + 1, :]).astype(F32).astype(BF16)
        rows.append(
            lax.dot_general(
                chosen, x[r * tree : (r + 1) * tree], (((0,), (0,)), ((), ())),
                preferred_element_type=F32,
            )
        )
    return rows


def pick_kernel(mdl_ref, acc_ref, tok_hbm, out_ref, tok, sem):
    cols = tok.shape[1]
    get = pltpu.make_async_copy(
        tok_hbm.at[:, pl.ds(pl.multiple_of(mdl_ref[0] * cols, 128), cols)], tok, sem
    )
    get.start()
    get.wait()
    for r, row in enumerate(pick(acc_ref, tok[...], tok.shape[0] // acc_ref.shape[0])):
        out_ref[r] = row


def pick_call(mdl, accepted, tokens, cols):
    return pl.pallas_call(
        pick_kernel,
        in_specs=[SMEM, VM, HBM],
        out_specs=VM,
        out_shape=jax.ShapeDtypeStruct(accepted.shape + (cols,), F32),
        scratch_shapes=[pltpu.VMEM((tokens.shape[0], cols), BF16), pltpu.SemaphoreType.DMA],
        compiler_params=params(4),
        name="pick_tokens",
    )(mdl, accepted, tokens)


def columns_of(mdl_ref, w_hbm, shift, side, count, cols):
    there = lax.rem(mdl_ref[0] // 2 + shift, count)
    start = (2 * there + lax.rem(mdl_ref[0] + side, 2)) * cols
    return w_hbm.at[:, pl.ds(pl.multiple_of(start, 128), cols)]


def columns_kernel(mdl_ref, w_hbm, send_ref, sems):
    count, _, cols = send_ref.shape
    copies = [
        pltpu.make_async_copy(
            columns_of(mdl_ref, w_hbm, i, 1, count, cols), send_ref.at[i], sems.at[i]
        )
        for i in range(count)
    ]
    for c in copies:
        c.start()
    for c in copies:
        c.wait()


def columns_call(mdl, w_out, count):
    cols = w_out.shape[1] // (2 * count)
    return pl.pallas_call(
        columns_kernel,
        in_specs=[SMEM, HBM],
        out_specs=VM,
        out_shape=jax.ShapeDtypeStruct((count, w_out.shape[0], cols), BF16),
        scratch_shapes=[pltpu.SemaphoreType.DMA((count,))],
        compiler_params=params(6),
        name="out_columns",
    )(mdl, w_out)


def first_kernel(mdl_ref, mine_ref, w_hbm, other_hbm, out_ref, other_ref, w, sems, *, shift):
    count, _, cols = other_hbm.shape
    get = pltpu.make_async_copy(columns_of(mdl_ref, w_hbm, shift, 0, count, cols), w, sems.at[0])
    get_other = pltpu.make_async_copy(other_hbm.at[shift], other_ref, sems.at[1])
    get.start()
    get_other.start()
    get.wait()
    out_ref[...] = dot(mine_ref[...], w[...])
    get_other.wait()


def out_first(mdl, mine, w_out, w_other, shift):
    rows, inner = mine.shape
    cols = w_other.shape[2]
    return pl.pallas_call(
        lambda *refs: first_kernel(*refs, shift=shift),
        in_specs=[SMEM, VM, HBM, HBM],
        out_specs=[VM, VM],
        out_shape=[
            jax.ShapeDtypeStruct((rows, cols), F32),
            jax.ShapeDtypeStruct((inner, cols), BF16),
        ],
        scratch_shapes=[pltpu.VMEM((inner, cols), BF16), pltpu.SemaphoreType.DMA((2,))],
        compiler_params=params(12),
        name="out_first",
    )(mdl, mine, w_out, w_other)


def second_kernel(first_ref, other_ref, w_ref, out_ref):
    out_ref[...] = (first_ref[...] + dot(other_ref[...], w_ref[...])).astype(BF16)


def out_second(first, other, w):
    return pl.pallas_call(
        second_kernel,
        in_specs=[VM] * 3,
        out_specs=VM,
        out_shape=jax.ShapeDtypeStruct(first.shape, BF16),
        compiler_params=params(12),
        name="out_second",
    )(first, other, w)


def out_kernel(mdl_ref, mine_ref, other_ref, w_hbm, wo_hbm, *refs, shifts):
    outs = refs[: len(shifts)]
    wa, wb, sems = refs[len(shifts) :]
    count, _, cols = wo_hbm.shape
    copies = []
    for i, shift in enumerate(shifts):
        two = (
            pltpu.make_async_copy(
                columns_of(mdl_ref, w_hbm, shift, 0, count, cols), wa.at[i], sems.at[0, i]
            ),
            pltpu.make_async_copy(wo_hbm.at[shift], wb.at[i], sems.at[1, i]),
        )
        for c in two:
            c.start()
        copies.append(two)
    for i, out in enumerate(outs):
        for c in copies[i]:
            c.wait()
        d = dot(mine_ref[...], wa[i]) + dot(other_ref[...], wb[i])
        out[...] = d.astype(out.dtype)


def out_call(mdl, mine, other, w_out, w_other, shifts, dtype):
    rows, inner = mine.shape
    cols = w_other.shape[2]
    n = len(shifts)
    return pl.pallas_call(
        lambda *refs: out_kernel(*refs, shifts=shifts),
        in_specs=[SMEM, VM, VM, HBM, HBM],
        out_specs=[VM] * n,
        out_shape=[jax.ShapeDtypeStruct((rows, cols), dtype)] * n,
        scratch_shapes=[
            pltpu.VMEM((n, inner, cols), BF16),
            pltpu.VMEM((n, inner, cols), BF16),
            pltpu.SemaphoreType.DMA((2, n)),
        ],
        compiler_params=params(12),
        name="out_proj",
    )(mdl, mine, other, w_out, w_other)


def last_kernel(acc_ref, own_ref, a_ref, b_ref, c_ref, tok_ref, out_ref, rows_ref):
    total = own_ref[...] + a_ref[...].astype(F32) + b_ref[...].astype(F32) + c_ref[...].astype(F32)
    rounded = total.astype(BF16)
    out_ref[...] = rounded
    for r, row in enumerate(pick(acc_ref, rounded, own_ref.shape[0] // acc_ref.shape[0])):
        rows_ref[r] = (tok_ref[r] + row).astype(BF16)


def last_call(accepted, own, a, b, c, picked):
    rows, cols = own.shape
    return pl.pallas_call(
        last_kernel,
        in_specs=[VM] * 6,
        out_specs=[VM, VM],
        out_shape=[
            jax.ShapeDtypeStruct((rows, cols), BF16),
            jax.ShapeDtypeStruct(picked.shape, BF16),
        ],
        compiler_params=params(8),
        name="last_sums",
    )(accepted, own, a, b, c, picked)


def shards(
    tokens, norm_gain, w_query, w_key, w_value, w_out, prompt_keys, prompt_values, cache_keys,
    cache_values, cache_length, request_group, ancestors, accepted,
):
    requests, tree = ancestors.shape[:2]
    rows = tokens.shape[0]
    hd = prompt_keys.shape[3]
    n_tok = lax.axis_size("tok")
    n_mdl = lax.axis_size("mdl")
    n_y = 4
    n_z = n_tok // n_y
    n_x = n_mdl // 2
    tok = lax.axis_index("tok")
    mdl = lax.axis_index("mdl")

    def along_y(v, n):
        perm = [(t, t // n_y * n_y + (t + n) % n_y) for t in range(n_tok)]
        return lax.ppermute(v, "tok", perm)

    def along_z(v, n):
        return lax.ppermute(v, "tok", [(t, (t + n * n_y) % n_tok) for t in range(n_tok)])

    def along_x(v, n):
        return lax.ppermute(v, "mdl", [(m, (m + 2 * n) % n_mdl) for m in range(n_mdl)])

    def other_core(v):
        return lax.ppermute(v, "mdl", [(m, m ^ 1) for m in range(n_mdl)])

    def in_hbm(v):
        return pltpu.with_memory_space_constraint(v, pltpu.HBM)

    tok_at = jnp.reshape(tok, (1,)).astype(jnp.int32)
    mdl_at = jnp.reshape(mdl, (1,)).astype(jnp.int32)

    squeeze = lambda v: v.reshape(v.shape[0], v.shape[1], v.shape[3])
    k, v = squeeze(prompt_keys), squeeze(prompt_values)
    k_r, k_l = along_y(k, 1), along_y(k, -1)
    v_r, v_l = along_y(v, 1), along_y(v, -1)

    exponent = np.arange(hd // 2, dtype=np.float64) * (2.0 / hd)
    inverse = jnp.asarray(np.tile(THETA**-exponent, 2)[None, :], dtype=F32)
    table = ancestors.reshape(rows, tree)
    q, new_k, new_v = project_call(
        *map(
            in_hbm,
            (
                cache_length, tokens, norm_gain.reshape(-1, hd), w_query, w_key, w_value, table,
                inverse,
            ),
        )
    )
    shifts = (2, 1, -1)
    q_far = [along_z(q, n) for n in shifts]

    w_send = columns_call(mdl_at, in_hbm(w_out), n_x)
    w_other = in_hbm(other_core(w_send))

    k_o = along_y(k_r, 1)
    v_o = along_y(v_l, -1)
    near = tuple(map(in_hbm, (k, k_r, k_l, v, v_r, v_l)))

    turns = [n % n_z * n_y for n in shifts]
    nears, parts = [], []
    for some in (slice(0, 1), slice(1, 3)):
        nears += near_call(request_group, tok_at, q_far[some], near, requests, turns[some], n_tok)
    for some in (slice(0, 1), slice(1, 3)):
        parts += far_call(
            request_group, tok_at, nears[some], q_far[some], k_o, v_o, requests, turns[some],
            n_tok,
        )
    back = [along_z(part, -n) for n, part in zip(shifts, parts)]
    home = home_call(
        request_group, tok_at, cache_length, q, (k, k_r, k_l, v, v_r, v_l, k_o, v_o), new_k, new_v, in_hbm(table),
        in_hbm(squeeze(cache_keys)), in_hbm(squeeze(cache_values)),
    )
    attended = merge_call(home, *back, requests, rows)

    attended_other = other_core(attended)
    weights = (in_hbm(w_out), w_other)
    first, w_second = out_first(mdl_at, attended, *weights, 2)
    far = along_x(out_second(first, attended_other, w_second), 2)
    both = (mdl_at, attended, attended_other, *weights)
    up, down = out_call(*both, (1, n_x - 1), BF16)
    up = along_x(up, 1)
    down = along_x(down, -1)
    (own_sum,) = out_call(*both, (0,), F32)
    picked = pick_call(mdl_at, accepted, in_hbm(tokens), w_other.shape[2])
    return tuple(last_call(accepted, own_sum, far, up, down, picked))


def solution(mesh):
    placed = (
        P("tok", None),
        P(),
        P(None, "mdl"),
        P(None, "mdl"),
        P(None, "mdl"),
        P("mdl", None),
        P(None, "tok", "mdl", None),
        P(None, "tok", "mdl", None),
        P("tok", None, "mdl", None),
        P("tok", None, "mdl", None),
        P("tok"),
        P(),
        P("tok", None, None),
        P("tok", None),
    )

    return jax.shard_map(
        shards,
        mesh=mesh,
        in_specs=placed,
        out_specs=(P("tok", "mdl"), P("tok", None, "mdl")),
        check_vma=False,
    )
```
